256 devices in a mesh: brick: 64 (over y, z, core), mp: 4 (over x).
Axes of the slice: x: 4, y: 4, z: 8, core: 2. Of those that a mesh axis runs over, the one named last changes fastest.
Arguments:
- voxel_feats: bfloat16 [196608, 512], P('brick'), may hold values from -6 to 6
- slot_rank: int32 [196608], P('brick'), may hold values from 0 to 131072, as said below
- curve_order: int32 [131072], P('brick'), may hold values from 0 to 196607, as said below
- patch_shift: int32 [1], replicated, may hold values from 1 to 1023
- qkv_weight: bfloat16 [512, 1536], P(None, 'mp')
- proj_weight: bfloat16 [512, 512], P('mp'), may hold values from -0.25 to 0.25
- up_weight: bfloat16 [512, 2048], P(None, 'mp'), may hold values from -0.25 to 0.25
- down_weight: bfloat16 [2048, 512], P('mp'), may hold values from -0.125 to 0.125
- norm_gains: float32 [2, 512], replicated, may hold values from 0.25 to 1.75
Outputs:
- voxel_out: bfloat16 [196608, 512], P('brick', 'mp')
The draws below stay inside these ranges and needn't reach their ends.
Inputs may be any that keep to these rules, and one draw needn't show every extreme that they name: `slot_rank`: within each brick's 3072 slots the occupied ones come first and hold distinct curve positions in increasing order; the rest hold 131072. Every curve position lies in exactly one slot. Curve shard k is positions k * 2048 to (k + 1) * 2048 - 1 and draws its voxels only from bricks k - 1, k, k + 1 and k + 2 (mod 64). A brick holds at most 768 voxels of one shard, and some brick holds exactly 768 of some shard; some brick has all 3072 slots occupied. curve_order[p] = brick * 3072 + slot of the voxel at curve position p, the inverse of slot_rank on occupied slots.
All inputs are finite; a program needn't handle non-finite values.
Results may differ from the reference program's by a relative error of at most 0.012.
The reference program's roundings to bfloat16 on the way count: a program that leaves them out, or rounds other values in their place, can miss the bound.
Values may be sent and summed in bfloat16 or wider, within the bound.
No kernel may reach another device: no remote copies, remote signals or barrier semaphores. Data moves between devices by JAX's collectives and lax.ppermute only.
A program may use at most 128 MiB of HBM per device.

```python
import math
import jax
import jax.numpy as jnp
import numpy as np
from jax import lax

C = 512
HEADS = 32
HID = 2048
PATCH = 1024
TOK_DEV = 2048
BRICKS = 64
TOKENS = 131072
CAP = 3072
N_MP = 4


def pattern_table():
    grid = np.stack(np.meshgrid(np.arange(1, 4), np.arange(1, 4), np.arange(1, 4), np.arange(1, 4), indexing='ij'), -1).reshape(-1, 4)
    return grid[grid.sum(axis=1) == 8].astype(np.int32)


def layout_tables(key):
    root = jax.random.fold_in(key, 911)
    table = jnp.asarray(pattern_table())
    picks = jax.random.randint(jax.random.fold_in(root, 1), (BRICKS,), 0, table.shape[0])
    shares = table[picks]
    shares = shares.at[1].set(jnp.array([3, 1, 1, 3], jnp.int32))
    shares = shares.at[0].set(jnp.array([1, 3, 3, 1], jnp.int32))
    shares = shares.at[BRICKS - 1].set(jnp.array([1, 1, 3, 3], jnp.int32))
    shares = shares.at[BRICKS - 2].set(jnp.array([2, 1, 2, 3], jnp.int32))
    unit_rows = TOK_DEV // 8
    ends = jnp.cumsum(shares * unit_rows, axis=1).astype(jnp.int32)
    spots = jnp.arange(TOK_DEV, dtype=jnp.int32)
    lanes = jnp.sum((ends[:, None, :] <= spots[None, :, None]).astype(jnp.int32), axis=2).astype(jnp.int32)
    shard_ids = jnp.arange(BRICKS, dtype=jnp.int32)
    labels = ((shard_ids[:, None] + lanes - 1) % BRICKS).reshape(-1).astype(jnp.int32)
    order = jnp.argsort(labels, stable=True).astype(jnp.int32)
    brick_count = jnp.bincount(labels, length=BRICKS).astype(jnp.int32)
    brick_start = (jnp.cumsum(brick_count) - brick_count).astype(jnp.int32)
    sorted_labels = labels[order]
    slot_index = jnp.arange(TOKENS, dtype=jnp.int32) - brick_start[sorted_labels]
    global_slot = (sorted_labels * CAP + slot_index).astype(jnp.int32)
    curve_order = jnp.zeros((TOKENS,), jnp.int32).at[order].set(global_slot)
    slot_rank = jnp.full((BRICKS * CAP,), TOKENS, jnp.int32).at[global_slot].set(order)
    return (slot_rank, curve_order)


def draw_slot_rank(key, part):
    return layout_tables(key)[0]


def draw_curve_order(key, part):
    return layout_tables(key)[1]


def draw_qkv_weight(key, part):
    weights_full = jax.random.normal(jax.random.fold_in(key, 17), (C, 3 * C), jnp.float32) * C ** (-0.5)
    return weights_full.astype(jnp.bfloat16)


def level_of(own_key, dims, cuts, smallest, high):
    factor_of, own = 1.0, jax.random.fold_in(own_key, 6)
    for position, shards_of in cuts:
        heights = jnp.exp(jax.random.uniform(jax.random.fold_in(own, position), (shards_of,), jnp.float32, smallest / len(cuts), high / len(cuts)))
        factor_of = factor_of * jnp.repeat(heights, dims[position] // shards_of).reshape([-1 if axis == position else 1 for axis in range(len(dims))])
    return factor_of


def normal_values(own_key, shape, scale, most, cuts=(), held_as=jnp.bfloat16):
    values = jax.random.normal(own_key, shape, jnp.float32) * scale
    if len(cuts) > 0:
        values = level_of(own_key, shape, cuts, -0.22, 0.18) * values
    return jnp.clip(values, min=-most, max=most).astype(held_as)


def setup_inputs(seed: int = 0) -> dict:
    key_list = jax.random.split(jax.random.key(seed), 10)
    voxel_feats = normal_values(key_list[0], (BRICKS * CAP, C), 1.0, 6.0, ((0, 64),))
    slot_rank = draw_slot_rank(jax.random.fold_in(key_list[9], 71), 0)
    curve_order = draw_curve_order(jax.random.fold_in(key_list[9], 71), 0)
    patch_shift = jax.random.randint(key_list[3], (1,), 1, PATCH).astype(jnp.int32)
    qkv_weight = draw_qkv_weight(jax.random.fold_in(key_list[9], 71), 0)
    proj_weight = normal_values(key_list[5], (C, C), C ** -0.5, 0.25, ((0, 4),))
    up_weight = normal_values(key_list[6], (C, HID), C ** -0.5, 0.25, ((1, 4),))
    down_weight = normal_values(key_list[7], (HID, C), HID ** -0.5, 0.125, ((0, 4),))
    norm_gains = jnp.clip(1.0 + 0.15 * jax.random.normal(key_list[8], (2, C), jnp.float32), 0.25, 1.75)
    return dict(voxel_feats=voxel_feats, slot_rank=slot_rank, curve_order=curve_order, patch_shift=patch_shift, qkv_weight=qkv_weight, proj_weight=proj_weight, up_weight=up_weight, down_weight=down_weight, norm_gains=norm_gains)


EPSILON = 1e-05

def layer_norm(values, gain):
    values = values.astype(jnp.float32)
    centred = values - lax.optimization_barrier(jnp.mean(values, axis=-1, keepdims=True))
    spread = lax.optimization_barrier(jnp.mean(centred * centred, axis=-1, keepdims=True))
    return (centred * lax.rsqrt(spread + EPSILON) * gain).astype(jnp.bfloat16)

def patch_attention(qkv_rows, heads_here, patch_len):
    row_count = qkv_rows.shape[0]
    head_dim = qkv_rows.shape[1] // (3 * heads_here)
    group_size = math.gcd(heads_here, 4)
    group_count = heads_here // group_size
    scale = head_dim ** (-0.5)

    def one_group(piece):
        query = piece[:, :, 0].astype(jnp.float32)
        keys_here = piece[:, :, 1].astype(jnp.float32)
        values_here = piece[:, :, 2].astype(jnp.float32)
        scores = jnp.einsum('qhd,khd->hqk', query, keys_here) * scale
        highest = lax.optimization_barrier(jnp.max(scores, axis=-1, keepdims=True))
        weights_exp = jnp.exp(scores - highest)
        softmax_weights = (weights_exp / lax.optimization_barrier(jnp.sum(weights_exp, axis=-1, keepdims=True))).astype(jnp.bfloat16)
        return jnp.einsum('hqk,khd->qhd', softmax_weights.astype(jnp.float32), values_here).astype(jnp.bfloat16)

    def one_patch(block):
        pieces = jnp.moveaxis(block.reshape(patch_len, group_count, group_size, 3, head_dim), 1, 0)
        outputs = lax.map(one_group, pieces)
        return jnp.moveaxis(outputs, 0, 1).reshape(patch_len, heads_here * head_dim)
    blocks = qkv_rows.reshape(row_count // patch_len, patch_len, qkv_rows.shape[1])
    return lax.map(one_patch, blocks).reshape(row_count, heads_here * head_dim)

def partial_sum_rounded(left, right, groups):
    width = left.shape[1] // groups
    total = jnp.zeros((left.shape[0], right.shape[1]), jnp.float32)
    for group_index in range(groups):
        term = jnp.dot(left[:, group_index * width:(group_index + 1) * width], right[group_index * width:(group_index + 1) * width], preferred_element_type=jnp.float32).astype(jnp.bfloat16)
        total = total + lax.optimization_barrier(term).astype(jnp.float32)
    return total

def reference(voxel_feats, slot_rank, curve_order, patch_shift, qkv_weight, proj_weight, up_weight, down_weight, norm_gains):
    curve = voxel_feats[curve_order]
    normed = layer_norm(curve, norm_gains[0])
    qkv_rows = jnp.dot(normed, qkv_weight, preferred_element_type=jnp.float32).astype(jnp.bfloat16)
    offset = patch_shift[0]
    rolled = jnp.roll(qkv_rows, -offset, axis=0)
    attended = jnp.roll(patch_attention(rolled, HEADS, PATCH), offset, axis=0)
    mixed = partial_sum_rounded(attended, proj_weight, N_MP)
    hidden_state = (curve.astype(jnp.float32) + mixed).astype(jnp.bfloat16)
    normed_two = layer_norm(hidden_state, norm_gains[1])
    expanded = jax.nn.gelu(jnp.dot(normed_two, up_weight, preferred_element_type=jnp.float32), approximate=False).astype(jnp.bfloat16)
    mlp_sum = partial_sum_rounded(expanded, down_weight, N_MP)
    result = (hidden_state.astype(jnp.float32) + mlp_sum).astype(jnp.bfloat16)
    live_slots = slot_rank < TOKENS
    picked = result[jnp.minimum(slot_rank, TOKENS - 1)]
    return jnp.where(live_slots[:, None], picked, jnp.zeros_like(picked))
```

```python
import functools

import jax
import jax.numpy as jnp
from jax import lax
from jax.experimental import pallas as pl
from jax.experimental.pallas import tpu as pltpu
from jax.sharding import PartitionSpec as P

PATCH = 1024
HEAD_DIM = 16
GROUP_HEADS = 8
EPSILON = 1e-05
LOG2E = 1.4426950408889634

TILE = 16
BLOCK = 128
WINDOW = 160
MOST_RUN = 768
PIECE = MOST_RUN + TILE
LANES = 4
BLOCKS = PATCH // BLOCK

F32 = jnp.float32
BF16 = jnp.bfloat16

ANY = pl.BlockSpec(memory_space=pl.ANY)
VMEM = pl.BlockSpec(memory_space=pltpu.VMEM)
SMEM = pl.BlockSpec(memory_space=pltpu.SMEM)


def nt_dot(left, right):
    return lax.dot_general(left, right, (((1,), (1,)), ((), ())), preferred_element_type=F32)


def nn_dot(left, right):
    return jnp.dot(left, right, preferred_element_type=F32)


def tn_dot(left, right):
    return lax.dot_general(left, right, (((0,), (0,)), ((), ())), preferred_element_type=F32)


def aligned(value):
    return pl.multiple_of(value, TILE)


def shifted(value, axis, steps):
    count = lax.axis_size(axis)
    pairs = [(source, (source + steps) % count) for source in range(count)]
    return lax.ppermute(value, axis, pairs)


def layer_norm(values, gain):
    values = values.astype(F32)
    centred = values - jnp.mean(values, axis=-1, keepdims=True)
    spread = jnp.mean(centred * centred, axis=-1, keepdims=True)
    return (centred * lax.rsqrt(spread + EPSILON) * gain).astype(BF16)


def cut_kernel(start_ref, feats_ref, *rest):
    outs, (buffers, in_sems, out_sems) = rest[:3], rest[3:]
    order = (2, 1, 0)
    loads = [
        pltpu.make_async_copy(
            feats_ref.at[pl.ds(aligned(start_ref[i]), PIECE)], buffers.at[i], in_sems.at[i]
        )
        for i in range(3)
    ]
    stores = [
        pltpu.make_async_copy(buffers.at[i], outs[i], out_sems.at[i]) for i in range(3)
    ]
    for i in order:
        loads[i].start()
    for i in order:
        loads[i].wait()
        stores[i].start()
    for i in order:
        stores[i].wait()


def cut_windows(starts, feats):
    piece = jax.ShapeDtypeStruct((PIECE, feats.shape[1]), feats.dtype)
    return pl.pallas_call(
        cut_kernel,
        out_shape=(piece,) * 3,
        in_specs=[SMEM, ANY],
        out_specs=(ANY,) * 3,
        scratch_shapes=[
            pltpu.VMEM((3, PIECE, feats.shape[1]), feats.dtype),
            pltpu.SemaphoreType.DMA((3,)),
            pltpu.SemaphoreType.DMA((3,)),
        ],
        name="cut_windows",
    )(starts, feats)


def gather_block(table_ref, block, spots, lane_refs):
    windows = [
        lane_refs[lane][pl.ds(aligned(table_ref[block, lane]), WINDOW), :]
        for lane in range(LANES)
    ]
    stacked = jnp.concatenate(windows, axis=0)
    hots = []
    lanes_iota = lax.broadcasted_iota(jnp.int32, (BLOCK, 128), 1)
    for chunk in range(LANES * WINDOW // 128):
        hots.append(jnp.where(spots == lanes_iota + chunk * 128, 1.0, 0.0).astype(BF16))
    hot = jnp.concatenate(hots, axis=1)
    return nn_dot(hot, stacked).astype(BF16)


def head_kernel(
    table_ref, start_ref, spots_ref, feats_ref, lane0_ref, lane2_ref, lane3_ref, out_ref, own_ref, sem
):
    load = pltpu.make_async_copy(
        feats_ref.at[pl.ds(aligned(start_ref[0]), PIECE)], own_ref, sem
    )
    load.start()
    load.wait()
    lane_refs = (lane0_ref, own_ref, lane2_ref, lane3_ref)

    def step(block, carry):
        rows = pl.ds(pl.multiple_of(block * BLOCK, BLOCK), BLOCK)
        out_ref[rows, :] = gather_block(table_ref, block, spots_ref[rows, :], lane_refs)
        return carry

    lax.fori_loop(0, BLOCKS, step, 0)


def head_rows(table, start, spots, feats, lanes):
    width = feats.shape[1]
    return pl.pallas_call(
        head_kernel,
        out_shape=jax.ShapeDtypeStruct((PATCH, width), BF16),
        in_specs=[SMEM, SMEM, VMEM, ANY, VMEM, VMEM, VMEM],
        out_specs=VMEM,
        scratch_shapes=[pltpu.VMEM((PIECE, width), BF16), pltpu.SemaphoreType.DMA],
        cost_estimate=pl.CostEstimate(
            flops=2 * PATCH * 768 * width, bytes_accessed=5 << 20, transcendentals=0
        ),
        name="head_rows",
    )(table, start, spots, feats, *lanes)


def attend_kernel(with_head, groups, queries, *refs):
    table_ref, start_ref, spots_ref, feats_ref = refs[:4]
    lane0_ref, lane2_ref, lane3_ref = refs[4:7]
    gain_ref = refs[7]
    qkv_refs = refs[8 : 8 + groups]
    proj_refs = refs[8 + groups : 8 + 2 * groups]
    at = 8 + 2 * groups
    if with_head:
        extra_ref = refs[at]
        at += 1
    out_ref = refs[at]
    own_ref, rows_ref, normed_ref, keys_ref, values_ref, query_ref, mixed_ref, score_ref, sem = refs[
        at + 1 :
    ]
    load = pltpu.make_async_copy(
        feats_ref.at[pl.ds(aligned(start_ref[0]), PIECE)], own_ref, sem
    )
    load.start()
    load.wait()
    lane_refs = (lane0_ref, own_ref, lane2_ref, lane3_ref)
    gain = gain_ref[0:1, :]

    def gather_step(block, carry):
        rows = pl.ds(pl.multiple_of(block * BLOCK, BLOCK), BLOCK)
        found = gather_block(table_ref, block, spots_ref[rows, :], lane_refs)
        if with_head:
            found = found + extra_ref[rows, :]
        rows_ref[rows, :] = found
        normed_ref[rows, :] = layer_norm(found, gain)
        return carry

    lax.fori_loop(0, BLOCKS, gather_step, 0)
    own_rows = pl.ds(pl.multiple_of(start_ref[1], queries), queries)
    span = GROUP_HEADS * HEAD_DIM
    for group in range(groups):
        weight = qkv_refs[group]
        query = nt_dot(weight[0:span, :], normed_ref[own_rows, :])
        query_ref[group] = (query * (HEAD_DIM ** (-0.5) * LOG2E)).astype(BF16)
        for part in range(4):
            rows = slice(part * 256, (part + 1) * 256)
            normed = normed_ref[rows, :]
            keys_ref[group, rows, :] = nt_dot(normed, weight[span : 2 * span, :]).astype(BF16)
            values_ref[group, :, rows] = nt_dot(weight[2 * span : 3 * span, :], normed).astype(BF16)

    head_of_row = lax.broadcasted_iota(jnp.int32, (span, queries), 0) // HEAD_DIM
    ones = jnp.ones((HEAD_DIM, PATCH), BF16)

    def head_step(head, carry):
        mine = head_of_row == head
        rows = pl.ds(pl.multiple_of(head * HEAD_DIM, HEAD_DIM), HEAD_DIM)
        for group in range(groups):
            query = query_ref[group]
            query = jnp.where(mine, query, jnp.zeros_like(query))
            slot = group % 2
            highest = None
            for part in range(4):
                keys = slice(part * 256, (part + 1) * 256)
                scores = nn_dot(keys_ref[group, keys, :], query)
                score_ref[slot, keys, :] = scores
                top = jnp.max(scores, axis=0, keepdims=True)
                highest = top if highest is None else jnp.maximum(highest, top)
            values = jnp.concatenate([values_ref[group, rows, :], ones], axis=0)
            total = None
            for part in range(4):
                keys = slice(part * 256, (part + 1) * 256)
                weights = jnp.exp2(score_ref[slot, keys, :] - highest).astype(BF16)
                term = nn_dot(values[:, keys], weights)
                total = term if total is None else total + term
            mixed_ref[group, rows, :] = (
                total[:HEAD_DIM] / total[HEAD_DIM : HEAD_DIM + 1]
            ).astype(BF16)
        return carry

    lax.fori_loop(0, GROUP_HEADS, head_step, 0)
    mixed = None
    for group in range(groups):
        term = tn_dot(mixed_ref[group], proj_refs[group][...]).astype(BF16).astype(F32)
        mixed = term if mixed is None else mixed + term
    out_ref[...] = (rows_ref[own_rows, :].astype(F32) + mixed).astype(BF16)


def attend(table, start, spots, feats, lanes, gains, qkv, proj, extra, queries):
    width = feats.shape[1]
    groups = len(qkv)
    span = GROUP_HEADS * HEAD_DIM
    operands = [table, start, spots, feats, *lanes, gains, *qkv, *proj]
    specs = [SMEM, SMEM, VMEM, ANY] + [VMEM] * (4 + 2 * groups)
    if extra is not None:
        operands.append(extra)
        specs.append(VMEM)
    return pl.pallas_call(
        functools.partial(attend_kernel, extra is not None, groups, queries),
        out_shape=jax.ShapeDtypeStruct((queries, width), BF16),
        in_specs=specs,
        out_specs=VMEM,
        scratch_shapes=[
            pltpu.VMEM((PIECE, width), BF16),
            pltpu.VMEM((PATCH, width), BF16),
            pltpu.VMEM((PATCH, width), BF16),
            pltpu.VMEM((groups, PATCH, span), BF16),
            pltpu.VMEM((groups, span, PATCH), BF16),
            pltpu.VMEM((groups, span, queries), BF16),
            pltpu.VMEM((groups, span, queries), BF16),
            pltpu.VMEM((2, PATCH, queries), F32),
            pltpu.SemaphoreType.DMA,
        ],
        cost_estimate=pl.CostEstimate(
            flops=40 * 10**9, bytes_accessed=10 << 20, transcendentals=8 << 20
        ),
        name="attend",
    )(*operands)


def mlp_kernel(groups, hidden_ref, gain_ref, *refs):
    up_refs, down_refs = refs[:groups], refs[groups : 2 * groups]
    out_ref, wide_ref = refs[2 * groups :]
    hidden = hidden_ref[...]
    normed = layer_norm(hidden, gain_ref[1:2, :])
    for group in range(groups):
        wide = nn_dot(normed, up_refs[group][...])
        wide_ref[group] = (wide * (0.5 + 0.5 * lax.erf(wide * 0.5**0.5))).astype(BF16)
    total = None
    for group in range(groups):
        term = nn_dot(wide_ref[group], down_refs[group][...]).astype(BF16).astype(F32)
        total = term if total is None else total + term
    result = (hidden.astype(F32) + total).astype(BF16)
    width = result.shape[1] // groups
    for group in range(groups):
        out_ref[group] = result[:, group * width : (group + 1) * width]


def mlp(hidden, gains, up, down):
    groups = len(up)
    rows, width = hidden.shape
    return pl.pallas_call(
        functools.partial(mlp_kernel, groups),
        out_shape=jax.ShapeDtypeStruct((groups, rows, width // groups), BF16),
        in_specs=[VMEM] * (2 + 2 * groups),
        out_specs=VMEM,
        scratch_shapes=[pltpu.VMEM((groups, rows, up[0].shape[1]), BF16)],
        cost_estimate=pl.CostEstimate(
            flops=4 * rows * width * up[0].shape[1] * groups,
            bytes_accessed=5 << 20,
            transcendentals=0,
        ),
        name="mlp",
    )(hidden, gains, *up, *down)


def pack_kernel(table_ref, spots_ref, tail_ref, first_ref, last_ref, *rest):
    outs, lanes_ref = rest[:LANES], rest[LANES]
    lanes_ref[...] = jnp.zeros_like(lanes_ref)
    tall = lax.broadcasted_iota(jnp.int32, (LANES * WINDOW, BLOCK), 0)
    for part, source in enumerate((tail_ref, first_ref, last_ref)):

        def step(block, carry):
            place = part * BLOCKS + block
            spots = spots_ref[pl.ds(place, 1), :]
            hot = jnp.where(tall == spots, 1.0, 0.0).astype(BF16)
            rows = source[pl.ds(pl.multiple_of(block * BLOCK, BLOCK), BLOCK), :]
            sent = nn_dot(hot, rows).astype(BF16)
            for lane in range(LANES):
                window = pl.ds(aligned(table_ref[place, lane]), WINDOW)
                lanes_ref[lane, window, :] = (
                    lanes_ref[lane, window, :] + sent[lane * WINDOW : (lane + 1) * WINDOW]
                )
            return carry

        lax.fori_loop(0, BLOCKS, step, 0)
    for lane in range(LANES):
        outs[lane][...] = lanes_ref[lane]


def pack_lanes(table, spots, tail, first, last):
    width = tail.shape[1]
    return pl.pallas_call(
        pack_kernel,
        out_shape=(jax.ShapeDtypeStruct((PIECE, width), BF16),) * LANES,
        in_specs=[SMEM] + [VMEM] * 4,
        out_specs=(VMEM,) * LANES,
        scratch_shapes=[pltpu.VMEM((LANES, PIECE, width), BF16)],
        name="pack_lanes",
    )(table, spots, tail, first, last)


def place_kernel(spans_ref, *refs):
    pieces, out_ref = refs[:LANES], refs[LANES]
    out_ref[...] = jnp.zeros_like(out_ref)
    row = lax.broadcasted_iota(jnp.int32, (PIECE, out_ref.shape[1]), 0)
    for lane in range(LANES):
        start = aligned(spans_ref[lane, 0])
        slots = row + start
        mine = (slots >= spans_ref[lane, 1]) & (slots < spans_ref[lane, 2])
        window = pl.ds(start, PIECE)
        out_ref[window, :] = jnp.where(mine, pieces[lane][...], out_ref[window, :])


def place_rows(spans, pieces, capacity):
    width = pieces[0].shape[1]
    return pl.pallas_call(
        place_kernel,
        out_shape=jax.ShapeDtypeStruct((capacity, width), BF16),
        in_specs=[SMEM] + [VMEM] * LANES,
        out_specs=VMEM,
        name="place_rows",
    )(spans, *pieces)


def ring_gather(block):
    half = block.shape[0] // 2
    ahead = shifted(block, "mp", 1)
    behind = shifted(block, "mp", -1)
    far = jnp.concatenate(
        [shifted(ahead[:half], "mp", 1), shifted(behind[half:], "mp", -1)], axis=0
    )
    return [block, ahead, far, behind]


def per_device(
    voxel_feats,
    slot_rank,
    curve_order,
    patch_shift,
    qkv_weight,
    proj_weight,
    up_weight,
    down_weight,
    norm_gains,
):
    bricks = lax.axis_size("brick")
    parts = lax.axis_size("mp")
    me = lax.axis_index("brick")
    capacity = voxel_feats.shape[0]
    shard = curve_order.shape[0]
    queries = PATCH // parts
    offset = patch_shift[0]
    lane_ids = jnp.arange(LANES, dtype=jnp.int32)
    last_start = capacity - PIECE

    targets = (me - lane_ids + 1) % bricks
    ends = jnp.stack([targets, targets + 1]) * shard
    counts = jnp.sum((slot_rank[None, None, :] < ends[:, :, None]).astype(jnp.int32), axis=2)
    run_start = jnp.minimum(counts[0] // TILE * TILE, last_start)
    spans = jnp.stack([run_start, counts[0], counts[1]], axis=1)

    piece0, piece2, piece3 = cut_windows(
        jnp.stack([run_start[0], run_start[2], run_start[3]]), voxel_feats
    )
    lane3 = shifted(piece3, "brick", -2)
    lane2 = shifted(piece2, "brick", -1)
    lane0 = shifted(piece0, "brick", 1)
    lanes = (lane0, lane2, lane3)

    span = GROUP_HEADS * HEAD_DIM
    column = jnp.arange(3 * span, dtype=jnp.int32)
    place = (column // HEAD_DIM % 3) * span + column // (3 * HEAD_DIM) * HEAD_DIM + column % HEAD_DIM
    order = (place[None, :] == column[:, None]).astype(BF16)
    qkv_rows = nt_dot(order, qkv_weight).astype(BF16)
    early = ring_gather(jnp.concatenate([qkv_rows, proj_weight], axis=0))
    late = ring_gather(jnp.concatenate([up_weight, down_weight], axis=0))
    qkv = [block[: 3 * span] for block in early]
    proj = [block[3 * span :] for block in early]
    up = [block[: up_weight.shape[0]] for block in late]
    down = [block[up_weight.shape[0] :] for block in late]

    source = curve_order // capacity
    slot = curve_order - source * capacity
    lane = (source - me + 1) % bricks
    from_lane = lane[None, :] == lane_ids[:, None]
    first_slot = jnp.min(jnp.where(from_lane, slot[None, :], capacity), axis=1)
    lane_start = jnp.minimum(first_slot // TILE * TILE, last_start)
    position = jnp.arange(shard, dtype=jnp.int32)
    block_first = jnp.arange(3 * BLOCKS, dtype=jnp.int32) * BLOCK + offset - PATCH
    before = jnp.sum(
        (from_lane[None, :, :] & (position[None, None, :] < block_first[:, None, None])).astype(
            jnp.int32
        ),
        axis=2,
    )
    table = jnp.clip(
        (first_slot - lane_start)[None, :] + before, 0, PIECE - WINDOW
    ) // TILE * TILE
    base = jnp.sum(jnp.where(from_lane, (lane_ids * WINDOW - lane_start)[:, None], 0), axis=0)
    fill = jnp.full((PATCH,), -1, jnp.int32)
    lane_wide = lax.dynamic_slice_in_dim(
        jnp.concatenate([fill, lane, fill]), offset, shard + PATCH, 0
    )
    spot_wide = lax.dynamic_slice_in_dim(
        jnp.concatenate([fill, slot + base, fill]), offset, shard + PATCH, 0
    )
    lane_wide = lane_wide.reshape(3 * BLOCKS, BLOCK)
    spot_wide = spot_wide.reshape(3 * BLOCKS, BLOCK)
    table_of = jnp.sum(
        jnp.where(lane_wide[:, :, None] == lane_ids[None, None, :], table[:, None, :], 0), axis=2
    )
    spots = jnp.where(lane_wide < 0, -1, spot_wide - table_of)
    tall = jnp.broadcast_to(spots.reshape(3, PATCH, 1), (3, PATCH, 128))

    own_start = jnp.stack([run_start[1], lax.axis_index("mp") * queries])
    head = head_rows(table[:BLOCKS], own_start, tall[0], voxel_feats, lanes)
    head_next = shifted(head, "brick", -1)
    common = (own_start, norm_gains, qkv, proj)

    def hidden_of(part, extra):
        rows = slice(part * BLOCKS, (part + 1) * BLOCKS)
        return attend(
            table[rows], own_start, tall[part], voxel_feats, lanes, norm_gains, qkv, proj, extra, queries
        )

    def columns_of(result):
        arrived = lax.all_to_all(result, "mp", split_axis=0, concat_axis=0, tiled=True)
        return arrived.reshape(PATCH, arrived.shape[2])

    first = columns_of(mlp(hidden_of(1, None), norm_gains, up, down))
    last = columns_of(mlp(hidden_of(2, head_next), norm_gains, up, down))
    tail = shifted(last, "brick", 1)
    back0, back1, back2, back3 = pack_lanes(table, spots, tail, first, last)
    pieces = (
        shifted(back0, "brick", -1),
        back1,
        shifted(back2, "brick", 1),
        shifted(back3, "brick", 2),
    )
    return place_rows(spans, pieces, capacity)


def solution(mesh):
    return jax.shard_map(
        per_device,
        mesh=mesh,
        in_specs=(
            P("brick", None),
            P("brick"),
            P("brick"),
            P(),
            P(None, "mp"),
            P("mp", None),
            P(None, "mp"),
            P("mp", None),
            P(),
        ),
        out_specs=P("brick", "mp"),
        check_vma=False,
    )
```

```python
import functools

import jax
import jax.numpy as jnp
from jax import lax
from jax.experimental import pallas as pl
from jax.experimental.pallas import tpu as pltpu
from jax.sharding import PartitionSpec as P

PATCH = 1024
HEAD_DIM = 16
GROUP_HEADS = 8
EPSILON = 1e-05
LOG2E = 1.4426950408889634

TILE = 16
BLOCK = 128
WINDOW = 160
MOST_RUN = 768
PIECE = MOST_RUN + TILE
LANES = 4
BLOCKS = PATCH // BLOCK

F32 = jnp.float32
BF16 = jnp.bfloat16

ANY = pl.BlockSpec(memory_space=pl.ANY)
VMEM = pl.BlockSpec(memory_space=pltpu.VMEM)
SMEM = pl.BlockSpec(memory_space=pltpu.SMEM)
HBM = pl.BlockSpec(memory_space=pltpu.HBM)


def nt_dot(left, right):
    return lax.dot_general(left, right, (((1,), (1,)), ((), ())), preferred_element_type=F32)


def nn_dot(left, right):
    return jnp.dot(left, right, preferred_element_type=F32)


def tn_dot(left, right):
    return lax.dot_general(left, right, (((0,), (0,)), ((), ())), preferred_element_type=F32)


def aligned(value):
    return pl.multiple_of(value, TILE)


def shifted(value, axis, steps):
    count = lax.axis_size(axis)
    pairs = [(source, (source + steps) % count) for source in range(count)]
    return lax.ppermute(value, axis, pairs)


def layer_norm(values, gain):
    values = values.astype(F32)
    centred = values - jnp.mean(values, axis=-1, keepdims=True)
    spread = jnp.mean(centred * centred, axis=-1, keepdims=True)
    return (centred * lax.rsqrt(spread + EPSILON) * gain).astype(BF16)


def window_start(first, capacity):
    return aligned(jnp.minimum(lax.div(first, TILE) * TILE, capacity - PIECE))


def cut_kernel(bricks, shard, ranks_ref, feats_ref, *rest):
    outs, counts_ref, sems = rest[:LANES], rest[LANES], rest[LANES + 1]
    capacity = feats_ref.shape[0]
    me = lax.axis_index("brick")
    ranks = ranks_ref[...]
    loads = []
    for lane in (3, 2, 0, 1):
        target = lax.rem(me - lane + 1 + bricks, bricks)
        first = jnp.sum((ranks < target * shard).astype(jnp.int32))
        counts_ref[0, lane] = first
        rows = pl.ds(window_start(first, capacity), PIECE)
        loads.append(pltpu.make_async_copy(feats_ref.at[rows], outs[lane], sems.at[lane]))
        loads[-1].start()
    for lane in range(LANES):
        target = lax.rem(me - lane + 1 + bricks, bricks)
        counts_ref[1, lane] = jnp.sum((ranks < (target + 1) * shard).astype(jnp.int32))
    for load in loads:
        load.wait()


def cut_windows(bricks, shard, ranks, feats):
    piece = jax.ShapeDtypeStruct((PIECE, feats.shape[1]), feats.dtype)
    return pl.pallas_call(
        functools.partial(cut_kernel, bricks, shard),
        out_shape=(piece,) * LANES + (jax.ShapeDtypeStruct((2, LANES), jnp.int32),),
        in_specs=[VMEM, HBM],
        out_specs=(VMEM,) * LANES + (SMEM,),
        scratch_shapes=[pltpu.SemaphoreType.DMA((LANES,))],
        compiler_params=pltpu.CompilerParams(vmem_limit_bytes=8 << 20),
        name="cut_windows",
    )(ranks, feats)


def index_kernel(bricks, capacity, shift_ref, order_ref, after_ref, spots_ref, table_ref, wide_ref):
    me = lax.axis_index("brick")
    order = order_ref[...]
    rows = order.shape[0]
    lane_of = jnp.zeros_like(order)
    spot_of = jnp.zeros_like(order)
    column = lax.broadcasted_iota(jnp.int32, (1, BLOCK), 1)
    leads = jnp.zeros((1, BLOCK), F32)
    for lane in range(LANES):
        source = lax.rem(me + lane - 1 + bricks, bricks)
        slot = order - source * capacity
        mine = (slot >= 0) & (slot < capacity)
        first = jnp.min(jnp.where(mine, slot, capacity), keepdims=True)
        start = jnp.minimum(first & -TILE, capacity - PIECE)
        lane_of = jnp.where(mine, lane, lane_of)
        spot_of = jnp.where(mine, slot - start + lane * WINDOW, spot_of)
        leads = jnp.where(column == lane, (first - start).astype(F32), leads)
    ahead = PATCH - shift_ref[0]
    down, across = lax.div(ahead, BLOCK), lax.rem(ahead, BLOCK)
    wide_ref[...] = jnp.full_like(wide_ref, -1)
    for index, value in enumerate((lane_of, spot_of)):
        turned = pltpu.roll(value, across, 1)
        wide_ref[index, 0, pl.ds(down, rows), :] = turned
        wide_ref[index, 1, pl.ds(down + 1, rows), :] = turned
    height = spots_ref.shape[0]
    near = lax.broadcasted_iota(jnp.int32, (height, BLOCK), 1) >= across
    lane_wide = jnp.where(near, wide_ref[0, 0, :height, :], wide_ref[0, 1, :height, :])
    spot_wide = jnp.where(near, wide_ref[1, 0, :height, :], wide_ref[1, 1, :height, :])
    held = jnp.zeros((height, BLOCK), F32)
    wide_column = lax.broadcasted_iota(jnp.int32, (height, BLOCK), 1)
    for lane in range(LANES):
        found = jnp.sum((lane_wide == lane).astype(F32), axis=1, keepdims=True)
        held = jnp.where(wide_column == lane, found, held)
    below = lax.broadcasted_iota(jnp.int32, (height, height), 1) < lax.broadcasted_iota(
        jnp.int32, (height, height), 0
    )
    before = nn_dot(below.astype(F32).astype(BF16), held.astype(BF16))
    table = jnp.minimum((leads + before).astype(jnp.int32) & -TILE, PIECE - WINDOW)
    table_ref[...] = table
    spots = spot_wide
    for lane in range(LANES):
        spots = jnp.where(lane_wide == lane, spot_wide - table[:, lane : lane + 1], spots)
    spots_ref[...] = jnp.where(lane_wide < 0, -1, spots)


def index_tables(bricks, capacity, shift, order, after):
    height = 3 * BLOCKS
    table = jax.ShapeDtypeStruct((height, BLOCK), jnp.int32)
    return pl.pallas_call(
        functools.partial(index_kernel, bricks, capacity),
        out_shape=(table, table),
        in_specs=[SMEM, VMEM, HBM],
        out_specs=(VMEM, VMEM),
        scratch_shapes=[pltpu.VMEM((2, 2, height + 2 * BLOCKS, BLOCK), jnp.int32)],
        compiler_params=pltpu.CompilerParams(vmem_limit_bytes=4 << 20),
        name="index_tables",
    )(shift, order, after)


def hot_rows(spots):
    tall = lax.broadcasted_iota(jnp.int32, (LANES * WINDOW, BLOCK), 0)
    return jnp.where(tall == spots, 1.0, 0.0).astype(BF16)


def gather_block(table_ref, spots_ref, place, lane_refs):
    windows = [
        lane_refs[lane][pl.ds(aligned(table_ref[place, lane]), WINDOW), :]
        for lane in range(LANES)
    ]
    stacked = jnp.concatenate(windows, axis=0)
    return tn_dot(hot_rows(spots_ref[place : place + 1, :]), stacked).astype(BF16)


def head_kernel(table_ref, spots_ref, *refs):
    out_ref = refs[-1]
    for block in range(BLOCKS):
        rows = slice(block * BLOCK, (block + 1) * BLOCK)
        out_ref[rows, :] = gather_block(table_ref, spots_ref, block, refs[:LANES])


def head_rows(table, spots, lanes, after):
    width = lanes[0].shape[1]
    return pl.pallas_call(
        head_kernel,
        out_shape=jax.ShapeDtypeStruct((PATCH, width), BF16),
        in_specs=[SMEM] + [VMEM] * (1 + LANES) + [ANY] * len(after),
        out_specs=VMEM,
        cost_estimate=pl.CostEstimate(
            flops=2 * PATCH * 768 * width, bytes_accessed=5 << 20, transcendentals=0
        ),
        compiler_params=pltpu.CompilerParams(vmem_limit_bytes=12 << 20),
        name="head_rows",
    )(table, spots, *lanes, *after)


def project_kernel(part, extras, table_ref, spots_ref, *refs):
    lane_refs, gain_ref = refs[:LANES], refs[LANES]
    near_ref, ahead_ref, far_a_ref, far_b_ref, behind_ref = refs[LANES + 1 : LANES + 6]
    extra_ref = refs[LANES + 6]
    own_ref, keys_ref, values_ref, query_ref, rows_ref, normed_ref, stack_ref = refs[-7:]
    queries = own_ref.shape[0]
    span = GROUP_HEADS * HEAD_DIM
    for group, ref in enumerate((near_ref, ahead_ref, None, behind_ref)):
        for kind in range(3):
            if ref is None:
                source = (far_a_ref, far_b_ref)[kind // 2]
                at = kind % 2 * span
            else:
                source, at = ref, kind * span
            stack_ref[kind, group * span : (group + 1) * span, :] = source[at : at + span, :]
    gain = gain_ref[0:1, :]
    for quarter in range(4):
        for block in range(quarter * 2, quarter * 2 + 2):
            rows = slice(block * BLOCK, (block + 1) * BLOCK)
            found = gather_block(table_ref, spots_ref, part * BLOCKS + BLOCKS + block, lane_refs)
            if part == 1:
                found = found + extra_ref[rows, :]
            rows_ref[rows, :] = found
            normed_ref[rows, :] = layer_norm(found, gain)
        rows = slice(quarter * 256, (quarter + 1) * 256)
        normed = normed_ref[rows, :]
        keys_ref[rows, :] = nt_dot(normed, stack_ref[1]).astype(BF16)
        values_ref[:, rows] = nt_dot(stack_ref[2], normed).astype(BF16)
    own_rows = pl.ds(pl.multiple_of(lax.axis_index("mp") * queries, queries), queries)
    own_ref[...] = rows_ref[own_rows, :]
    query = nt_dot(stack_ref[0], normed_ref[own_rows, :])
    query_ref[...] = (query * (HEAD_DIM ** (-0.5) * LOG2E)).astype(BF16)


def project(part, table, spots, lanes, gains, early, extra, queries):
    width = lanes[0].shape[1]
    shape = lambda *dims: jax.ShapeDtypeStruct(dims, BF16)
    return pl.pallas_call(
        functools.partial(project_kernel, part, len(extra)),
        out_shape=(shape(queries, width), shape(PATCH, width), shape(width, PATCH), shape(width, queries)),
        in_specs=[SMEM] + [VMEM] * (LANES + 7) + ([VMEM] + [ANY] * (len(extra) - 1) if part else [ANY] * len(extra)),
        out_specs=(VMEM,) * 4,
        scratch_shapes=[
            pltpu.VMEM((PATCH, width), BF16),
            pltpu.VMEM((PATCH, width), BF16),
            pltpu.VMEM((3, width, width), BF16),
        ],
        cost_estimate=pl.CostEstimate(flops=10 * 10**9, bytes_accessed=10 << 20, transcendentals=0),
        compiler_params=pltpu.CompilerParams(vmem_limit_bytes=20 << 20),
        name="project_last" if part else "project_first",
    )(table, spots, *lanes, gains, *early, *extra)


def attend_kernel(after, own_ref, keys_ref, values_ref, query_ref, *refs):
    near_ref, ahead_ref, far_b_ref, behind_ref = refs[:4]
    out_ref, mixed_ref, score_ref = refs[4 + after :]
    queries = own_ref.shape[0]
    groups = 4
    span = GROUP_HEADS * HEAD_DIM

    head_of_row = lax.broadcasted_iota(jnp.int32, (span, queries), 0) // HEAD_DIM
    ones = jnp.ones((HEAD_DIM, BLOCK), BF16)

    def query_of(group, head):
        query = query_ref[group * span : (group + 1) * span, :]
        return jnp.where(head_of_row == head, query, jnp.zeros_like(query))

    def score(slot, group, query, chunk, highest):
        rows = slice(chunk * BLOCK, (chunk + 1) * BLOCK)
        scores = nn_dot(keys_ref[rows, group * span : (group + 1) * span], query)
        score_ref[slot, rows, :] = scores
        top = jnp.max(scores.reshape(BLOCK // 8, 8, queries), axis=0)
        return top if highest is None else jnp.maximum(highest, top)

    highest = None
    query = query_of(0, 0)
    for chunk in range(BLOCKS):
        highest = score(0, 0, query, chunk, highest)

    def head_step(head, highest):
        for group in range(groups):
            top = jnp.max(highest, axis=0, keepdims=True)
            later = (group + 1) % groups
            query = query_of(later, head if later else jnp.minimum(head + 1, GROUP_HEADS - 1))
            rows = pl.ds(pl.multiple_of(group * span + head * HEAD_DIM, HEAD_DIM), HEAD_DIM)
            total, highest = None, None
            for chunk in range(BLOCKS):
                keys = slice(chunk * BLOCK, (chunk + 1) * BLOCK)
                highest = score(later % 2, later, query, chunk, highest)
                weights = jnp.exp2(score_ref[group % 2, keys, :] - top).astype(BF16)
                values = jnp.concatenate([values_ref[rows, keys], ones], axis=0)
                term = nn_dot(values, weights)
                total = term if total is None else total + term
            mixed_ref[rows, :] = (total[:HEAD_DIM] / total[HEAD_DIM : HEAD_DIM + 1]).astype(BF16)
        return highest

    lax.fori_loop(0, GROUP_HEADS, head_step, highest)
    mixed = None
    for group in range(groups):
        rows = slice(group * span, (group + 1) * span)
        weight = (near_ref, ahead_ref, far_b_ref, behind_ref)[group]
        weight = weight[span : 2 * span, :] if group == 2 else weight[3 * span :, :]
        term = tn_dot(mixed_ref[rows, :], weight).astype(BF16).astype(F32)
        mixed = term if mixed is None else mixed + term
    out_ref[...] = (own_ref[...].astype(F32) + mixed).astype(BF16)


def attend(part, projected, early, after):
    queries, width = projected[0].shape
    near, ahead, far_a, far_b, behind = early
    return pl.pallas_call(
        functools.partial(attend_kernel, len(after)),
        out_shape=jax.ShapeDtypeStruct((queries, width), BF16),
        in_specs=[VMEM] * 8 + [ANY] * len(after),
        out_specs=VMEM,
        scratch_shapes=[
            pltpu.VMEM((width, queries), BF16),
            pltpu.VMEM((2, PATCH, queries), F32),
        ],
        cost_estimate=pl.CostEstimate(
            flops=30 * 10**9, bytes_accessed=5 << 20, transcendentals=8 << 20
        ),
        compiler_params=pltpu.CompilerParams(vmem_limit_bytes=16 << 20),
        name="attend_last" if part else "attend_first",
    )(*projected, near, ahead, far_b, behind, *after)


def mlp_kernel(groups, hidden_ref, gain_ref, *refs):
    up_refs, down_refs = refs[:groups], refs[groups : 2 * groups]
    wide_ref, before_ref, result_ref = refs[-3:]
    outs = refs[-3 - groups : -3]
    queries, width = hidden_ref.shape
    normed = layer_norm(hidden_ref[...], gain_ref[1:2, :])
    pieces = [(group, chunk) for group in range(groups) for chunk in range(queries // BLOCK)]

    def widen(index):
        group, chunk = pieces[index]
        before_ref[index % 2] = nn_dot(normed[chunk * BLOCK : (chunk + 1) * BLOCK], up_refs[group][...])

    widen(0)
    for index, (group, chunk) in enumerate(pieces):
        if index + 1 < len(pieces):
            widen(index + 1)
        wide = before_ref[index % 2]
        wide_ref[group, chunk * BLOCK : (chunk + 1) * BLOCK, :] = (
            wide * (0.5 + 0.5 * lax.erf(wide * 0.5**0.5))
        ).astype(BF16)
    total = None
    for group in range(groups):
        term = nn_dot(wide_ref[group], down_refs[group][...]).astype(BF16).astype(F32)
        total = term if total is None else total + term
    result_ref[...] = (hidden_ref[...].astype(F32) + total).astype(BF16)
    cut = width // groups
    rank = lax.axis_index("mp")
    for step in range(groups):
        column = pl.multiple_of(lax.rem(rank + step, groups) * cut, cut)
        outs[step][...] = result_ref[:, pl.ds(column, cut)]


def mlp(hidden, gains, up, down, after):
    groups = len(up)
    rows, width = hidden.shape
    middle = up[0].shape[1]
    return pl.pallas_call(
        functools.partial(mlp_kernel, groups),
        out_shape=(jax.ShapeDtypeStruct((rows, width // groups), BF16),) * groups,
        in_specs=[VMEM] * (2 + 2 * groups) + [ANY] * len(after),
        out_specs=(VMEM,) * groups,
        scratch_shapes=[
            pltpu.VMEM((groups, rows, middle), BF16),
            pltpu.VMEM((2, BLOCK, middle), F32),
            pltpu.VMEM((rows, width), BF16),
        ],
        cost_estimate=pl.CostEstimate(
            flops=4 * rows * width * middle * groups, bytes_accessed=5 << 20, transcendentals=0
        ),
        compiler_params=pltpu.CompilerParams(vmem_limit_bytes=16 << 20),
        name="mlp",
    )(hidden, gains, *up, *down, *after)


def pack_kernel(shift_ref, table_ref, spots_ref, *rest):
    sources, rest = rest[:12], rest[12:]
    outs, lanes_ref, rows_ref = rest[:LANES], rest[LANES], rest[LANES + 1]
    queries = sources[0].shape[0]
    lanes_ref[...] = jnp.zeros_like(lanes_ref)
    rank = lax.axis_index("mp")
    for index, source in enumerate(sources):
        sender = lax.rem(rank - index % 4 + 4, 4)
        at = pl.multiple_of(index // 4 * PATCH + sender * queries, queries)
        rows_ref[pl.ds(at, queries), :] = source[...]
    begin = lax.div(PATCH - shift_ref[0], BLOCK)
    for step in range(2 * BLOCKS + 1):
        place = jnp.minimum(begin + step, 3 * BLOCKS - 1)
        fresh = begin + step < 3 * BLOCKS
        spots = jnp.where(fresh, spots_ref[pl.ds(place, 1), :], -1)
        rows = rows_ref[pl.ds(pl.multiple_of(place * BLOCK, BLOCK), BLOCK), :]
        sent = nn_dot(hot_rows(spots), rows).astype(BF16)
        for lane in range(LANES):
            window = pl.ds(aligned(table_ref[place, lane]), WINDOW)
            lanes_ref[lane, window, :] = (
                lanes_ref[lane, window, :] + sent[lane * WINDOW : (lane + 1) * WINDOW]
            )
    for lane in range(LANES):
        outs[lane][...] = lanes_ref[lane]


def pack_lanes(shift, table, spots, sources):
    width = sources[0].shape[1]
    return pl.pallas_call(
        pack_kernel,
        out_shape=(jax.ShapeDtypeStruct((PIECE, width), BF16),) * LANES,
        in_specs=[SMEM, SMEM] + [VMEM] * (1 + len(sources)),
        out_specs=(VMEM,) * LANES,
        scratch_shapes=[
            pltpu.VMEM((LANES, PIECE, width), BF16),
            pltpu.VMEM((3 * PATCH, width), BF16),
        ],
        compiler_params=pltpu.CompilerParams(vmem_limit_bytes=12 << 20),
        name="pack_lanes",
    )(shift, table, spots, *sources)


def place_kernel(counts_ref, *refs):
    pieces, out_ref = refs[:LANES], refs[LANES]
    capacity = out_ref.shape[0]
    out_ref[...] = jnp.zeros_like(out_ref)
    row = lax.broadcasted_iota(jnp.int32, (PIECE, out_ref.shape[1]), 0)
    for lane in range(LANES):
        start = window_start(counts_ref[0, lane], capacity)
        slots = row + start
        mine = (slots >= counts_ref[0, lane]) & (slots < counts_ref[1, lane])
        window = pl.ds(start, PIECE)
        out_ref[window, :] = jnp.where(mine, pieces[lane][...], out_ref[window, :])


def place_rows(counts, pieces, capacity):
    width = pieces[0].shape[1]
    return pl.pallas_call(
        place_kernel,
        out_shape=jax.ShapeDtypeStruct((capacity, width), BF16),
        in_specs=[SMEM] + [VMEM] * LANES,
        out_specs=VMEM,
        compiler_params=pltpu.CompilerParams(vmem_limit_bytes=12 << 20),
        name="place_rows",
    )(counts, *pieces)


def per_device(
    voxel_feats,
    slot_rank,
    curve_order,
    patch_shift,
    qkv_weight,
    proj_weight,
    up_weight,
    down_weight,
    norm_gains,
):
    bricks = lax.axis_size("brick")
    parts = lax.axis_size("mp")
    capacity, width = voxel_feats.shape
    shard = curve_order.shape[0]
    queries = PATCH // parts

    piece0, own, piece2, piece3, counts = cut_windows(
        bricks, shard, slot_rank.reshape(capacity // 128, 128), voxel_feats
    )
    lane3 = shifted(piece3, "brick", -2)
    lane2 = shifted(piece2, "brick", -1)
    lane0 = shifted(piece0, "brick", 1)
    lanes = (lane0, own, lane2, lane3)
    counts, qkv_weight, proj_weight = lax.optimization_barrier((counts, qkv_weight, proj_weight))

    span = GROUP_HEADS * HEAD_DIM
    column = jnp.arange(3 * span, dtype=jnp.int32)
    place = (column // HEAD_DIM % 3) * span + column // (3 * HEAD_DIM) * HEAD_DIM + column % HEAD_DIM
    order = (place[None, :] == column[:, None]).astype(BF16)
    qkv_rows = nt_dot(order, qkv_weight).astype(BF16)
    near = jnp.concatenate([qkv_rows, proj_weight], axis=0)
    ahead, behind = shifted(near, "mp", 1), shifted(near, "mp", -1)
    half = near.shape[0] // 2
    far_a, far_b = shifted(ahead[:half], "mp", 1), shifted(behind[half:], "mp", -1)
    early = (near, ahead, far_a, far_b, behind)
    ahead, behind, up_out, down_out = lax.optimization_barrier(
        (ahead, behind, up_weight, down_weight)
    )
    up_ahead, up_behind = shifted(up_out, "mp", 1), shifted(up_out, "mp", -1)
    down_ahead, down_behind = shifted(down_out, "mp", 1), shifted(down_out, "mp", -1)

    spots, table = index_tables(
        bricks, capacity, patch_shift, curve_order.reshape(shard // BLOCK, BLOCK), near
    )
    head = head_rows(table, spots, lanes, (far_a, far_b))
    head_next = shifted(head, "brick", -1)
    common = (table, spots, lanes, norm_gains, early)
    projected = project(0, *common, (head,), queries)
    up_ahead, down_behind, *projected = lax.optimization_barrier(
        (up_ahead, down_behind, *projected)
    )
    up_far, down_far = shifted(up_ahead, "mp", 1), shifted(down_behind, "mp", -1)
    up = (up_weight, up_ahead, up_far, up_behind)
    down = (down_weight, down_ahead, down_far, down_behind)
    hidden = attend(0, projected, early, ())
    projected = project(1, *common, (head_next, hidden), queries)
    blocks = mlp(hidden, norm_gains, up, down, (projected[0],))
    first = [blocks[0]] + [shifted(blocks[step], "mp", step) for step in range(1, parts)]
    hidden = attend(1, projected, early, (blocks[0],))
    blocks = mlp(hidden, norm_gains, up, down, ())
    last = [blocks[0]] + [shifted(blocks[step], "mp", step) for step in range(1, parts)]

    def onward(step):
        pairs = [
            (brick * parts + rank, (brick + 1) % bricks * parts + (rank + step) % parts)
            for brick in range(bricks)
            for rank in range(parts)
        ]
        return lax.ppermute(blocks[step], ("brick", "mp"), pairs)

    tail = [onward(step) for step in range(parts)]
    back0, back1, back2, back3 = pack_lanes(patch_shift, table, spots, (*tail, *first, *last))
    pieces = (
        shifted(back0, "brick", -1),
        back1,
        shifted(back2, "brick", 1),
        shifted(back3, "brick", 2),
    )
    return place_rows(counts, pieces, capacity)


def solution(mesh):
    return jax.shard_map(
        per_device,
        mesh=mesh,
        in_specs=(
            P("brick", None),
            P("brick"),
            P("brick"),
            P(),
            P(None, "mp"),
            P("mp", None),
            P(None, "mp"),
            P("mp", None),
            P(),
        ),
        out_specs=P("brick", "mp"),
        check_vma=False,
    )
```

```python
import functools

import jax
import jax.numpy as jnp
from jax import lax
from jax.experimental import pallas as pl
from jax.experimental.pallas import tpu as pltpu
from jax.sharding import PartitionSpec as P

PATCH = 1024
HEAD_DIM = 16
GROUP_HEADS = 8
EPSILON = 1e-05
LOG2E = 1.4426950408889634

TILE = 16
BLOCK = 128
WINDOW = 160
MOST_RUN = 768
PIECE = MOST_RUN + TILE
LANES = 4
BLOCKS = PATCH // BLOCK


F32 = jnp.float32
BF16 = jnp.bfloat16

ANY = pl.BlockSpec(memory_space=pl.ANY)
VMEM = pl.BlockSpec(memory_space=pltpu.VMEM)
SMEM = pl.BlockSpec(memory_space=pltpu.SMEM)
HBM = pl.BlockSpec(memory_space=pltpu.HBM)


def nt_dot(left, right):
    return lax.dot_general(left, right, (((1,), (1,)), ((), ())), preferred_element_type=F32)


def nn_dot(left, right):
    return jnp.dot(left, right, preferred_element_type=F32)


def tn_dot(left, right):
    return lax.dot_general(left, right, (((0,), (0,)), ((), ())), preferred_element_type=F32)


def aligned(value):
    return pl.multiple_of(value, TILE)


def shifted(value, axis, steps):
    count = lax.axis_size(axis)
    pairs = [(source, (source + steps) % count) for source in range(count)]
    return lax.ppermute(value, axis, pairs)


def layer_norm(values, gain):
    values = values.astype(F32)
    centred = values - jnp.mean(values, axis=-1, keepdims=True)
    spread = jnp.mean(centred * centred, axis=-1, keepdims=True)
    return (centred * lax.rsqrt(spread + EPSILON) * gain).astype(BF16)


def window_start(first, capacity):
    return aligned(jnp.minimum(lax.div(first, TILE) * TILE, capacity - PIECE))


def cut_kernel(bricks, shard, ranks_ref, feats_ref, *rest):
    outs, counts_ref, sems = rest[:LANES], rest[LANES], rest[LANES + 1]
    capacity = feats_ref.shape[0]
    me = lax.axis_index("brick")
    ranks = ranks_ref[...]
    loads = []
    for lane in (3, 2, 0, 1):
        target = lax.rem(me - lane + 1 + bricks, bricks)
        first = jnp.sum((ranks < target * shard).astype(jnp.int32))
        counts_ref[0, lane] = first
        rows = pl.ds(window_start(first, capacity), PIECE)
        loads.append(pltpu.make_async_copy(feats_ref.at[rows], outs[lane], sems.at[lane]))
        loads[-1].start()
    for lane in range(LANES):
        target = lax.rem(me - lane + 1 + bricks, bricks)
        counts_ref[1, lane] = jnp.sum((ranks < (target + 1) * shard).astype(jnp.int32))
    for load in loads:
        load.wait()


def cut_windows(bricks, shard, ranks, feats):
    piece = jax.ShapeDtypeStruct((PIECE, feats.shape[1]), feats.dtype)
    return pl.pallas_call(
        functools.partial(cut_kernel, bricks, shard),
        out_shape=(piece,) * LANES + (jax.ShapeDtypeStruct((2, LANES), jnp.int32),),
        in_specs=[VMEM, HBM],
        out_specs=(VMEM,) * LANES + (SMEM,),
        scratch_shapes=[pltpu.SemaphoreType.DMA((LANES,))],
        compiler_params=pltpu.CompilerParams(vmem_limit_bytes=60 << 20),
        name="cut_windows",
    )(ranks, feats)


def index_kernel(bricks, capacity, shift_ref, order_ref, after_ref, spots_ref, table_ref, wide_ref):
    me = lax.axis_index("brick")
    order = order_ref[...]
    rows = order.shape[0]
    lane_of = jnp.zeros_like(order)
    spot_of = jnp.zeros_like(order)
    column = lax.broadcasted_iota(jnp.int32, (1, BLOCK), 1)
    leads = jnp.zeros((1, BLOCK), F32)
    for lane in range(LANES):
        source = lax.rem(me + lane - 1 + bricks, bricks)
        slot = order - source * capacity
        mine = (slot >= 0) & (slot < capacity)
        first = jnp.min(jnp.where(mine, slot, capacity), keepdims=True)
        start = jnp.minimum(first & -TILE, capacity - PIECE)
        lane_of = jnp.where(mine, lane, lane_of)
        spot_of = jnp.where(mine, slot - start + lane * WINDOW, spot_of)
        leads = jnp.where(column == lane, (first - start).astype(F32), leads)
    ahead = PATCH - shift_ref[0]
    down, across = lax.div(ahead, BLOCK), lax.rem(ahead, BLOCK)
    wide_ref[...] = jnp.full_like(wide_ref, -1)
    for index, value in enumerate((lane_of, spot_of)):
        turned = pltpu.roll(value, across, 1)
        wide_ref[index, 0, pl.ds(down, rows), :] = turned
        wide_ref[index, 1, pl.ds(down + 1, rows), :] = turned
    height = spots_ref.shape[0]
    near = lax.broadcasted_iota(jnp.int32, (height, BLOCK), 1) >= across
    lane_wide = jnp.where(near, wide_ref[0, 0, :height, :], wide_ref[0, 1, :height, :])
    spot_wide = jnp.where(near, wide_ref[1, 0, :height, :], wide_ref[1, 1, :height, :])
    held = jnp.zeros((height, BLOCK), F32)
    wide_column = lax.broadcasted_iota(jnp.int32, (height, BLOCK), 1)
    for lane in range(LANES):
        found = jnp.sum((lane_wide == lane).astype(F32), axis=1, keepdims=True)
        held = jnp.where(wide_column == lane, found, held)
    below = lax.broadcasted_iota(jnp.int32, (height, height), 1) < lax.broadcasted_iota(
        jnp.int32, (height, height), 0
    )
    before = nn_dot(below.astype(F32).astype(BF16), held.astype(BF16))
    table = jnp.minimum((leads + before).astype(jnp.int32) & -TILE, PIECE - WINDOW)
    table_ref[...] = table
    spots = spot_wide
    for lane in range(LANES):
        spots = jnp.where(lane_wide == lane, spot_wide - table[:, lane : lane + 1], spots)
    spots_ref[...] = jnp.where(lane_wide < 0, -1, spots)


def index_tables(bricks, capacity, shift, order, after):
    height = 3 * BLOCKS
    table = jax.ShapeDtypeStruct((height, BLOCK), jnp.int32)
    return pl.pallas_call(
        functools.partial(index_kernel, bricks, capacity),
        out_shape=(table, table),
        in_specs=[SMEM, VMEM, HBM],
        out_specs=(VMEM, VMEM),
        scratch_shapes=[pltpu.VMEM((2, 2, height + 2 * BLOCKS, BLOCK), jnp.int32)],
        compiler_params=pltpu.CompilerParams(vmem_limit_bytes=4 << 20),
        name="index_tables",
    )(shift, order, after)


def hot_rows(spots):
    tall = lax.broadcasted_iota(jnp.int32, (LANES * WINDOW, BLOCK), 0)
    return jnp.where(tall == spots, 1.0, 0.0).astype(BF16)


def gather_block(table_ref, spots_ref, place, lane_refs):
    windows = [
        lane_refs[lane][pl.ds(aligned(table_ref[place, lane]), WINDOW), :]
        for lane in range(LANES)
    ]
    stacked = jnp.concatenate(windows, axis=0)
    return tn_dot(hot_rows(spots_ref[place : place + 1, :]), stacked).astype(BF16)


def head_kernel(table_ref, spots_ref, *refs):
    out_ref = refs[-1]
    for block in range(BLOCKS):
        rows = slice(block * BLOCK, (block + 1) * BLOCK)
        out_ref[rows, :] = gather_block(table_ref, spots_ref, block, refs[:LANES])


def head_rows(table, spots, lanes, after):
    width = lanes[0].shape[1]
    return pl.pallas_call(
        head_kernel,
        out_shape=jax.ShapeDtypeStruct((PATCH, width), BF16),
        in_specs=[SMEM] + [VMEM] * (1 + LANES) + [ANY] * len(after),
        out_specs=VMEM,
        cost_estimate=pl.CostEstimate(
            flops=2 * PATCH * 768 * width, bytes_accessed=5 << 20, transcendentals=0
        ),
        compiler_params=pltpu.CompilerParams(vmem_limit_bytes=12 << 20),
        name="head_rows",
    )(table, spots, *lanes, *after)


def project_kernel(part, table_ref, spots_ref, *refs):
    lane_refs, gain_ref = refs[:LANES], refs[LANES]
    near_ref, ahead_ref, far_a_ref, far_b_ref, behind_ref = refs[LANES + 1 : LANES + 6]
    extra_ref = refs[LANES + 6]
    own_ref, keys_ref, values_ref, query_ref, rows_ref, normed_ref, stack_ref = refs[-7:]
    queries = own_ref.shape[0]
    span = GROUP_HEADS * HEAD_DIM
    for group, ref in enumerate((near_ref, ahead_ref, None, behind_ref)):
        for kind in range(3):
            if ref is None:
                source = (far_a_ref, far_b_ref)[kind // 2]
                at = kind % 2 * span
            else:
                source, at = ref, kind * span
            stack_ref[kind, group * span : (group + 1) * span, :] = source[at : at + span, :]
    gain = gain_ref[0:1, :]
    for quarter in range(4):
        for block in range(quarter * 2, quarter * 2 + 2):
            rows = slice(block * BLOCK, (block + 1) * BLOCK)
            found = gather_block(table_ref, spots_ref, part * BLOCKS + BLOCKS + block, lane_refs)
            if part == 1:
                found = found + extra_ref[rows, :]
            rows_ref[rows, :] = found
            normed_ref[rows, :] = layer_norm(found, gain)
        rows = slice(quarter * 256, (quarter + 1) * 256)
        normed = normed_ref[rows, :]
        keys_ref[rows, :] = nt_dot(normed, stack_ref[1]).astype(BF16)
        values_ref[:, rows] = nt_dot(stack_ref[2], normed).astype(BF16)
    own_rows = pl.ds(pl.multiple_of(lax.axis_index("mp") * queries, queries), queries)
    own_ref[...] = rows_ref[own_rows, :]
    query = nt_dot(stack_ref[0], normed_ref[own_rows, :])
    query_ref[...] = (query * (HEAD_DIM ** (-0.5) * LOG2E)).astype(BF16)


def project(part, table, spots, lanes, gains, early, extra, queries):
    width = lanes[0].shape[1]
    shape = lambda *dims: jax.ShapeDtypeStruct(dims, BF16)
    return pl.pallas_call(
        functools.partial(project_kernel, part),
        out_shape=(shape(queries, width), shape(PATCH, width), shape(width, PATCH), shape(width, queries)),
        in_specs=[SMEM] + [VMEM] * (LANES + 7) + ([VMEM] + [ANY] * (len(extra) - 1) if part else [ANY] * len(extra)),
        out_specs=(VMEM,) * 4,
        scratch_shapes=[
            pltpu.VMEM((PATCH, width), BF16),
            pltpu.VMEM((PATCH, width), BF16),
            pltpu.VMEM((3, width, width), BF16),
        ],
        cost_estimate=pl.CostEstimate(flops=10 * 10**9, bytes_accessed=10 << 20, transcendentals=0),
        compiler_params=pltpu.CompilerParams(vmem_limit_bytes=20 << 20),
        name="project_last" if part else "project_first",
    )(table, spots, *lanes, gains, *early, *extra)


def attend_kernel(groups, final, keys_ref, values_ref, query_ref, *refs):
    mixed_ref, score_ref = refs[-2:]
    out_ref = refs[-3] if final else None
    queries = query_ref.shape[1]
    span = GROUP_HEADS * HEAD_DIM
    first = groups[0]

    head_of_row = lax.broadcasted_iota(jnp.int32, (span, queries), 0) // HEAD_DIM
    ones = jnp.ones((HEAD_DIM, BLOCK), BF16)

    def query_of(group, head):
        query = query_ref[group * span : (group + 1) * span, :]
        return jnp.where(head_of_row == head, query, jnp.zeros_like(query))

    def score(slot, group, query, chunk, highest):
        rows = slice(chunk * BLOCK, (chunk + 1) * BLOCK)
        scores = nn_dot(keys_ref[rows, group * span : (group + 1) * span], query)
        score_ref[slot, rows, :] = scores
        top = jnp.max(scores.reshape(BLOCK // 8, 8, queries), axis=0)
        return top if highest is None else jnp.maximum(highest, top)

    highest = None
    query = query_of(first, 0)
    for chunk in range(BLOCKS):
        highest = score(0, first, query, chunk, highest)

    def head_step(head, highest):
        for index, group in enumerate(groups):
            top = jnp.max(highest, axis=0, keepdims=True)
            last = index + 1 == len(groups)
            later = groups[0] if last else groups[index + 1]
            query = query_of(later, jnp.minimum(head + 1, GROUP_HEADS - 1) if last else head)
            rows = pl.ds(pl.multiple_of(group * span + head * HEAD_DIM, HEAD_DIM), HEAD_DIM)
            total, highest = None, None
            for chunk in range(BLOCKS):
                keys = slice(chunk * BLOCK, (chunk + 1) * BLOCK)
                highest = score((index + 1) % 2, later, query, chunk, highest)
                weights = jnp.exp2(score_ref[index % 2, keys, :] - top).astype(BF16)
                values = jnp.concatenate([values_ref[rows, keys], ones], axis=0)
                term = nn_dot(values, weights)
                total = term if total is None else total + term
            held = pl.ds(pl.multiple_of((group - first) * span + head * HEAD_DIM, HEAD_DIM), HEAD_DIM)
            mixed_ref[held, :] = (total[:HEAD_DIM] / total[HEAD_DIM : HEAD_DIM + 1]).astype(BF16)
        return highest

    lax.fori_loop(0, GROUP_HEADS, head_step, highest)
    if not final:
        return
    own_ref, near_ref, ahead_ref, far_b_ref, behind_ref = refs[:5]
    mixed = None
    for group in range(4):
        if group < first:
            held = refs[5][group * span : (group + 1) * span, :]
        else:
            held = mixed_ref[(group - first) * span : (group - first + 1) * span, :]
        weight = (near_ref, ahead_ref, far_b_ref, behind_ref)[group]
        weight = weight[span : 2 * span, :] if group == 2 else weight[3 * span :, :]
        term = tn_dot(held, weight).astype(BF16).astype(F32)
        mixed = term if mixed is None else mixed + term
    out_ref[...] = (own_ref[...].astype(F32) + mixed).astype(BF16)


def attend(groups, projected, early, prior, after):
    own, keys, values, query = projected
    queries, width = own.shape
    span = GROUP_HEADS * HEAD_DIM
    height = len(groups) * span
    final = groups[-1] == 3
    near, ahead, _, far_b, behind = early
    operands = [keys, values, query]
    if final:
        operands += [own, near, ahead, far_b, behind, *prior]
    scratch = [pltpu.VMEM((2, PATCH, queries), F32)]
    if final:
        scratch = [pltpu.VMEM((height, queries), BF16)] + scratch
    return pl.pallas_call(
        functools.partial(attend_kernel, groups, final),
        out_shape=jax.ShapeDtypeStruct((queries, width) if final else (height, queries), BF16),
        in_specs=[VMEM] * len(operands) + [ANY] * len(after),
        out_specs=VMEM,
        scratch_shapes=scratch,
        cost_estimate=pl.CostEstimate(
            flops=8 * 10**9 * len(groups),
            bytes_accessed=5 << 20,
            transcendentals=(2 << 20) * len(groups),
        ),
        compiler_params=pltpu.CompilerParams(vmem_limit_bytes=16 << 20),
    )(*operands, *after)


def mlp_kernel(groups, hidden_ref, gain_ref, *refs):
    up_refs, down_refs = refs[:groups], refs[groups : 2 * groups]
    wide_ref, before_ref, result_ref = refs[-3:]
    outs = refs[-3 - groups : -3]
    queries, width = hidden_ref.shape
    normed = layer_norm(hidden_ref[...], gain_ref[1:2, :])
    pieces = [(group, chunk) for group in range(groups) for chunk in range(queries // BLOCK)]

    def widen(index):
        group, chunk = pieces[index]
        before_ref[index % 2] = nn_dot(normed[chunk * BLOCK : (chunk + 1) * BLOCK], up_refs[group][...])

    widen(0)
    for index, (group, chunk) in enumerate(pieces):
        if index + 1 < len(pieces):
            widen(index + 1)
        wide = before_ref[index % 2]
        wide_ref[group, chunk * BLOCK : (chunk + 1) * BLOCK, :] = (
            wide * (0.5 + 0.5 * lax.erf(wide * 0.5**0.5))
        ).astype(BF16)
    total = None
    for group in range(groups):
        term = nn_dot(wide_ref[group], down_refs[group][...]).astype(BF16).astype(F32)
        total = term if total is None else total + term
    result_ref[...] = (hidden_ref[...].astype(F32) + total).astype(BF16)
    cut = width // groups
    rank = lax.axis_index("mp")
    for step in range(groups):
        column = pl.multiple_of(lax.rem(rank + step, groups) * cut, cut)
        outs[step][...] = result_ref[:, pl.ds(column, cut)]


def mlp(hidden, gains, up, down, after):
    groups = len(up)
    rows, width = hidden.shape
    middle = up[0].shape[1]
    return pl.pallas_call(
        functools.partial(mlp_kernel, groups),
        out_shape=(jax.ShapeDtypeStruct((rows, width // groups), BF16),) * groups,
        in_specs=[VMEM] * (2 + 2 * groups) + [ANY] * len(after),
        out_specs=(VMEM,) * groups,
        scratch_shapes=[
            pltpu.VMEM((groups, rows, middle), BF16),
            pltpu.VMEM((2, BLOCK, middle), F32),
            pltpu.VMEM((rows, width), BF16),
        ],
        cost_estimate=pl.CostEstimate(
            flops=4 * rows * width * middle * groups, bytes_accessed=5 << 20, transcendentals=0
        ),
        compiler_params=pltpu.CompilerParams(vmem_limit_bytes=16 << 20),
        name="mlp",
    )(hidden, gains, *up, *down, *after)


def pack_kernel(shift_ref, table_ref, spots_ref, *rest):
    sources, rest = rest[:12], rest[12:]
    outs, lanes_ref, rows_ref = rest[:LANES], rest[LANES], rest[LANES + 1]
    queries = sources[0].shape[0]
    lanes_ref[...] = jnp.zeros_like(lanes_ref)
    rank = lax.axis_index("mp")
    for index, source in enumerate(sources):
        sender = lax.rem(rank - index % 4 + 4, 4)
        at = pl.multiple_of(index // 4 * PATCH + sender * queries, queries)
        rows_ref[pl.ds(at, queries), :] = source[...]
    begin = lax.div(PATCH - shift_ref[0], BLOCK)
    for step in range(2 * BLOCKS + 1):
        place = jnp.minimum(begin + step, 3 * BLOCKS - 1)
        fresh = begin + step < 3 * BLOCKS
        spots = jnp.where(fresh, spots_ref[pl.ds(place, 1), :], -1)
        rows = rows_ref[pl.ds(pl.multiple_of(place * BLOCK, BLOCK), BLOCK), :]
        sent = nn_dot(hot_rows(spots), rows).astype(BF16)
        for lane in range(LANES):
            window = pl.ds(aligned(table_ref[place, lane]), WINDOW)
            lanes_ref[lane, window, :] = (
                lanes_ref[lane, window, :] + sent[lane * WINDOW : (lane + 1) * WINDOW]
            )
    for lane in range(LANES):
        outs[lane][...] = lanes_ref[lane]


def pack_lanes(shift, table, spots, sources):
    width = sources[0].shape[1]
    return pl.pallas_call(
        pack_kernel,
        out_shape=(jax.ShapeDtypeStruct((PIECE, width), BF16),) * LANES,
        in_specs=[SMEM, SMEM] + [VMEM] * (1 + len(sources)),
        out_specs=(VMEM,) * LANES,
        scratch_shapes=[
            pltpu.VMEM((LANES, PIECE, width), BF16),
            pltpu.VMEM((3 * PATCH, width), BF16),
        ],
        compiler_params=pltpu.CompilerParams(vmem_limit_bytes=12 << 20),
        name="pack_lanes",
    )(shift, table, spots, *sources)


def place_kernel(counts_ref, *refs):
    pieces, out_ref = refs[:LANES], refs[LANES]
    capacity = out_ref.shape[0]
    out_ref[...] = jnp.zeros_like(out_ref)
    row = lax.broadcasted_iota(jnp.int32, (PIECE, out_ref.shape[1]), 0)
    for lane in range(LANES):
        start = window_start(counts_ref[0, lane], capacity)
        slots = row + start
        mine = (slots >= counts_ref[0, lane]) & (slots < counts_ref[1, lane])
        window = pl.ds(start, PIECE)
        out_ref[window, :] = jnp.where(mine, pieces[lane][...], out_ref[window, :])


def place_rows(counts, pieces, capacity):
    width = pieces[0].shape[1]
    return pl.pallas_call(
        place_kernel,
        out_shape=jax.ShapeDtypeStruct((capacity, width), BF16),
        in_specs=[SMEM] + [VMEM] * LANES,
        out_specs=VMEM,
        compiler_params=pltpu.CompilerParams(vmem_limit_bytes=12 << 20),
        name="place_rows",
    )(counts, *pieces)


def body(
    voxel_feats,
    slot_rank,
    curve_order,
    patch_shift,
    qkv_weight,
    proj_weight,
    up_weight,
    down_weight,
    norm_gains,
):
    bricks = lax.axis_size("brick")
    parts = lax.axis_size("mp")
    capacity, _ = voxel_feats.shape
    shard = curve_order.shape[0]
    queries = PATCH // parts

    piece0, own, piece2, piece3, counts = cut_windows(
        bricks, shard, slot_rank.reshape(capacity // 128, 128), voxel_feats
    )
    lane3 = shifted(piece3, "brick", -2)
    lane2 = shifted(piece2, "brick", -1)
    lane0 = shifted(piece0, "brick", 1)
    lanes = (lane0, own, lane2, lane3)
    counts, qkv_weight, proj_weight = lax.optimization_barrier((counts, qkv_weight, proj_weight))

    span = GROUP_HEADS * HEAD_DIM
    column = jnp.arange(3 * span, dtype=jnp.int32)
    place = (column // HEAD_DIM % 3) * span + column // (3 * HEAD_DIM) * HEAD_DIM + column % HEAD_DIM
    order = (place[None, :] == column[:, None]).astype(BF16)
    qkv_rows = nt_dot(order, qkv_weight).astype(BF16)
    near = jnp.concatenate([qkv_rows, proj_weight], axis=0)
    ahead, behind = shifted(near, "mp", 1), shifted(near, "mp", -1)
    half = near.shape[0] // 2
    far_a, far_b = shifted(ahead[:half], "mp", 1), shifted(behind[half:], "mp", -1)
    early = (near, ahead, far_a, far_b, behind)
    ahead, behind, up_out, down_out = lax.optimization_barrier(
        (ahead, behind, up_weight, down_weight)
    )
    up_ahead, up_behind = shifted(up_out, "mp", 1), shifted(up_out, "mp", -1)
    down_ahead, down_behind = shifted(down_out, "mp", 1), shifted(down_out, "mp", -1)

    spots, table = index_tables(
        bricks, capacity, patch_shift, curve_order.reshape(shard // BLOCK, BLOCK), near
    )
    head = head_rows(table, spots, lanes, (far_a, far_b))
    head_next = shifted(head, "brick", -1)
    common = (table, spots, lanes, norm_gains, early)
    patch0 = project(0, *common, (head,), queries)
    mixed = attend((0, 1), patch0, early, (), ())
    up_ahead, down_behind, mixed = lax.optimization_barrier((up_ahead, down_behind, mixed))
    up_far, down_far = shifted(up_ahead, "mp", 1), shifted(down_behind, "mp", -1)
    up = (up_weight, up_ahead, up_far, up_behind)
    down = (down_weight, down_ahead, down_far, down_behind)
    patch1 = project(1, *common, (head_next, mixed), queries)

    blocks = mlp(attend((0, 1, 2, 3), patch1, early, (), ()), norm_gains, up, down, ())

    def onward(step):
        pairs = [
            (brick * parts + rank, (brick + 1) % bricks * parts + (rank + step) % parts)
            for brick in range(bricks)
            for rank in range(parts)
        ]
        return lax.ppermute(blocks[step], ("brick", "mp"), pairs)

    tail, last = [], [blocks[0]]
    for step in range(parts):
        tail.append(onward(step))
        if step:
            last.append(shifted(blocks[step], "mp", step))
    hidden = attend((2, 3), patch0, early, (mixed,), (blocks[0],))
    blocks = mlp(hidden, norm_gains, up, down, ())
    first = [blocks[0]] + [shifted(blocks[step], "mp", step) for step in range(1, parts)]
    back0, back1, back2, back3 = pack_lanes(patch_shift, table, spots, (*tail, *first, *last))
    pieces = (
        shifted(back0, "brick", -1),
        back1,
        shifted(back2, "brick", 1),
        shifted(back3, "brick", 2),
    )
    return place_rows(counts, pieces, capacity)


def solution(mesh):
    return jax.shard_map(
        body,
        mesh=mesh,
        in_specs=(
            P("brick", None),
            P("brick"),
            P("brick"),
            P(),
            P(None, "mp"),
            P("mp", None),
            P(None, "mp"),
            P("mp", None),
            P(),
        ),
        out_specs=P("brick", "mp"),
        check_vma=False,
    )
```

```python
import functools

import jax
import jax.numpy as jnp
from jax import lax
from jax.experimental import pallas as pl
from jax.experimental.pallas import tpu as pltpu
from jax.sharding import PartitionSpec as P

PATCH = 1024
HEAD_DIM = 16
GROUP_HEADS = 8
EPSILON = 1e-05
LOG2E = 1.4426950408889634

TILE = 16
BLOCK = 128
WINDOW = 160
MOST_RUN = 768
PIECE = MOST_RUN + TILE
LANES = 4
BLOCKS = PATCH // BLOCK


F32 = jnp.float32
BF16 = jnp.bfloat16

ANY = pl.BlockSpec(memory_space=pl.ANY)
VMEM = pl.BlockSpec(memory_space=pltpu.VMEM)
SMEM = pl.BlockSpec(memory_space=pltpu.SMEM)
HBM = pl.BlockSpec(memory_space=pltpu.HBM)


def nt_dot(left, right):
    return lax.dot_general(left, right, (((1,), (1,)), ((), ())), preferred_element_type=F32)


def nn_dot(left, right):
    return jnp.dot(left, right, preferred_element_type=F32)


def tn_dot(left, right):
    return lax.dot_general(left, right, (((0,), (0,)), ((), ())), preferred_element_type=F32)


def aligned(value):
    return pl.multiple_of(value, TILE)


def shifted(value, axis, steps):
    count = lax.axis_size(axis)
    pairs = [(source, (source + steps) % count) for source in range(count)]
    return lax.ppermute(value, axis, pairs)


def layer_norm(values, gain):
    values = values.astype(F32)
    centred = values - jnp.mean(values, axis=-1, keepdims=True)
    spread = jnp.mean(centred * centred, axis=-1, keepdims=True)
    return (centred * lax.rsqrt(spread + EPSILON) * gain).astype(BF16)


def window_start(first, capacity):
    return aligned(jnp.minimum(lax.div(first, TILE) * TILE, capacity - PIECE))


def cut_kernel(bricks, shard, ranks_ref, feats_ref, *rest):
    outs, counts_ref, sems = rest[:LANES], rest[LANES], rest[LANES + 1]
    capacity = feats_ref.shape[0]
    me = lax.axis_index("brick")
    ranks = ranks_ref[...]
    loads = []
    for lane in (3, 2, 0, 1):
        target = lax.rem(me - lane + 1 + bricks, bricks)
        first = jnp.sum((ranks < target * shard).astype(jnp.int32))
        counts_ref[0, lane] = first
        rows = pl.ds(window_start(first, capacity), PIECE)
        loads.append(pltpu.make_async_copy(feats_ref.at[rows], outs[lane], sems.at[lane]))
        loads[-1].start()
    for lane in range(LANES):
        target = lax.rem(me - lane + 1 + bricks, bricks)
        counts_ref[1, lane] = jnp.sum((ranks < (target + 1) * shard).astype(jnp.int32))
    for load in loads:
        load.wait()


def cut_windows(bricks, shard, ranks, feats):
    piece = jax.ShapeDtypeStruct((PIECE, feats.shape[1]), feats.dtype)
    return pl.pallas_call(
        functools.partial(cut_kernel, bricks, shard),
        out_shape=(piece,) * LANES + (jax.ShapeDtypeStruct((2, LANES), jnp.int32),),
        in_specs=[VMEM, HBM],
        out_specs=(VMEM,) * LANES + (SMEM,),
        scratch_shapes=[pltpu.SemaphoreType.DMA((LANES,))],
        compiler_params=pltpu.CompilerParams(vmem_limit_bytes=8 << 20),
        name="cut_windows",
    )(ranks, pltpu.with_memory_space_constraint(feats, pltpu.HBM))


def index_kernel(bricks, capacity, shift_ref, order_ref, after_ref, spots_ref, table_ref, wide_ref):
    me = lax.axis_index("brick")
    order = order_ref[...]
    rows = order.shape[0]
    lane_of = jnp.zeros_like(order)
    spot_of = jnp.zeros_like(order)
    column = lax.broadcasted_iota(jnp.int32, (1, BLOCK), 1)
    leads = jnp.zeros((1, BLOCK), F32)
    for lane in range(LANES):
        source = lax.rem(me + lane - 1 + bricks, bricks)
        slot = order - source * capacity
        mine = (slot >= 0) & (slot < capacity)
        first = jnp.min(jnp.where(mine, slot, capacity), keepdims=True)
        start = jnp.minimum(first & -TILE, capacity - PIECE)
        lane_of = jnp.where(mine, lane, lane_of)
        spot_of = jnp.where(mine, slot - start + lane * WINDOW, spot_of)
        leads = jnp.where(column == lane, (first - start).astype(F32), leads)
    ahead = PATCH - shift_ref[0]
    down, across = lax.div(ahead, BLOCK), lax.rem(ahead, BLOCK)
    wide_ref[...] = jnp.full_like(wide_ref, -1)
    for index, value in enumerate((lane_of, spot_of)):
        turned = pltpu.roll(value, across, 1)
        wide_ref[index, 0, pl.ds(down, rows), :] = turned
        wide_ref[index, 1, pl.ds(down + 1, rows), :] = turned
    height = spots_ref.shape[0]
    near = lax.broadcasted_iota(jnp.int32, (height, BLOCK), 1) >= across
    lane_wide = jnp.where(near, wide_ref[0, 0, :height, :], wide_ref[0, 1, :height, :])
    spot_wide = jnp.where(near, wide_ref[1, 0, :height, :], wide_ref[1, 1, :height, :])
    held = jnp.zeros((height, BLOCK), F32)
    wide_column = lax.broadcasted_iota(jnp.int32, (height, BLOCK), 1)
    for lane in range(LANES):
        found = jnp.sum((lane_wide == lane).astype(F32), axis=1, keepdims=True)
        held = jnp.where(wide_column == lane, found, held)
    below = lax.broadcasted_iota(jnp.int32, (height, height), 1) < lax.broadcasted_iota(
        jnp.int32, (height, height), 0
    )
    before = nn_dot(below.astype(F32).astype(BF16), held.astype(BF16))
    table = jnp.minimum((leads + before).astype(jnp.int32) & -TILE, PIECE - WINDOW)
    table_ref[...] = table
    spots = spot_wide
    for lane in range(LANES):
        spots = jnp.where(lane_wide == lane, spot_wide - table[:, lane : lane + 1], spots)
    spots_ref[...] = jnp.where(lane_wide < 0, -1, spots)


def index_tables(bricks, capacity, shift, order, after):
    height = 3 * BLOCKS
    table = jax.ShapeDtypeStruct((height, BLOCK), jnp.int32)
    return pl.pallas_call(
        functools.partial(index_kernel, bricks, capacity),
        out_shape=(table, table),
        in_specs=[SMEM, VMEM, HBM],
        out_specs=(VMEM, VMEM),
        scratch_shapes=[pltpu.VMEM((2, 2, height + 2 * BLOCKS, BLOCK), jnp.int32)],
        compiler_params=pltpu.CompilerParams(vmem_limit_bytes=4 << 20),
        name="index_tables",
    )(shift, order, after)


def hot_rows(spots):
    tall = lax.broadcasted_iota(jnp.int32, (LANES * WINDOW, BLOCK), 0)
    return jnp.where(tall == spots, 1.0, 0.0).astype(BF16)


def gather_block(table_ref, spots_ref, place, lane_refs):
    windows = [
        lane_refs[lane][pl.ds(aligned(table_ref[place, lane]), WINDOW), :]
        for lane in range(LANES)
    ]
    stacked = jnp.concatenate(windows, axis=0)
    return tn_dot(hot_rows(spots_ref[place : place + 1, :]), stacked).astype(BF16)


def head_kernel(table_ref, spots_ref, *refs):
    out_ref = refs[-1]
    for block in range(BLOCKS):
        rows = slice(block * BLOCK, (block + 1) * BLOCK)
        out_ref[rows, :] = gather_block(table_ref, spots_ref, block, refs[:LANES])


def head_rows(table, spots, lanes, after):
    width = lanes[0].shape[1]
    return pl.pallas_call(
        head_kernel,
        out_shape=jax.ShapeDtypeStruct((PATCH, width), BF16),
        in_specs=[SMEM] + [VMEM] * (1 + LANES) + [ANY] * len(after),
        out_specs=VMEM,
        cost_estimate=pl.CostEstimate(
            flops=2 * PATCH * 768 * width, bytes_accessed=5 << 20, transcendentals=0
        ),
        compiler_params=pltpu.CompilerParams(vmem_limit_bytes=12 << 20),
        name="head_rows",
    )(table, spots, *lanes, *after)


def project_kernel(part, table_ref, spots_ref, *refs):
    lane_refs, gain_ref = refs[:LANES], refs[LANES]
    near_ref, ahead_ref, far_a_ref, far_b_ref, behind_ref = refs[LANES + 1 : LANES + 6]
    extra_ref = refs[LANES + 6]
    own_ref, keys_ref, values_ref, query_ref, rows_ref, normed_ref, stack_ref = refs[-7:]
    queries = own_ref.shape[0]
    span = GROUP_HEADS * HEAD_DIM
    for group, ref in enumerate((near_ref, ahead_ref, None, behind_ref)):
        for kind in range(3):
            if ref is None:
                source = (far_a_ref, far_b_ref)[kind // 2]
                at = kind % 2 * span
            else:
                source, at = ref, kind * span
            stack_ref[kind, group * span : (group + 1) * span, :] = source[at : at + span, :]
    gain = gain_ref[0:1, :]
    for quarter in range(4):
        for block in range(quarter * 2, quarter * 2 + 2):
            rows = slice(block * BLOCK, (block + 1) * BLOCK)
            found = gather_block(table_ref, spots_ref, part * BLOCKS + BLOCKS + block, lane_refs)
            if part == 1:
                found = found + extra_ref[rows, :]
            rows_ref[rows, :] = found
            normed_ref[rows, :] = layer_norm(found, gain)
        rows = slice(quarter * 256, (quarter + 1) * 256)
        normed = normed_ref[rows, :]
        keys_ref[rows, :] = nt_dot(normed, stack_ref[1]).astype(BF16)
        values_ref[:, rows] = nt_dot(stack_ref[2], normed).astype(BF16)
    own_rows = pl.ds(pl.multiple_of(lax.axis_index("mp") * queries, queries), queries)
    own_ref[...] = rows_ref[own_rows, :]
    query = nt_dot(stack_ref[0], normed_ref[own_rows, :])
    query_ref[...] = (query * (HEAD_DIM ** (-0.5) * LOG2E)).astype(BF16)


def project(part, table, spots, lanes, gains, early, extra, queries):
    width = lanes[0].shape[1]
    shape = lambda *dims: jax.ShapeDtypeStruct(dims, BF16)
    return pl.pallas_call(
        functools.partial(project_kernel, part),
        out_shape=(shape(queries, width), shape(PATCH, width), shape(width, PATCH), shape(width, queries)),
        in_specs=[SMEM] + [VMEM] * (LANES + 7) + ([VMEM] + [ANY] * (len(extra) - 1) if part else [ANY] * len(extra)),
        out_specs=(VMEM,) * 4,
        scratch_shapes=[
            pltpu.VMEM((PATCH, width), BF16),
            pltpu.VMEM((PATCH, width), BF16),
            pltpu.VMEM((3, width, width), BF16),
        ],
        cost_estimate=pl.CostEstimate(flops=10 * 10**9, bytes_accessed=10 << 20, transcendentals=0),
        compiler_params=pltpu.CompilerParams(vmem_limit_bytes=20 << 20),
        name="project_last" if part else "project_first",
    )(table, spots, *lanes, gains, *early, *extra)


def attend_kernel(groups, final, keys_ref, values_ref, query_ref, *refs):
    mixed_ref, score_ref = refs[-2:]
    out_ref = refs[-3] if final else None
    queries = query_ref.shape[1]
    span = GROUP_HEADS * HEAD_DIM
    first = groups[0]

    head_of_row = lax.broadcasted_iota(jnp.int32, (span, queries), 0) // HEAD_DIM
    ones = jnp.ones((HEAD_DIM, BLOCK), BF16)

    def query_of(group, head):
        query = query_ref[group * span : (group + 1) * span, :]
        return jnp.where(head_of_row == head, query, jnp.zeros_like(query))

    def score(slot, group, query, chunk, highest):
        rows = slice(chunk * BLOCK, (chunk + 1) * BLOCK)
        scores = nn_dot(keys_ref[rows, group * span : (group + 1) * span], query)
        score_ref[slot, rows, :] = scores
        top = jnp.max(scores.reshape(BLOCK // 8, 8, queries), axis=0)
        return top if highest is None else jnp.maximum(highest, top)

    highest = None
    query = query_of(first, 0)
    for chunk in range(BLOCKS):
        highest = score(0, first, query, chunk, highest)

    def head_step(head, highest):
        for index, group in enumerate(groups):
            top = jnp.max(highest, axis=0, keepdims=True)
            last = index + 1 == len(groups)
            later = groups[0] if last else groups[index + 1]
            query = query_of(later, jnp.minimum(head + 1, GROUP_HEADS - 1) if last else head)
            rows = pl.ds(pl.multiple_of(group * span + head * HEAD_DIM, HEAD_DIM), HEAD_DIM)
            total, highest = None, None
            for chunk in range(BLOCKS):
                keys = slice(chunk * BLOCK, (chunk + 1) * BLOCK)
                highest = score((index + 1) % 2, later, query, chunk, highest)
                weights = jnp.exp2(score_ref[index % 2, keys, :] - top).astype(BF16)
                values = jnp.concatenate([values_ref[rows, keys], ones], axis=0)
                term = nn_dot(values, weights)
                total = term if total is None else total + term
            held = pl.ds(pl.multiple_of((group - first) * span + head * HEAD_DIM, HEAD_DIM), HEAD_DIM)
            mixed_ref[held, :] = (total[:HEAD_DIM] / total[HEAD_DIM : HEAD_DIM + 1]).astype(BF16)
        return highest

    lax.fori_loop(0, GROUP_HEADS, head_step, highest)
    if not final:
        return
    own_ref, near_ref, ahead_ref, far_b_ref, behind_ref = refs[:5]
    mixed = None
    for group in range(4):
        if group < first:
            held = refs[5][group * span : (group + 1) * span, :]
        else:
            held = mixed_ref[(group - first) * span : (group - first + 1) * span, :]
        weight = (near_ref, ahead_ref, far_b_ref, behind_ref)[group]
        weight = weight[span : 2 * span, :] if group == 2 else weight[3 * span :, :]
        term = tn_dot(held, weight).astype(BF16).astype(F32)
        mixed = term if mixed is None else mixed + term
    out_ref[...] = (own_ref[...].astype(F32) + mixed).astype(BF16)


def attend(groups, projected, early, prior, after):
    own, keys, values, query = projected
    queries, width = own.shape
    span = GROUP_HEADS * HEAD_DIM
    height = len(groups) * span
    final = groups[-1] == 3
    near, ahead, _, far_b, behind = early
    operands = [keys, values, query]
    if final:
        operands += [own, near, ahead, far_b, behind, *prior]
    scratch = [pltpu.VMEM((2, PATCH, queries), F32)]
    if final:
        scratch = [pltpu.VMEM((height, queries), BF16)] + scratch
    return pl.pallas_call(
        functools.partial(attend_kernel, groups, final),
        out_shape=jax.ShapeDtypeStruct((queries, width) if final else (height, queries), BF16),
        in_specs=[VMEM] * len(operands) + [ANY] * len(after),
        out_specs=VMEM,
        scratch_shapes=scratch,
        cost_estimate=pl.CostEstimate(
            flops=8 * 10**9 * len(groups),
            bytes_accessed=5 << 20,
            transcendentals=(2 << 20) * len(groups),
        ),
        compiler_params=pltpu.CompilerParams(vmem_limit_bytes=16 << 20),
    )(*operands, *after)


def mlp_kernel(groups, hidden_ref, gain_ref, up_ref, down_ref, ahead_ref, far_up_ref, far_down_ref, behind_ref, *refs):
    depth = hidden_ref.shape[1]
    up_refs = (up_ref, ahead_ref.at[:depth], far_up_ref, behind_ref.at[:depth])
    down_refs = (down_ref, ahead_ref.at[depth:], far_down_ref, behind_ref.at[depth:])
    wide_ref, before_ref, result_ref = refs[-3:]
    outs = refs[-3 - groups : -3]
    queries, width = hidden_ref.shape
    normed = layer_norm(hidden_ref[...], gain_ref[1:2, :])
    pieces = [(group, chunk) for group in range(groups) for chunk in range(queries // BLOCK)]

    def widen(index):
        group, chunk = pieces[index]
        before_ref[index % 2] = nn_dot(normed[chunk * BLOCK : (chunk + 1) * BLOCK], up_refs[group][...])

    widen(0)
    for index, (group, chunk) in enumerate(pieces):
        if index + 1 < len(pieces):
            widen(index + 1)
        wide = before_ref[index % 2]
        wide_ref[group, chunk * BLOCK : (chunk + 1) * BLOCK, :] = (
            wide * (0.5 + 0.5 * lax.erf(wide * 0.5**0.5))
        ).astype(BF16)
    total = None
    for group in range(groups):
        term = nn_dot(wide_ref[group], down_refs[group][...]).astype(BF16).astype(F32)
        total = term if total is None else total + term
    result_ref[...] = (hidden_ref[...].astype(F32) + total).astype(BF16)
    cut = width // groups
    rank = lax.axis_index("mp")
    for step in range(groups):
        column = pl.multiple_of(lax.rem(rank + step, groups) * cut, cut)
        outs[step][...] = result_ref[:, pl.ds(column, cut)]


def mlp(hidden, gains, weights):
    groups = 4
    rows, width = hidden.shape
    middle = weights[0].shape[1]
    return pl.pallas_call(
        functools.partial(mlp_kernel, groups),
        out_shape=(jax.ShapeDtypeStruct((rows, width // groups), BF16),) * groups,
        in_specs=[VMEM] * 8,
        out_specs=(VMEM,) * groups,
        scratch_shapes=[
            pltpu.VMEM((groups, rows, middle), BF16),
            pltpu.VMEM((2, BLOCK, middle), F32),
            pltpu.VMEM((rows, width), BF16),
        ],
        cost_estimate=pl.CostEstimate(
            flops=4 * rows * width * middle * groups, bytes_accessed=5 << 20, transcendentals=0
        ),
        compiler_params=pltpu.CompilerParams(vmem_limit_bytes=16 << 20),
        name="mlp",
    )(hidden, gains, *weights)


def collect_kernel(*refs):
    sources, out_ref = refs[:4], refs[4]
    collect(sources, out_ref, 0)


def collect(sources, out_ref, base):
    queries = sources[0].shape[0]
    rank = lax.axis_index("mp")
    for index, source in enumerate(sources):
        sender = lax.rem(rank - index + 4, 4)
        at = pl.multiple_of(base + sender * queries, queries)
        out_ref[pl.ds(at, queries), :] = source[...]


def collect_rows(sources):
    return pl.pallas_call(
        collect_kernel,
        out_shape=jax.ShapeDtypeStruct((PATCH, sources[0].shape[1]), BF16),
        in_specs=[VMEM] * 4,
        out_specs=VMEM,
        compiler_params=pltpu.CompilerParams(vmem_limit_bytes=4 << 20),
        name="collect_rows",
    )(*sources)


def pack_kernel(shift_ref, table_ref, spots_ref, *rest):
    tail_ref, last_ref, sources, rest = rest[0], rest[1], rest[2:6], rest[6:]
    outs, lanes_ref, rows_ref = rest[:LANES], rest[LANES], rest[LANES + 1]
    lanes_ref[...] = jnp.zeros_like(lanes_ref)
    rows_ref[:PATCH, :] = tail_ref[...]
    rows_ref[2 * PATCH :, :] = last_ref[...]
    collect(sources, rows_ref, PATCH)
    begin = lax.div(PATCH - shift_ref[0], BLOCK)
    for step in range(2 * BLOCKS + 1):
        place = jnp.minimum(begin + step, 3 * BLOCKS - 1)
        fresh = begin + step < 3 * BLOCKS
        spots = jnp.where(fresh, spots_ref[pl.ds(place, 1), :], -1)
        rows = rows_ref[pl.ds(pl.multiple_of(place * BLOCK, BLOCK), BLOCK), :]
        sent = nn_dot(hot_rows(spots), rows).astype(BF16)
        for lane in range(LANES):
            window = pl.ds(aligned(table_ref[place, lane]), WINDOW)
            lanes_ref[lane, window, :] = (
                lanes_ref[lane, window, :] + sent[lane * WINDOW : (lane + 1) * WINDOW]
            )
    for lane in range(LANES):
        outs[lane][...] = lanes_ref[lane]


def pack_lanes(shift, table, spots, sources):
    width = sources[0].shape[1]
    return pl.pallas_call(
        pack_kernel,
        out_shape=(jax.ShapeDtypeStruct((PIECE, width), BF16),) * LANES,
        in_specs=[SMEM, SMEM] + [VMEM] * (1 + len(sources)),
        out_specs=(VMEM,) * LANES,
        scratch_shapes=[
            pltpu.VMEM((LANES, PIECE, width), BF16),
            pltpu.VMEM((3 * PATCH, width), BF16),
        ],
        compiler_params=pltpu.CompilerParams(vmem_limit_bytes=12 << 20),
        name="pack_lanes",
    )(shift, table, spots, *sources)


def place_kernel(counts_ref, *refs):
    pieces, out_ref = refs[:LANES], refs[LANES]
    capacity = out_ref.shape[0]
    out_ref[...] = jnp.zeros_like(out_ref)
    row = lax.broadcasted_iota(jnp.int32, (PIECE, out_ref.shape[1]), 0)
    for lane in range(LANES):
        start = window_start(counts_ref[0, lane], capacity)
        slots = row + start
        mine = (slots >= counts_ref[0, lane]) & (slots < counts_ref[1, lane])
        window = pl.ds(start, PIECE)
        out_ref[window, :] = jnp.where(mine, pieces[lane][...], out_ref[window, :])


def place_rows(counts, pieces, capacity):
    width = pieces[0].shape[1]
    return pl.pallas_call(
        place_kernel,
        out_shape=jax.ShapeDtypeStruct((capacity, width), BF16),
        in_specs=[SMEM] + [VMEM] * LANES,
        out_specs=VMEM,
        compiler_params=pltpu.CompilerParams(vmem_limit_bytes=12 << 20),
        name="place_rows",
    )(counts, *pieces)


def body(
    voxel_feats,
    slot_rank,
    curve_order,
    patch_shift,
    qkv_weight,
    proj_weight,
    up_weight,
    down_weight,
    norm_gains,
):
    bricks = lax.axis_size("brick")
    parts = lax.axis_size("mp")
    capacity, _ = voxel_feats.shape
    shard = curve_order.shape[0]
    queries = PATCH // parts

    piece0, own, piece2, piece3, counts = cut_windows(
        bricks, shard, slot_rank.reshape(capacity // 128, 128), voxel_feats
    )
    lane3 = shifted(piece3, "brick", -2)
    lane2 = shifted(piece2, "brick", -1)
    lane0 = shifted(piece0, "brick", 1)
    lanes = (lane0, own, lane2, lane3)
    counts, qkv_weight, proj_weight = lax.optimization_barrier((counts, qkv_weight, proj_weight))

    span = GROUP_HEADS * HEAD_DIM
    column = jnp.arange(3 * span, dtype=jnp.int32)
    place = (column // HEAD_DIM % 3) * span + column // (3 * HEAD_DIM) * HEAD_DIM + column % HEAD_DIM
    order = (place[None, :] == column[:, None]).astype(BF16)
    qkv_rows = nt_dot(order, qkv_weight).astype(BF16)
    near = jnp.concatenate([qkv_rows, proj_weight], axis=0)
    ahead, behind = shifted(near, "mp", 1), shifted(near, "mp", -1)
    half = near.shape[0] // 2
    far_a, far_b = shifted(ahead[:half], "mp", 1), shifted(behind[half:], "mp", -1)
    early = (near, ahead, far_a, far_b, behind)
    late = jnp.concatenate([up_weight, down_weight], axis=0)
    late, ahead, behind = lax.optimization_barrier((late, ahead, behind))
    late_ahead, late_behind = shifted(late, "mp", 1), shifted(late, "mp", -1)

    spots, table = index_tables(
        bricks, capacity, patch_shift, curve_order.reshape(shard // BLOCK, BLOCK), near
    )
    head = head_rows(table, spots, lanes, (far_a, far_b))
    head_next = shifted(head, "brick", -1)
    common = (table, spots, lanes, norm_gains, early)
    patch0 = project(0, *common, (head,), queries)
    mixed = attend((0, 1), patch0, early, (), ())
    late_ahead, late_behind, mixed = lax.optimization_barrier((late_ahead, late_behind, mixed))
    middle = late.shape[0] // 2
    far_up = shifted(late_ahead[:middle], "mp", 1)
    far_down = shifted(late_behind[middle:], "mp", -1)
    weights = (up_weight, down_weight, late_ahead, far_up, far_down, late_behind)
    patch1 = project(1, *common, (head_next, mixed), queries)

    blocks = mlp(attend((0, 1, 2, 3), patch1, early, (), ()), norm_gains, weights)

    last = [blocks[0]]
    for step in range(1, parts):
        last.append(shifted(blocks[step], "mp", step))
    hidden = attend((2, 3), patch0, early, (mixed,), (blocks[0],))
    last = collect_rows(last)
    tail = shifted(last, "brick", 1)
    blocks = mlp(hidden, norm_gains, weights)
    first = [blocks[0]] + [shifted(blocks[step], "mp", step) for step in range(1, parts)]
    back0, back1, back2, back3 = pack_lanes(patch_shift, table, spots, (tail, last, *first))
    back3 = shifted(back3, "brick", 2)
    back2 = shifted(back2, "brick", 1)
    back0 = shifted(back0, "brick", -1)
    return place_rows(counts, (back0, back1, back2, back3), capacity)


def solution(mesh):
    return jax.shard_map(
        body,
        mesh=mesh,
        in_specs=(
            P("brick", None),
            P("brick"),
            P("brick"),
            P(),
            P(None, "mp"),
            P("mp", None),
            P(None, "mp"),
            P("mp", None),
            P(),
        ),
        out_specs=P("brick", "mp"),
        check_vma=False,
    )
```

```python
import functools

import jax
import jax.numpy as jnp
from jax import lax
from jax.experimental import pallas as pl
from jax.experimental.pallas import tpu as pltpu
from jax.sharding import PartitionSpec as P

PATCH = 1024
HEAD_DIM = 16
GROUP_HEADS = 8
EPSILON = 1e-05
LOG2E = 1.4426950408889634

TILE = 16
BLOCK = 128
WINDOW = 160
MOST_RUN = 768
PIECE = MOST_RUN + TILE
LANES = 4
BLOCKS = PATCH // BLOCK


F32 = jnp.float32
BF16 = jnp.bfloat16

ANY = pl.BlockSpec(memory_space=pl.ANY)
VMEM = pl.BlockSpec(memory_space=pltpu.VMEM)
SMEM = pl.BlockSpec(memory_space=pltpu.SMEM)
HBM = pl.BlockSpec(memory_space=pltpu.HBM)


def nt_dot(left, right):
    return lax.dot_general(left, right, (((1,), (1,)), ((), ())), preferred_element_type=F32)


def nn_dot(left, right):
    return jnp.dot(left, right, preferred_element_type=F32)


def tn_dot(left, right):
    return lax.dot_general(left, right, (((0,), (0,)), ((), ())), preferred_element_type=F32)


def aligned(value):
    return pl.multiple_of(value, TILE)


def shifted(value, axis, steps):
    count = lax.axis_size(axis)
    pairs = [(source, (source + steps) % count) for source in range(count)]
    return lax.ppermute(value, axis, pairs)


def layer_norm(values, gain):
    values = values.astype(F32)
    centred = values - jnp.mean(values, axis=-1, keepdims=True)
    spread = jnp.mean(centred * centred, axis=-1, keepdims=True)
    return (centred * lax.rsqrt(spread + EPSILON) * gain).astype(BF16)


def window_start(first, capacity):
    return aligned(jnp.minimum(lax.div(first, TILE) * TILE, capacity - PIECE))


def cut_kernel(bricks, shard, ranks_ref, feats_ref, *rest):
    outs, counts_ref, sems = rest[:LANES], rest[LANES], rest[LANES + 1]
    capacity = feats_ref.shape[0]
    me = lax.axis_index("brick")
    ranks = ranks_ref[...]
    loads = []
    for lane in (3, 2, 0, 1):
        target = lax.rem(me - lane + 1 + bricks, bricks)
        first = jnp.sum((ranks < target * shard).astype(jnp.int32))
        counts_ref[0, lane] = first
        rows = pl.ds(window_start(first, capacity), PIECE)
        loads.append(pltpu.make_async_copy(feats_ref.at[rows], outs[lane], sems.at[lane]))
        loads[-1].start()
    for lane in range(LANES):
        target = lax.rem(me - lane + 1 + bricks, bricks)
        counts_ref[1, lane] = jnp.sum((ranks < (target + 1) * shard).astype(jnp.int32))
    for load in loads:
        load.wait()


def cut_windows(bricks, shard, ranks, feats):
    piece = jax.ShapeDtypeStruct((PIECE, feats.shape[1]), feats.dtype)
    return pl.pallas_call(
        functools.partial(cut_kernel, bricks, shard),
        out_shape=(piece,) * LANES + (jax.ShapeDtypeStruct((2, LANES), jnp.int32),),
        in_specs=[VMEM, HBM],
        out_specs=(VMEM,) * LANES + (SMEM,),
        scratch_shapes=[pltpu.SemaphoreType.DMA((LANES,))],
        compiler_params=pltpu.CompilerParams(vmem_limit_bytes=8 << 20),
        name="cut_windows",
    )(ranks, pltpu.with_memory_space_constraint(feats, pltpu.HBM))


def weights_kernel(qkv_ref, proj_ref, up_ref, down_ref, after_ref, near_ref, half_ref):
    span = GROUP_HEADS * HEAD_DIM
    shape = (3 * span, 3 * span)
    row = lax.broadcasted_iota(jnp.int32, shape, 0)
    column = lax.broadcasted_iota(jnp.int32, shape, 1)
    kind, rest = row // span, row % span
    source = rest // HEAD_DIM * (3 * HEAD_DIM) + kind * HEAD_DIM + rest % HEAD_DIM
    order = jnp.where(column == source, 1.0, 0.0).astype(BF16)
    near_ref[: 3 * span, :] = nt_dot(order, qkv_ref[...]).astype(BF16)
    near_ref[3 * span :, :] = proj_ref[...]
    odd = lax.rem(lax.axis_index("brick"), 2) == 1

    @pl.when(jnp.logical_not(odd))
    def _():
        half_ref[: 2 * span, :] = near_ref[: 2 * span, :]
        half_ref[2 * span :, :] = up_ref[...]

    @pl.when(odd)
    def _():
        half_ref[: 2 * span, :] = near_ref[2 * span :, :]
        half_ref[2 * span :, :] = down_ref[...]


def sort_weights(qkv, proj, up, down, after):
    width = proj.shape[1]
    span = GROUP_HEADS * HEAD_DIM
    return pl.pallas_call(
        weights_kernel,
        out_shape=(
            jax.ShapeDtypeStruct((4 * span, width), BF16),
            jax.ShapeDtypeStruct((2 * span + up.shape[0], width), BF16),
        ),
        in_specs=[VMEM] * 4 + [ANY],
        out_specs=(VMEM, VMEM),
        compiler_params=pltpu.CompilerParams(vmem_limit_bytes=8 << 20),
        name="sort_weights",
    )(qkv, proj, up, down, after)


def index_kernel(bricks, capacity, shift_ref, order_ref, after_ref, spots_ref, table_ref, wide_ref):
    me = lax.axis_index("brick")
    order = order_ref[...]
    rows = order.shape[0]
    lane_of = jnp.zeros_like(order)
    spot_of = jnp.zeros_like(order)
    column = lax.broadcasted_iota(jnp.int32, (1, BLOCK), 1)
    leads = jnp.zeros((1, BLOCK), F32)
    for lane in range(LANES):
        source = lax.rem(me + lane - 1 + bricks, bricks)
        slot = order - source * capacity
        mine = (slot >= 0) & (slot < capacity)
        first = jnp.min(jnp.where(mine, slot, capacity), keepdims=True)
        start = jnp.minimum(first & -TILE, capacity - PIECE)
        lane_of = jnp.where(mine, lane, lane_of)
        spot_of = jnp.where(mine, slot - start + lane * WINDOW, spot_of)
        leads = jnp.where(column == lane, (first - start).astype(F32), leads)
    ahead = PATCH - shift_ref[0]
    down, across = lax.div(ahead, BLOCK), lax.rem(ahead, BLOCK)
    wide_ref[...] = jnp.full_like(wide_ref, -1)
    for index, value in enumerate((lane_of, spot_of)):
        turned = pltpu.roll(value, across, 1)
        wide_ref[index, 0, pl.ds(down, rows), :] = turned
        wide_ref[index, 1, pl.ds(down + 1, rows), :] = turned
    height = spots_ref.shape[0]
    near = lax.broadcasted_iota(jnp.int32, (height, BLOCK), 1) >= across
    lane_wide = jnp.where(near, wide_ref[0, 0, :height, :], wide_ref[0, 1, :height, :])
    spot_wide = jnp.where(near, wide_ref[1, 0, :height, :], wide_ref[1, 1, :height, :])
    held = jnp.zeros((height, BLOCK), F32)
    wide_column = lax.broadcasted_iota(jnp.int32, (height, BLOCK), 1)
    for lane in range(LANES):
        found = jnp.sum((lane_wide == lane).astype(F32), axis=1, keepdims=True)
        held = jnp.where(wide_column == lane, found, held)
    below = lax.broadcasted_iota(jnp.int32, (height, height), 1) < lax.broadcasted_iota(
        jnp.int32, (height, height), 0
    )
    before = nn_dot(below.astype(F32).astype(BF16), held.astype(BF16))
    table = jnp.minimum((leads + before).astype(jnp.int32) & -TILE, PIECE - WINDOW)
    table_ref[...] = table
    spots = spot_wide
    for lane in range(LANES):
        spots = jnp.where(lane_wide == lane, spot_wide - table[:, lane : lane + 1], spots)
    spots_ref[...] = jnp.where(lane_wide < 0, -1, spots)


def index_tables(bricks, capacity, shift, order, after):
    height = 3 * BLOCKS
    table = jax.ShapeDtypeStruct((height, BLOCK), jnp.int32)
    return pl.pallas_call(
        functools.partial(index_kernel, bricks, capacity),
        out_shape=(table, table),
        in_specs=[SMEM, VMEM, HBM],
        out_specs=(VMEM, VMEM),
        scratch_shapes=[pltpu.VMEM((2, 2, height + 2 * BLOCKS, BLOCK), jnp.int32)],
        compiler_params=pltpu.CompilerParams(vmem_limit_bytes=4 << 20),
        name="index_tables",
    )(shift, order, after)


def hot_rows(spots):
    tall = lax.broadcasted_iota(jnp.int32, (LANES * WINDOW, BLOCK), 0)
    return jnp.where(tall == spots, 1.0, 0.0).astype(BF16)


def gather_block(table_ref, spots_ref, place, lane_refs):
    windows = [
        lane_refs[lane][pl.ds(aligned(table_ref[place, lane]), WINDOW), :]
        for lane in range(LANES)
    ]
    stacked = jnp.concatenate(windows, axis=0)
    return tn_dot(hot_rows(spots_ref[place : place + 1, :]), stacked).astype(BF16)


def head_kernel(table_ref, spots_ref, *refs):
    out_ref = refs[-1]
    for block in range(BLOCKS):
        rows = slice(block * BLOCK, (block + 1) * BLOCK)
        out_ref[rows, :] = gather_block(table_ref, spots_ref, block, refs[:LANES])


def head_rows(table, spots, lanes, after):
    width = lanes[0].shape[1]
    return pl.pallas_call(
        head_kernel,
        out_shape=jax.ShapeDtypeStruct((PATCH, width), BF16),
        in_specs=[SMEM] + [VMEM] * (1 + LANES) + [ANY] * len(after),
        out_specs=VMEM,
        cost_estimate=pl.CostEstimate(
            flops=2 * PATCH * 768 * width, bytes_accessed=5 << 20, transcendentals=0
        ),
        compiler_params=pltpu.CompilerParams(vmem_limit_bytes=12 << 20),
        name="head_rows",
    )(table, spots, *lanes, *after)


def by_core(fill, weight_refs):
    odd = lax.rem(lax.axis_index("brick"), 2) == 1
    ahead, far, _, behind, ahead_other, far_other, _, behind_other = weight_refs[1:]
    mine, other = (ahead, far, behind), (ahead_other, far_other, behind_other)

    @pl.when(jnp.logical_not(odd))
    def _():
        fill(mine, other)

    @pl.when(odd)
    def _():
        fill(other, mine)


def project_kernel(part, table_ref, spots_ref, *refs):
    lane_refs, gain_ref = refs[:LANES], refs[LANES]
    weight_refs = refs[LANES + 1 : LANES + 10]
    extra_ref = refs[LANES + 10]
    own_ref, keys_ref, values_ref, query_ref, rows_ref, normed_ref, stack_ref = refs[-7:]
    queries = own_ref.shape[0]
    span = GROUP_HEADS * HEAD_DIM
    near_ref = weight_refs[0]
    for kind in range(3):
        stack_ref[kind, :span, :] = near_ref[kind * span : (kind + 1) * span, :]

    def fill(evens, odds):
        for group in range(1, 4):
            rows = slice(group * span, (group + 1) * span)
            stack_ref[0, rows, :] = evens[group - 1][:span, :]
            stack_ref[1, rows, :] = evens[group - 1][span : 2 * span, :]
            stack_ref[2, rows, :] = odds[group - 1][:span, :]

    by_core(fill, weight_refs)
    gain = gain_ref[0:1, :]
    for quarter in range(4):
        for block in range(quarter * 2, quarter * 2 + 2):
            rows = slice(block * BLOCK, (block + 1) * BLOCK)
            found = gather_block(table_ref, spots_ref, part * BLOCKS + BLOCKS + block, lane_refs)
            if part == 1:
                found = found + extra_ref[rows, :]
            rows_ref[rows, :] = found
            normed_ref[rows, :] = layer_norm(found, gain)
        rows = slice(quarter * 256, (quarter + 1) * 256)
        normed = normed_ref[rows, :]
        keys_ref[rows, :] = nt_dot(normed, stack_ref[1]).astype(BF16)
        values_ref[:, rows] = nt_dot(stack_ref[2], normed).astype(BF16)
    own_rows = pl.ds(pl.multiple_of(lax.axis_index("mp") * queries, queries), queries)
    own_ref[...] = rows_ref[own_rows, :]
    query = nt_dot(stack_ref[0], normed_ref[own_rows, :])
    query_ref[...] = (query * (HEAD_DIM ** (-0.5) * LOG2E)).astype(BF16)


def project(part, table, spots, lanes, gains, early, extra, queries):
    width = lanes[0].shape[1]
    shape = lambda *dims: jax.ShapeDtypeStruct(dims, BF16)
    return pl.pallas_call(
        functools.partial(project_kernel, part),
        out_shape=(shape(queries, width), shape(PATCH, width), shape(width, PATCH), shape(width, queries)),
        in_specs=[SMEM] + [VMEM] * (LANES + 11) + ([VMEM] + [ANY] * (len(extra) - 1) if part else [ANY] * len(extra)),
        out_specs=(VMEM,) * 4,
        scratch_shapes=[
            pltpu.VMEM((PATCH, width), BF16),
            pltpu.VMEM((PATCH, width), BF16),
            pltpu.VMEM((3, width, width), BF16),
        ],
        cost_estimate=pl.CostEstimate(flops=10 * 10**9, bytes_accessed=10 << 20, transcendentals=0),
        compiler_params=pltpu.CompilerParams(vmem_limit_bytes=20 << 20),
        name="project_last" if part else "project_first",
    )(table, spots, *lanes, gains, *early, *extra)


def attend_kernel(groups, final, keys_ref, values_ref, query_ref, *refs):
    mixed_ref, score_ref = refs[-2:]
    out_ref = refs[-4] if final else None
    queries = query_ref.shape[1]
    span = GROUP_HEADS * HEAD_DIM
    first = groups[0]

    head_of_row = lax.broadcasted_iota(jnp.int32, (span, queries), 0) // HEAD_DIM
    ones = jnp.ones((HEAD_DIM, BLOCK), BF16)

    def query_of(group, head):
        query = query_ref[group * span : (group + 1) * span, :]
        return jnp.where(head_of_row == head, query, jnp.zeros_like(query))

    def score(slot, group, query, chunk, highest):
        rows = slice(chunk * BLOCK, (chunk + 1) * BLOCK)
        scores = nn_dot(keys_ref[rows, group * span : (group + 1) * span], query)
        score_ref[slot, rows, :] = scores
        top = jnp.max(scores.reshape(BLOCK // 8, 8, queries), axis=0)
        return top if highest is None else jnp.maximum(highest, top)

    highest = None
    query = query_of(first, 0)
    for chunk in range(BLOCKS):
        highest = score(0, first, query, chunk, highest)

    def head_step(head, highest):
        for index, group in enumerate(groups):
            top = jnp.max(highest, axis=0, keepdims=True)
            last = index + 1 == len(groups)
            later = groups[0] if last else groups[index + 1]
            query = query_of(later, jnp.minimum(head + 1, GROUP_HEADS - 1) if last else head)
            rows = pl.ds(pl.multiple_of(group * span + head * HEAD_DIM, HEAD_DIM), HEAD_DIM)
            total, highest = None, None
            for chunk in range(BLOCKS):
                keys = slice(chunk * BLOCK, (chunk + 1) * BLOCK)
                highest = score((index + 1) % 2, later, query, chunk, highest)
                weights = jnp.exp2(score_ref[index % 2, keys, :] - top).astype(BF16)
                values = jnp.concatenate([values_ref[rows, keys], ones], axis=0)
                term = nn_dot(values, weights)
                total = term if total is None else total + term
            held = pl.ds(pl.multiple_of((group - first) * span + head * HEAD_DIM, HEAD_DIM), HEAD_DIM)
            mixed_ref[held, :] = (total[:HEAD_DIM] / total[HEAD_DIM : HEAD_DIM + 1]).astype(BF16)
        return highest

    lax.fori_loop(0, GROUP_HEADS, head_step, highest)
    if not final:
        return
    own_ref, weight_refs = refs[0], refs[1:10]
    proj_ref = refs[-3]
    near_ref = weight_refs[0]
    proj_ref[0] = near_ref[3 * span :, :]

    def fill(evens, odds):
        for group in range(1, 4):
            proj_ref[group] = odds[group - 1][span : 2 * span, :]

    by_core(fill, weight_refs)
    mixed = None
    for group in range(4):
        if group < first:
            held = refs[10][group * span : (group + 1) * span, :]
        else:
            held = mixed_ref[(group - first) * span : (group - first + 1) * span, :]
        term = tn_dot(held, proj_ref[group]).astype(BF16).astype(F32)
        mixed = term if mixed is None else mixed + term
    out_ref[...] = (own_ref[...].astype(F32) + mixed).astype(BF16)


def attend(groups, projected, early, prior, after):
    own, keys, values, query = projected
    queries, width = own.shape
    span = GROUP_HEADS * HEAD_DIM
    height = len(groups) * span
    final = groups[-1] == 3
    operands = [keys, values, query]
    if final:
        operands += [own, *early, *prior]
    scratch = [pltpu.VMEM((2, PATCH, queries), F32)]
    if final:
        scratch = [
            pltpu.VMEM((4, span, width), BF16),
            pltpu.VMEM((height, queries), BF16),
        ] + scratch
    return pl.pallas_call(
        functools.partial(attend_kernel, groups, final),
        out_shape=jax.ShapeDtypeStruct((queries, width) if final else (height, queries), BF16),
        in_specs=[VMEM] * len(operands) + [ANY] * len(after),
        out_specs=VMEM,
        scratch_shapes=scratch,
        cost_estimate=pl.CostEstimate(
            flops=8 * 10**9 * len(groups),
            bytes_accessed=5 << 20,
            transcendentals=(2 << 20) * len(groups),
        ),
        compiler_params=pltpu.CompilerParams(vmem_limit_bytes=16 << 20),
    )(*operands, *after)


def mlp_kernel(groups, hidden_ref, gain_ref, up_ref, down_ref, *refs):
    weight_refs, refs = refs[:9], refs[9:]
    refs, ups_ref, downs_ref = refs[:-2], refs[-2], refs[-1]
    depth = hidden_ref.shape[1]
    split = weight_refs[2].shape[0]
    lead = weight_refs[1].shape[0] - depth
    ahead, far_a, far_b, behind, ahead_o, far_a_o, far_b_o, behind_o = weight_refs[1:]
    mine, other = (ahead, far_a, far_b, behind), (ahead_o, far_a_o, far_b_o, behind_o)

    def fill(out_ref, sources):
        out_ref[0] = sources[0][lead:, :]
        out_ref[1, : split - lead, :] = sources[1][lead:, :]
        out_ref[1, split - lead :, :] = sources[2][...]
        out_ref[2] = sources[3][lead:, :]

    odd = lax.rem(lax.axis_index("brick"), 2) == 1

    @pl.when(jnp.logical_not(odd))
    def _():
        fill(ups_ref, mine)
        fill(downs_ref, other)

    @pl.when(odd)
    def _():
        fill(ups_ref, other)
        fill(downs_ref, mine)

    up_refs = (up_ref,) + tuple(ups_ref.at[group] for group in range(3))
    down_refs = (down_ref,) + tuple(downs_ref.at[group] for group in range(3))
    wide_ref, before_ref, result_ref = refs[-3:]
    outs = refs[-3 - groups : -3]
    queries, width = hidden_ref.shape
    normed = layer_norm(hidden_ref[...], gain_ref[1:2, :])
    pieces = [(group, chunk) for group in range(groups) for chunk in range(queries // BLOCK)]

    def widen(index):
        group, chunk = pieces[index]
        before_ref[index % 2] = nn_dot(normed[chunk * BLOCK : (chunk + 1) * BLOCK], up_refs[group][...])

    widen(0)
    for index, (group, chunk) in enumerate(pieces):
        if index + 1 < len(pieces):
            widen(index + 1)
        wide = before_ref[index % 2]
        wide_ref[group, chunk * BLOCK : (chunk + 1) * BLOCK, :] = (
            wide * (0.5 + 0.5 * lax.erf(wide * 0.5**0.5))
        ).astype(BF16)
    total = None
    for group in range(groups):
        term = nn_dot(wide_ref[group], down_refs[group][...]).astype(BF16).astype(F32)
        total = term if total is None else total + term
    result_ref[...] = (hidden_ref[...].astype(F32) + total).astype(BF16)
    cut = width // groups
    rank = lax.axis_index("mp")
    for step in range(groups):
        column = pl.multiple_of(lax.rem(rank + step, groups) * cut, cut)
        outs[step][...] = result_ref[:, pl.ds(column, cut)]


def mlp(hidden, gains, up, down, weights):
    groups = 4
    rows, width = hidden.shape
    middle = up.shape[1]
    return pl.pallas_call(
        functools.partial(mlp_kernel, groups),
        out_shape=(jax.ShapeDtypeStruct((rows, width // groups), BF16),) * groups,
        in_specs=[VMEM] * 13,
        out_specs=(VMEM,) * groups,
        scratch_shapes=[
            pltpu.VMEM((groups, rows, middle), BF16),
            pltpu.VMEM((2, BLOCK, middle), F32),
            pltpu.VMEM((rows, width), BF16),
            pltpu.VMEM((groups - 1, width, middle), BF16),
            pltpu.VMEM((groups - 1, middle, width), BF16),
        ],
        cost_estimate=pl.CostEstimate(
            flops=4 * rows * width * middle * groups, bytes_accessed=5 << 20, transcendentals=0
        ),
        compiler_params=pltpu.CompilerParams(vmem_limit_bytes=18 << 20),
        name="mlp",
    )(hidden, gains, up, down, *weights)


def collect_kernel(*refs):
    sources, out_ref = refs[:4], refs[4]
    collect(sources, out_ref, 0)


def collect(sources, out_ref, base):
    queries = sources[0].shape[0]
    rank = lax.axis_index("mp")
    for index, source in enumerate(sources):
        sender = lax.rem(rank - index + 4, 4)
        at = pl.multiple_of(base + sender * queries, queries)
        out_ref[pl.ds(at, queries), :] = source[...]


def collect_rows(sources):
    return pl.pallas_call(
        collect_kernel,
        out_shape=jax.ShapeDtypeStruct((PATCH, sources[0].shape[1]), BF16),
        in_specs=[VMEM] * 4,
        out_specs=VMEM,
        compiler_params=pltpu.CompilerParams(vmem_limit_bytes=4 << 20),
        name="collect_rows",
    )(*sources)


def pack_kernel(shift_ref, table_ref, spots_ref, *rest):
    tail_ref, last_ref, sources, rest = rest[0], rest[1], rest[2:6], rest[6:]
    outs, lanes_ref, rows_ref = rest[:LANES], rest[LANES], rest[LANES + 1]
    lanes_ref[...] = jnp.zeros_like(lanes_ref)
    rows_ref[:PATCH, :] = tail_ref[...]
    rows_ref[2 * PATCH :, :] = last_ref[...]
    collect(sources, rows_ref, PATCH)
    begin = lax.div(PATCH - shift_ref[0], BLOCK)
    for step in range(2 * BLOCKS + 1):
        place = jnp.minimum(begin + step, 3 * BLOCKS - 1)
        fresh = begin + step < 3 * BLOCKS
        spots = jnp.where(fresh, spots_ref[pl.ds(place, 1), :], -1)
        rows = rows_ref[pl.ds(pl.multiple_of(place * BLOCK, BLOCK), BLOCK), :]
        sent = nn_dot(hot_rows(spots), rows).astype(BF16)
        for lane in range(LANES):
            window = pl.ds(aligned(table_ref[place, lane]), WINDOW)
            lanes_ref[lane, window, :] = (
                lanes_ref[lane, window, :] + sent[lane * WINDOW : (lane + 1) * WINDOW]
            )
    for lane in range(LANES):
        outs[lane][...] = lanes_ref[lane]


def pack_lanes(shift, table, spots, sources):
    width = sources[0].shape[1]
    return pl.pallas_call(
        pack_kernel,
        out_shape=(jax.ShapeDtypeStruct((PIECE, width), BF16),) * LANES,
        in_specs=[SMEM, SMEM] + [VMEM] * (1 + len(sources)),
        out_specs=(VMEM,) * LANES,
        scratch_shapes=[
            pltpu.VMEM((LANES, PIECE, width), BF16),
            pltpu.VMEM((3 * PATCH, width), BF16),
        ],
        compiler_params=pltpu.CompilerParams(vmem_limit_bytes=12 << 20),
        name="pack_lanes",
    )(shift, table, spots, *sources)


def place_kernel(counts_ref, *refs):
    pieces, out_ref = refs[:LANES], refs[LANES]
    capacity = out_ref.shape[0]
    out_ref[...] = jnp.zeros_like(out_ref)
    row = lax.broadcasted_iota(jnp.int32, (PIECE, out_ref.shape[1]), 0)
    for lane in range(LANES):
        start = window_start(counts_ref[0, lane], capacity)
        slots = row + start
        mine = (slots >= counts_ref[0, lane]) & (slots < counts_ref[1, lane])
        window = pl.ds(start, PIECE)
        out_ref[window, :] = jnp.where(mine, pieces[lane][...], out_ref[window, :])


def place_rows(counts, pieces, capacity):
    width = pieces[0].shape[1]
    return pl.pallas_call(
        place_kernel,
        out_shape=jax.ShapeDtypeStruct((capacity, width), BF16),
        in_specs=[SMEM] + [VMEM] * LANES,
        out_specs=VMEM,
        compiler_params=pltpu.CompilerParams(vmem_limit_bytes=12 << 20),
        name="place_rows",
    )(counts, *pieces)


def body(
    voxel_feats,
    slot_rank,
    curve_order,
    patch_shift,
    qkv_weight,
    proj_weight,
    up_weight,
    down_weight,
    norm_gains,
):
    bricks = lax.axis_size("brick")
    parts = lax.axis_size("mp")
    capacity, _ = voxel_feats.shape
    shard = curve_order.shape[0]
    queries = PATCH // parts

    piece0, own, piece2, piece3, counts = cut_windows(
        bricks, shard, slot_rank.reshape(capacity // 128, 128), voxel_feats
    )
    lane3 = shifted(piece3, "brick", -2)
    lane2 = shifted(piece2, "brick", -1)
    lane0 = shifted(piece0, "brick", 1)
    lanes = (lane0, own, lane2, lane3)
    near, half = sort_weights(qkv_weight, proj_weight, up_weight, down_weight, own)
    middle = half.shape[0] // 2

    def swapped(value):
        return lax.ppermute(value, "brick", [(brick, brick ^ 1) for brick in range(bricks)])

    ahead = shifted(half, "mp", 1)
    behind = shifted(half, "mp", -1)
    far_a = shifted(ahead[:middle], "mp", 1)
    far_b = shifted(behind[middle:], "mp", -1)
    ahead_other, behind_other = swapped(ahead), swapped(behind)
    far_a_other = swapped(far_a)
    far_b_other = swapped(far_b)
    weights = (near, ahead, far_a, far_b, behind, ahead_other, far_a_other, far_b_other, behind_other)

    spots, table = index_tables(
        bricks, capacity, patch_shift, curve_order.reshape(shard // BLOCK, BLOCK), near
    )
    head = head_rows(table, spots, lanes, (far_a, far_b))
    head_next = shifted(head, "brick", -1)
    common = (table, spots, lanes, norm_gains, weights)
    patch0 = project(0, *common, (head,), queries)
    mixed = attend((0, 1), patch0, weights, (), ())
    patch1 = project(1, *common, (head_next, mixed), queries)

    blocks = mlp(attend((0, 1, 2, 3), patch1, weights, (), ()), norm_gains, up_weight, down_weight, weights)

    last = [blocks[0]]
    for step in range(1, parts):
        last.append(shifted(blocks[step], "mp", step))
    hidden = attend((2, 3), patch0, weights, (mixed,), (blocks[0],))
    last = collect_rows(last)
    tail = shifted(last, "brick", 1)
    blocks = mlp(hidden, norm_gains, up_weight, down_weight, weights)
    first = [blocks[0]] + [shifted(blocks[step], "mp", step) for step in range(1, parts)]
    back0, back1, back2, back3 = pack_lanes(patch_shift, table, spots, (tail, last, *first))
    back3 = shifted(back3, "brick", 2)
    back2 = shifted(back2, "brick", 1)
    back0 = shifted(back0, "brick", -1)
    return place_rows(counts, (back0, back1, back2, back3), capacity)


def solution(mesh):
    return jax.shard_map(
        body,
        mesh=mesh,
        in_specs=(
            P("brick", None),
            P("brick"),
            P("brick"),
            P(),
            P(None, "mp"),
            P("mp", None),
            P(None, "mp"),
            P("mp", None),
            P(),
        ),
        out_specs=P("brick", "mp"),
        check_vma=False,
    )
```

```python
import functools

import jax
import jax.numpy as jnp
from jax import lax
from jax.experimental import pallas as pl
from jax.experimental.pallas import tpu as pltpu
from jax.sharding import PartitionSpec as P

PATCH = 1024
HEAD_DIM = 16
GROUP_HEADS = 8
EPSILON = 1e-05
LOG2E = 1.4426950408889634

TILE = 16
BLOCK = 128
WINDOW = 160
MOST_RUN = 768
PIECE = MOST_RUN + TILE
LANES = 4
BLOCKS = PATCH // BLOCK


F32 = jnp.float32
BF16 = jnp.bfloat16

ANY = pl.BlockSpec(memory_space=pl.ANY)
VMEM = pl.BlockSpec(memory_space=pltpu.VMEM)
SMEM = pl.BlockSpec(memory_space=pltpu.SMEM)
HBM = pl.BlockSpec(memory_space=pltpu.HBM)


def nt_dot(left, right):
    return lax.dot_general(left, right, (((1,), (1,)), ((), ())), preferred_element_type=F32)


def nn_dot(left, right):
    return jnp.dot(left, right, preferred_element_type=F32)


def tn_dot(left, right):
    return lax.dot_general(left, right, (((0,), (0,)), ((), ())), preferred_element_type=F32)


def aligned(value):
    return pl.multiple_of(value, TILE)


def shifted(value, axis, steps):
    count = lax.axis_size(axis)
    pairs = [(source, (source + steps) % count) for source in range(count)]
    return lax.ppermute(value, axis, pairs)


def layer_norm(values, gain):
    values = values.astype(F32)
    centred = values - jnp.mean(values, axis=-1, keepdims=True)
    spread = jnp.mean(centred * centred, axis=-1, keepdims=True)
    return (centred * lax.rsqrt(spread + EPSILON) * gain).astype(BF16)


def window_start(first, capacity):
    return aligned(jnp.minimum(lax.div(first, TILE) * TILE, capacity - PIECE))


def cut_kernel(bricks, shard, ranks_ref, feats_ref, *rest):
    outs, counts_ref, sems = rest[:3], rest[3], rest[4]
    capacity = feats_ref.shape[0]
    me = lax.axis_index("brick")
    ranks = ranks_ref[...]
    loads = []
    for index, lane in enumerate((3, 2, 0)):
        target = lax.rem(me - lane + 1 + bricks, bricks)
        first = jnp.sum((ranks < target * shard).astype(jnp.int32))
        counts_ref[0, lane] = first
        rows = pl.ds(window_start(first, capacity), PIECE)
        loads.append(pltpu.make_async_copy(feats_ref.at[rows], outs[index], sems.at[index]))
        loads[-1].start()
    counts_ref[0, 1] = jnp.sum((ranks < me * shard).astype(jnp.int32))
    for lane in range(LANES):
        target = lax.rem(me - lane + 1 + bricks, bricks)
        counts_ref[1, lane] = jnp.sum((ranks < (target + 1) * shard).astype(jnp.int32))
    for load in loads:
        load.wait()


def cut_windows(bricks, shard, ranks, feats):
    piece = jax.ShapeDtypeStruct((PIECE, feats.shape[1]), feats.dtype)
    return pl.pallas_call(
        functools.partial(cut_kernel, bricks, shard),
        out_shape=(piece,) * 3 + (jax.ShapeDtypeStruct((2, LANES), jnp.int32),),
        in_specs=[VMEM, HBM],
        out_specs=(VMEM,) * 3 + (SMEM,),
        scratch_shapes=[pltpu.SemaphoreType.DMA((3,))],
        compiler_params=pltpu.CompilerParams(vmem_limit_bytes=8 << 20),
        name="cut_windows",
    )(ranks, pltpu.with_memory_space_constraint(feats, pltpu.HBM))


def weights_kernel(qkv_ref, proj_ref, up_ref, down_ref, after_ref, near_ref, half_ref):
    span = GROUP_HEADS * HEAD_DIM
    shape = (3 * span, 3 * span)
    row = lax.broadcasted_iota(jnp.int32, shape, 0)
    column = lax.broadcasted_iota(jnp.int32, shape, 1)
    kind, rest = row // span, row % span
    source = rest // HEAD_DIM * (3 * HEAD_DIM) + kind * HEAD_DIM + rest % HEAD_DIM
    order = jnp.where(column == source, 1.0, 0.0).astype(BF16)
    near_ref[: 3 * span, :] = nt_dot(order, qkv_ref[...]).astype(BF16)
    near_ref[3 * span :, :] = proj_ref[...]
    odd = lax.rem(lax.axis_index("brick"), 2) == 1

    @pl.when(jnp.logical_not(odd))
    def _():
        half_ref[: 2 * span, :] = near_ref[: 2 * span, :]
        half_ref[2 * span :, :] = up_ref[...]

    @pl.when(odd)
    def _():
        half_ref[: 2 * span, :] = near_ref[2 * span :, :]
        half_ref[2 * span :, :] = down_ref[...]


def sort_weights(qkv, proj, up, down, after):
    width = proj.shape[1]
    span = GROUP_HEADS * HEAD_DIM
    return pl.pallas_call(
        weights_kernel,
        out_shape=(
            jax.ShapeDtypeStruct((4 * span, width), BF16),
            jax.ShapeDtypeStruct((2 * span + up.shape[0], width), BF16),
        ),
        in_specs=[VMEM] * 4 + [ANY],
        out_specs=(VMEM, VMEM),
        compiler_params=pltpu.CompilerParams(vmem_limit_bytes=8 << 20),
        name="sort_weights",
    )(qkv, proj, up, down, after)


def index_kernel(
    bricks, shift_ref, counts_ref, order_ref, feats_ref, after_ref, spots_ref, table_ref, own_ref, wide_ref, sem
):
    capacity = feats_ref.shape[0]
    rows = pl.ds(window_start(counts_ref[0, 1], capacity), PIECE)
    load = pltpu.make_async_copy(feats_ref.at[rows], own_ref, sem)
    load.start()
    me = lax.axis_index("brick")
    order = order_ref[...]
    rows = order.shape[0]
    lane_of = jnp.zeros_like(order)
    spot_of = jnp.zeros_like(order)
    column = lax.broadcasted_iota(jnp.int32, (1, BLOCK), 1)
    leads = jnp.zeros((1, BLOCK), F32)
    for lane in range(LANES):
        source = lax.rem(me + lane - 1 + bricks, bricks)
        slot = order - source * capacity
        mine = (slot >= 0) & (slot < capacity)
        first = jnp.min(jnp.where(mine, slot, capacity), keepdims=True)
        start = jnp.minimum(first & -TILE, capacity - PIECE)
        lane_of = jnp.where(mine, lane, lane_of)
        spot_of = jnp.where(mine, slot - start + lane * WINDOW, spot_of)
        leads = jnp.where(column == lane, (first - start).astype(F32), leads)
    ahead = PATCH - shift_ref[0]
    down, across = lax.div(ahead, BLOCK), lax.rem(ahead, BLOCK)
    wide_ref[...] = jnp.full_like(wide_ref, -1)
    for index, value in enumerate((lane_of, spot_of)):
        turned = pltpu.roll(value, across, 1)
        wide_ref[index, 0, pl.ds(down, rows), :] = turned
        wide_ref[index, 1, pl.ds(down + 1, rows), :] = turned
    height = spots_ref.shape[0]
    near = lax.broadcasted_iota(jnp.int32, (height, BLOCK), 1) >= across
    lane_wide = jnp.where(near, wide_ref[0, 0, :height, :], wide_ref[0, 1, :height, :])
    spot_wide = jnp.where(near, wide_ref[1, 0, :height, :], wide_ref[1, 1, :height, :])
    held = jnp.zeros((height, BLOCK), F32)
    wide_column = lax.broadcasted_iota(jnp.int32, (height, BLOCK), 1)
    for lane in range(LANES):
        found = jnp.sum((lane_wide == lane).astype(F32), axis=1, keepdims=True)
        held = jnp.where(wide_column == lane, found, held)
    below = lax.broadcasted_iota(jnp.int32, (height, height), 1) < lax.broadcasted_iota(
        jnp.int32, (height, height), 0
    )
    before = nn_dot(below.astype(F32).astype(BF16), held.astype(BF16))
    table = jnp.minimum((leads + before).astype(jnp.int32) & -TILE, PIECE - WINDOW)
    table_ref[...] = table
    spots = spot_wide
    for lane in range(LANES):
        spots = jnp.where(lane_wide == lane, spot_wide - table[:, lane : lane + 1], spots)
    spots_ref[...] = jnp.where(lane_wide < 0, -1, spots)
    load.wait()


def index_tables(bricks, shift, counts, order, feats, after):
    height = 3 * BLOCKS
    table = jax.ShapeDtypeStruct((height, BLOCK), jnp.int32)
    return pl.pallas_call(
        functools.partial(index_kernel, bricks),
        out_shape=(table, table, jax.ShapeDtypeStruct((PIECE, feats.shape[1]), feats.dtype)),
        in_specs=[SMEM, SMEM, VMEM, HBM, ANY],
        out_specs=(VMEM,) * 3,
        scratch_shapes=[
            pltpu.VMEM((2, 2, height + 2 * BLOCKS, BLOCK), jnp.int32),
            pltpu.SemaphoreType.DMA,
        ],
        compiler_params=pltpu.CompilerParams(vmem_limit_bytes=4 << 20),
        name="index_tables",
    )(shift, counts, order, pltpu.with_memory_space_constraint(feats, pltpu.HBM), after)


def hot_rows(spots):
    tall = lax.broadcasted_iota(jnp.int32, (LANES * WINDOW, BLOCK), 0)
    return jnp.where(tall == spots, 1.0, 0.0).astype(BF16)


def gather_block(table_ref, spots_ref, place, lane_refs):
    windows = [
        lane_refs[lane][pl.ds(aligned(table_ref[place, lane]), WINDOW), :]
        for lane in range(LANES)
    ]
    stacked = jnp.concatenate(windows, axis=0)
    return tn_dot(hot_rows(spots_ref[place : place + 1, :]), stacked).astype(BF16)


def head_kernel(table_ref, spots_ref, *refs):
    out_ref = refs[-1]
    for block in range(BLOCKS):
        rows = slice(block * BLOCK, (block + 1) * BLOCK)
        out_ref[rows, :] = gather_block(table_ref, spots_ref, block, refs[:LANES])


def head_rows(table, spots, lanes, after):
    width = lanes[0].shape[1]
    return pl.pallas_call(
        head_kernel,
        out_shape=jax.ShapeDtypeStruct((PATCH, width), BF16),
        in_specs=[SMEM] + [VMEM] * (1 + LANES) + [ANY] * len(after),
        out_specs=VMEM,
        cost_estimate=pl.CostEstimate(
            flops=2 * PATCH * 768 * width, bytes_accessed=5 << 20, transcendentals=0
        ),
        compiler_params=pltpu.CompilerParams(vmem_limit_bytes=12 << 20),
        name="head_rows",
    )(table, spots, *lanes, *after)


def by_core(fill, weight_refs):
    odd = lax.rem(lax.axis_index("brick"), 2) == 1
    ahead, far, _, behind, ahead_other, far_other, _, behind_other = weight_refs[1:]
    mine, other = (ahead, far, behind), (ahead_other, far_other, behind_other)

    @pl.when(jnp.logical_not(odd))
    def _():
        fill(mine, other)

    @pl.when(odd)
    def _():
        fill(other, mine)


def project_kernel(part, table_ref, spots_ref, *refs):
    lane_refs, gain_ref = refs[:LANES], refs[LANES]
    weight_refs = refs[LANES + 1 : LANES + 10]
    extra_ref = refs[LANES + 10]
    own_ref, keys_ref, values_ref, query_ref, rows_ref, normed_ref, stack_ref = refs[-7:]
    queries = own_ref.shape[0]
    span = GROUP_HEADS * HEAD_DIM
    near_ref = weight_refs[0]
    for kind in range(3):
        stack_ref[kind, :span, :] = near_ref[kind * span : (kind + 1) * span, :]

    def fill(evens, odds):
        for group in range(1, 4):
            rows = slice(group * span, (group + 1) * span)
            stack_ref[0, rows, :] = evens[group - 1][:span, :]
            stack_ref[1, rows, :] = evens[group - 1][span : 2 * span, :]
            stack_ref[2, rows, :] = odds[group - 1][:span, :]

    by_core(fill, weight_refs)
    gain = gain_ref[0:1, :]
    for quarter in range(4):
        for block in range(quarter * 2, quarter * 2 + 2):
            rows = slice(block * BLOCK, (block + 1) * BLOCK)
            found = gather_block(table_ref, spots_ref, part * BLOCKS + BLOCKS + block, lane_refs)
            if part == 1:
                found = found + extra_ref[rows, :]
            rows_ref[rows, :] = found
            normed_ref[rows, :] = layer_norm(found, gain)
        rows = slice(quarter * 256, (quarter + 1) * 256)
        normed = normed_ref[rows, :]
        keys_ref[rows, :] = nt_dot(normed, stack_ref[1]).astype(BF16)
        values_ref[:, rows] = nt_dot(stack_ref[2], normed).astype(BF16)
    own_rows = pl.ds(pl.multiple_of(lax.axis_index("mp") * queries, queries), queries)
    own_ref[...] = rows_ref[own_rows, :]
    query = nt_dot(stack_ref[0], normed_ref[own_rows, :])
    query_ref[...] = (query * (HEAD_DIM ** (-0.5) * LOG2E)).astype(BF16)


def project(part, table, spots, lanes, gains, early, extra, queries):
    width = lanes[0].shape[1]
    shape = lambda *dims: jax.ShapeDtypeStruct(dims, BF16)
    return pl.pallas_call(
        functools.partial(project_kernel, part),
        out_shape=(shape(queries, width), shape(PATCH, width), shape(width, PATCH), shape(width, queries)),
        in_specs=[SMEM] + [VMEM] * (LANES + 11) + ([VMEM] + [ANY] * (len(extra) - 1) if part else [ANY] * len(extra)),
        out_specs=(VMEM,) * 4,
        scratch_shapes=[
            pltpu.VMEM((PATCH, width), BF16),
            pltpu.VMEM((PATCH, width), BF16),
            pltpu.VMEM((3, width, width), BF16),
        ],
        cost_estimate=pl.CostEstimate(flops=10 * 10**9, bytes_accessed=10 << 20, transcendentals=0),
        compiler_params=pltpu.CompilerParams(vmem_limit_bytes=20 << 20),
        name="project_last" if part else "project_first",
    )(table, spots, *lanes, gains, *early, *extra)


def attend_kernel(groups, final, keys_ref, values_ref, query_ref, *refs):
    mixed_ref, score_ref = refs[-2:]
    out_ref = refs[-4] if final else None
    queries = query_ref.shape[1]
    span = GROUP_HEADS * HEAD_DIM
    first = groups[0]

    head_of_row = lax.broadcasted_iota(jnp.int32, (span, queries), 0) // HEAD_DIM
    ones = jnp.ones((HEAD_DIM, BLOCK), BF16)

    def query_of(group, head):
        query = query_ref[group * span : (group + 1) * span, :]
        return jnp.where(head_of_row == head, query, jnp.zeros_like(query))

    def score(slot, group, query, chunk, highest):
        rows = slice(chunk * BLOCK, (chunk + 1) * BLOCK)
        scores = nn_dot(keys_ref[rows, group * span : (group + 1) * span], query)
        score_ref[slot, rows, :] = scores
        top = jnp.max(scores.reshape(BLOCK // 8, 8, queries), axis=0)
        return top if highest is None else jnp.maximum(highest, top)

    highest = None
    query = query_of(first, 0)
    for chunk in range(BLOCKS):
        highest = score(0, first, query, chunk, highest)

    def head_step(head, highest):
        for index, group in enumerate(groups):
            top = jnp.max(highest, axis=0, keepdims=True)
            last = index + 1 == len(groups)
            later = groups[0] if last else groups[index + 1]
            query = query_of(later, jnp.minimum(head + 1, GROUP_HEADS - 1) if last else head)
            rows = pl.ds(pl.multiple_of(group * span + head * HEAD_DIM, HEAD_DIM), HEAD_DIM)
            total, highest = None, None
            for chunk in range(BLOCKS):
                keys = slice(chunk * BLOCK, (chunk + 1) * BLOCK)
                highest = score((index + 1) % 2, later, query, chunk, highest)
                weights = jnp.exp2(score_ref[index % 2, keys, :] - top).astype(BF16)
                values = jnp.concatenate([values_ref[rows, keys], ones], axis=0)
                term = nn_dot(values, weights)
                total = term if total is None else total + term
            held = pl.ds(pl.multiple_of((group - first) * span + head * HEAD_DIM, HEAD_DIM), HEAD_DIM)
            mixed_ref[held, :] = (total[:HEAD_DIM] / total[HEAD_DIM : HEAD_DIM + 1]).astype(BF16)
        return highest

    lax.fori_loop(0, GROUP_HEADS, head_step, highest)
    if not final:
        return
    own_ref, weight_refs = refs[0], refs[1:10]
    proj_ref = refs[-3]
    near_ref = weight_refs[0]
    proj_ref[0] = near_ref[3 * span :, :]

    def fill(evens, odds):
        for group in range(1, 4):
            proj_ref[group] = odds[group - 1][span : 2 * span, :]

    by_core(fill, weight_refs)
    mixed = None
    for group in range(4):
        if group < first:
            held = refs[10][group * span : (group + 1) * span, :]
        else:
            held = mixed_ref[(group - first) * span : (group - first + 1) * span, :]
        term = tn_dot(held, proj_ref[group]).astype(BF16).astype(F32)
        mixed = term if mixed is None else mixed + term
    out_ref[...] = (own_ref[...].astype(F32) + mixed).astype(BF16)


def attend(groups, projected, early, prior, after):
    own, keys, values, query = projected
    queries, width = own.shape
    span = GROUP_HEADS * HEAD_DIM
    height = len(groups) * span
    final = groups[-1] == 3
    operands = [keys, values, query]
    if final:
        operands += [own, *early, *prior]
    scratch = [pltpu.VMEM((2, PATCH, queries), F32)]
    if final:
        scratch = [
            pltpu.VMEM((4, span, width), BF16),
            pltpu.VMEM((height, queries), BF16),
        ] + scratch
    return pl.pallas_call(
        functools.partial(attend_kernel, groups, final),
        out_shape=jax.ShapeDtypeStruct((queries, width) if final else (height, queries), BF16),
        in_specs=[VMEM] * len(operands) + [ANY] * len(after),
        out_specs=VMEM,
        scratch_shapes=scratch,
        cost_estimate=pl.CostEstimate(
            flops=8 * 10**9 * len(groups),
            bytes_accessed=5 << 20,
            transcendentals=(2 << 20) * len(groups),
        ),
        compiler_params=pltpu.CompilerParams(vmem_limit_bytes=16 << 20),
    )(*operands, *after)


def mlp_kernel(groups, hidden_ref, gain_ref, up_ref, down_ref, *refs):
    weight_refs, refs = refs[:9], refs[9:]
    refs, ups_ref, downs_ref = refs[:-2], refs[-2], refs[-1]
    depth = hidden_ref.shape[1]
    split = weight_refs[2].shape[0]
    lead = weight_refs[1].shape[0] - depth
    ahead, far_a, far_b, behind, ahead_o, far_a_o, far_b_o, behind_o = weight_refs[1:]
    mine, other = (ahead, far_a, far_b, behind), (ahead_o, far_a_o, far_b_o, behind_o)

    def fill(out_ref, sources):
        out_ref[0] = sources[0][lead:, :]
        out_ref[1, : split - lead, :] = sources[1][lead:, :]
        out_ref[1, split - lead :, :] = sources[2][...]
        out_ref[2] = sources[3][lead:, :]

    odd = lax.rem(lax.axis_index("brick"), 2) == 1

    @pl.when(jnp.logical_not(odd))
    def _():
        fill(ups_ref, mine)
        fill(downs_ref, other)

    @pl.when(odd)
    def _():
        fill(ups_ref, other)
        fill(downs_ref, mine)

    up_refs = (up_ref,) + tuple(ups_ref.at[group] for group in range(3))
    down_refs = (down_ref,) + tuple(downs_ref.at[group] for group in range(3))
    wide_ref, before_ref, result_ref = refs[-3:]
    outs = refs[-3 - groups : -3]
    queries, width = hidden_ref.shape
    normed = layer_norm(hidden_ref[...], gain_ref[1:2, :])
    pieces = [(group, chunk) for group in range(groups) for chunk in range(queries // BLOCK)]

    def widen(index):
        group, chunk = pieces[index]
        before_ref[index % 2] = nn_dot(normed[chunk * BLOCK : (chunk + 1) * BLOCK], up_refs[group][...])

    widen(0)
    for index, (group, chunk) in enumerate(pieces):
        if index + 1 < len(pieces):
            widen(index + 1)
        wide = before_ref[index % 2]
        wide_ref[group, chunk * BLOCK : (chunk + 1) * BLOCK, :] = (
            wide * (0.5 + 0.5 * lax.erf(wide * 0.5**0.5))
        ).astype(BF16)
    total = None
    for group in range(groups):
        term = nn_dot(wide_ref[group], down_refs[group][...]).astype(BF16).astype(F32)
        total = term if total is None else total + term
    result_ref[...] = (hidden_ref[...].astype(F32) + total).astype(BF16)
    cut = width // groups
    rank = lax.axis_index("mp")
    for step in range(groups):
        column = pl.multiple_of(lax.rem(rank + step, groups) * cut, cut)
        outs[step][...] = result_ref[:, pl.ds(column, cut)]


def mlp(hidden, gains, up, down, weights):
    groups = 4
    rows, width = hidden.shape
    middle = up.shape[1]
    return pl.pallas_call(
        functools.partial(mlp_kernel, groups),
        out_shape=(jax.ShapeDtypeStruct((rows, width // groups), BF16),) * groups,
        in_specs=[VMEM] * 13,
        out_specs=(VMEM,) * groups,
        scratch_shapes=[
            pltpu.VMEM((groups, rows, middle), BF16),
            pltpu.VMEM((2, BLOCK, middle), F32),
            pltpu.VMEM((rows, width), BF16),
            pltpu.VMEM((groups - 1, width, middle), BF16),
            pltpu.VMEM((groups - 1, middle, width), BF16),
        ],
        cost_estimate=pl.CostEstimate(
            flops=4 * rows * width * middle * groups, bytes_accessed=5 << 20, transcendentals=0
        ),
        compiler_params=pltpu.CompilerParams(vmem_limit_bytes=18 << 20),
        name="mlp",
    )(hidden, gains, up, down, *weights)


def collect_kernel(*refs):
    sources, out_ref = refs[:4], refs[4]
    collect(sources, out_ref, 0)


def collect(sources, out_ref, base):
    queries = sources[0].shape[0]
    rank = lax.axis_index("mp")
    for index, source in enumerate(sources):
        sender = lax.rem(rank - index + 4, 4)
        at = pl.multiple_of(base + sender * queries, queries)
        out_ref[pl.ds(at, queries), :] = source[...]


def collect_rows(sources):
    return pl.pallas_call(
        collect_kernel,
        out_shape=jax.ShapeDtypeStruct((PATCH, sources[0].shape[1]), BF16),
        in_specs=[VMEM] * 4,
        out_specs=VMEM,
        compiler_params=pltpu.CompilerParams(vmem_limit_bytes=4 << 20),
        name="collect_rows",
    )(*sources)


def pack_kernel(shift_ref, table_ref, spots_ref, *rest):
    tail_ref, last_ref, sources, rest = rest[0], rest[1], rest[2:6], rest[6:]
    outs, lanes_ref, rows_ref = rest[:LANES], rest[LANES], rest[LANES + 1]
    lanes_ref[...] = jnp.zeros_like(lanes_ref)
    rows_ref[:PATCH, :] = tail_ref[...]
    rows_ref[2 * PATCH :, :] = last_ref[...]
    collect(sources, rows_ref, PATCH)
    begin = lax.div(PATCH - shift_ref[0], BLOCK)
    for step in range(2 * BLOCKS + 1):
        place = jnp.minimum(begin + step, 3 * BLOCKS - 1)
        fresh = begin + step < 3 * BLOCKS
        spots = jnp.where(fresh, spots_ref[pl.ds(place, 1), :], -1)
        rows = rows_ref[pl.ds(pl.multiple_of(place * BLOCK, BLOCK), BLOCK), :]
        sent = nn_dot(hot_rows(spots), rows).astype(BF16)
        for lane in range(LANES):
            window = pl.ds(aligned(table_ref[place, lane]), WINDOW)
            lanes_ref[lane, window, :] = (
                lanes_ref[lane, window, :] + sent[lane * WINDOW : (lane + 1) * WINDOW]
            )
    for lane in range(LANES):
        outs[lane][...] = lanes_ref[lane]


def pack_lanes(shift, table, spots, sources):
    width = sources[0].shape[1]
    return pl.pallas_call(
        pack_kernel,
        out_shape=(jax.ShapeDtypeStruct((PIECE, width), BF16),) * LANES,
        in_specs=[SMEM, SMEM] + [VMEM] * (1 + len(sources)),
        out_specs=(VMEM,) * LANES,
        scratch_shapes=[
            pltpu.VMEM((LANES, PIECE, width), BF16),
            pltpu.VMEM((3 * PATCH, width), BF16),
        ],
        compiler_params=pltpu.CompilerParams(vmem_limit_bytes=12 << 20),
        name="pack_lanes",
    )(shift, table, spots, *sources)


def place_kernel(counts_ref, *refs):
    pieces, out_ref = refs[:LANES], refs[LANES]
    capacity = out_ref.shape[0]
    out_ref[...] = jnp.zeros_like(out_ref)
    row = lax.broadcasted_iota(jnp.int32, (PIECE, out_ref.shape[1]), 0)
    for lane in range(LANES):
        start = window_start(counts_ref[0, lane], capacity)
        slots = row + start
        mine = (slots >= counts_ref[0, lane]) & (slots < counts_ref[1, lane])
        window = pl.ds(start, PIECE)
        out_ref[window, :] = jnp.where(mine, pieces[lane][...], out_ref[window, :])


def place_rows(counts, pieces, capacity):
    width = pieces[0].shape[1]
    return pl.pallas_call(
        place_kernel,
        out_shape=jax.ShapeDtypeStruct((capacity, width), BF16),
        in_specs=[SMEM] + [VMEM] * LANES,
        out_specs=VMEM,
        compiler_params=pltpu.CompilerParams(vmem_limit_bytes=12 << 20),
        name="place_rows",
    )(counts, *pieces)


def body(
    voxel_feats,
    slot_rank,
    curve_order,
    patch_shift,
    qkv_weight,
    proj_weight,
    up_weight,
    down_weight,
    norm_gains,
):
    bricks = lax.axis_size("brick")
    parts = lax.axis_size("mp")
    capacity, _ = voxel_feats.shape
    shard = curve_order.shape[0]
    queries = PATCH // parts

    piece3, piece2, piece0, counts = cut_windows(
        bricks, shard, slot_rank.reshape(capacity // 128, 128), voxel_feats
    )
    lane3 = shifted(piece3, "brick", -2)
    lane2 = shifted(piece2, "brick", -1)
    lane0 = shifted(piece0, "brick", 1)
    near, half = sort_weights(qkv_weight, proj_weight, up_weight, down_weight, piece0)
    middle = half.shape[0] // 2

    def swapped(value):
        return lax.ppermute(value, "brick", [(brick, brick ^ 1) for brick in range(bricks)])

    ahead = shifted(half, "mp", 1)
    behind = shifted(half, "mp", -1)
    far_a = shifted(ahead[:middle], "mp", 1)
    far_b = shifted(behind[middle:], "mp", -1)
    ahead_other = swapped(ahead)
    behind_other = swapped(behind)
    far_a_other = swapped(far_a)
    far_b_other = swapped(far_b)
    weights = (near, ahead, far_a, far_b, behind, ahead_other, far_a_other, far_b_other, behind_other)

    spots, table, own = index_tables(
        bricks, patch_shift, counts, curve_order.reshape(shard // BLOCK, BLOCK), voxel_feats, near
    )
    lanes = (lane0, own, lane2, lane3)
    head = head_rows(table, spots, lanes, ())
    head_next = shifted(head, "brick", -1)
    common = (table, spots, lanes, norm_gains, weights)
    patch0 = project(0, *common, (head,), queries)
    mixed = attend((0, 1), patch0, weights, (), ())
    patch1 = project(1, *common, (head_next, mixed), queries)

    blocks = mlp(attend((0, 1, 2, 3), patch1, weights, (), ()), norm_gains, up_weight, down_weight, weights)

    last = [blocks[0]]
    for step in range(1, parts):
        last.append(shifted(blocks[step], "mp", step))
    hidden = attend((2, 3), patch0, weights, (mixed,), (blocks[0],))
    last = collect_rows(last)
    tail = shifted(last, "brick", 1)
    blocks = mlp(hidden, norm_gains, up_weight, down_weight, weights)
    first = [blocks[0]] + [shifted(blocks[step], "mp", step) for step in range(1, parts)]
    back0, back1, back2, back3 = pack_lanes(patch_shift, table, spots, (tail, last, *first))
    back3 = shifted(back3, "brick", 2)
    back2 = shifted(back2, "brick", 1)
    back0 = shifted(back0, "brick", -1)
    return place_rows(counts, (back0, back1, back2, back3), capacity)


def solution(mesh):
    return jax.shard_map(
        body,
        mesh=mesh,
        in_specs=(
            P("brick", None),
            P("brick"),
            P("brick"),
            P(),
            P(None, "mp"),
            P("mp", None),
            P(None, "mp"),
            P("mp", None),
            P(),
        ),
        out_specs=P("brick", "mp"),
        check_vma=False,
    )
```

```python
import functools

import jax
import jax.numpy as jnp
from jax import lax
from jax.experimental import pallas as pl
from jax.experimental.pallas import tpu as pltpu
from jax.sharding import PartitionSpec as P

PATCH = 1024
HEAD_DIM = 16
GROUP_HEADS = 8
EPSILON = 1e-05
SCALE = HEAD_DIM ** (-0.5) * 1.4426950408889634
SAFE_SCORE = 100.0
SAFE_VALUE = 1e4

TILE = 16
BLOCK = 128
WINDOW = 160
MOST_RUN = 768
PIECE = MOST_RUN + TILE
LANES = 4
BLOCKS = PATCH // BLOCK


F32 = jnp.float32
BF16 = jnp.bfloat16

ANY = pl.BlockSpec(memory_space=pl.ANY)
VMEM = pl.BlockSpec(memory_space=pltpu.VMEM)
SMEM = pl.BlockSpec(memory_space=pltpu.SMEM)
HBM = pl.BlockSpec(memory_space=pltpu.HBM)


def nt_dot(left, right):
    return lax.dot_general(left, right, (((1,), (1,)), ((), ())), preferred_element_type=F32)


def nn_dot(left, right):
    return jnp.dot(left, right, preferred_element_type=F32)


def tn_dot(left, right):
    return lax.dot_general(left, right, (((0,), (0,)), ((), ())), preferred_element_type=F32)


def aligned(value):
    return pl.multiple_of(value, TILE)


def shifted(value, axis, steps):
    count = lax.axis_size(axis)
    pairs = [(source, (source + steps) % count) for source in range(count)]
    return lax.ppermute(value, axis, pairs)


def layer_norm(values, gain):
    values = values.astype(F32)
    centred = values - jnp.mean(values, axis=-1, keepdims=True)
    spread = jnp.mean(centred * centred, axis=-1, keepdims=True)
    return (centred * lax.rsqrt(spread + EPSILON) * gain).astype(BF16)


def window_start(first, capacity):
    return aligned(jnp.minimum(lax.div(first, TILE) * TILE, capacity - PIECE))


def cut_kernel(bricks, shard, ranks_ref, feats_ref, *rest):
    outs, counts_ref, sems = rest[:3], rest[3], rest[4]
    capacity = feats_ref.shape[0]
    me = lax.axis_index("brick")
    ranks = ranks_ref[...]
    loads = []
    for index, lane in enumerate((3, 2, 0)):
        target = lax.rem(me - lane + 1 + bricks, bricks)
        first = jnp.sum((ranks < target * shard).astype(jnp.int32))
        counts_ref[0, lane] = first
        rows = pl.ds(window_start(first, capacity), PIECE)
        loads.append(pltpu.make_async_copy(feats_ref.at[rows], outs[index], sems.at[index]))
        loads[-1].start()
    counts_ref[0, 1] = jnp.sum((ranks < me * shard).astype(jnp.int32))
    for lane in range(LANES):
        target = lax.rem(me - lane + 1 + bricks, bricks)
        counts_ref[1, lane] = jnp.sum((ranks < (target + 1) * shard).astype(jnp.int32))
    for load in loads:
        load.wait()


def cut_windows(bricks, shard, ranks, feats):
    piece = jax.ShapeDtypeStruct((PIECE, feats.shape[1]), feats.dtype)
    return pl.pallas_call(
        functools.partial(cut_kernel, bricks, shard),
        out_shape=(piece,) * 3 + (jax.ShapeDtypeStruct((2, LANES), jnp.int32),),
        in_specs=[VMEM, HBM],
        out_specs=(VMEM,) * 3 + (SMEM,),
        scratch_shapes=[pltpu.SemaphoreType.DMA((3,))],
        compiler_params=pltpu.CompilerParams(vmem_limit_bytes=8 << 20),
        name="cut_windows",
    )(ranks, pltpu.with_memory_space_constraint(feats, pltpu.HBM))


def weights_kernel(qkv_ref, proj_ref, up_ref, down_ref, after_ref, near_ref, half_ref):
    span = GROUP_HEADS * HEAD_DIM
    shape = (3 * span, 3 * span)
    row = lax.broadcasted_iota(jnp.int32, shape, 0)
    column = lax.broadcasted_iota(jnp.int32, shape, 1)
    kind, rest = row // span, row % span
    source = rest // HEAD_DIM * (3 * HEAD_DIM) + kind * HEAD_DIM + rest % HEAD_DIM
    order = jnp.where(column == source, 1.0, 0.0).astype(BF16)
    near_ref[: 3 * span, :] = nt_dot(order, qkv_ref[...]).astype(BF16)
    near_ref[3 * span :, :] = proj_ref[...]
    odd = lax.rem(lax.axis_index("brick"), 2) == 1

    @pl.when(jnp.logical_not(odd))
    def _():
        half_ref[: 2 * span, :] = near_ref[: 2 * span, :]
        half_ref[2 * span :, :] = up_ref[...]

    @pl.when(odd)
    def _():
        half_ref[: 2 * span, :] = near_ref[2 * span :, :]
        half_ref[2 * span :, :] = down_ref[...]


def sort_weights(qkv, proj, up, down, after):
    width = proj.shape[1]
    span = GROUP_HEADS * HEAD_DIM
    return pl.pallas_call(
        weights_kernel,
        out_shape=(
            jax.ShapeDtypeStruct((4 * span, width), BF16),
            jax.ShapeDtypeStruct((2 * span + up.shape[0], width), BF16),
        ),
        in_specs=[VMEM] * 4 + [ANY],
        out_specs=(VMEM, VMEM),
        compiler_params=pltpu.CompilerParams(vmem_limit_bytes=8 << 20),
        name="sort_weights",
    )(qkv, proj, up, down, after)


def index_kernel(
    bricks, shift_ref, counts_ref, order_ref, feats_ref, after_ref, spots_ref, table_ref, own_ref, wide_ref, sem
):
    capacity = feats_ref.shape[0]
    rows = pl.ds(window_start(counts_ref[0, 1], capacity), PIECE)
    load = pltpu.make_async_copy(feats_ref.at[rows], own_ref, sem)
    load.start()
    me = lax.axis_index("brick")
    order = order_ref[...]
    rows = order.shape[0]
    lane_of = jnp.zeros_like(order)
    spot_of = jnp.zeros_like(order)
    column = lax.broadcasted_iota(jnp.int32, (1, BLOCK), 1)
    leads = jnp.zeros((1, BLOCK), F32)
    for lane in range(LANES):
        source = lax.rem(me + lane - 1 + bricks, bricks)
        slot = order - source * capacity
        mine = (slot >= 0) & (slot < capacity)
        first = jnp.min(jnp.where(mine, slot, capacity), keepdims=True)
        start = jnp.minimum(first & -TILE, capacity - PIECE)
        lane_of = jnp.where(mine, lane, lane_of)
        spot_of = jnp.where(mine, slot - start + lane * WINDOW, spot_of)
        leads = jnp.where(column == lane, (first - start).astype(F32), leads)
    ahead = PATCH - shift_ref[0]
    down, across = lax.div(ahead, BLOCK), lax.rem(ahead, BLOCK)
    wide_ref[...] = jnp.full_like(wide_ref, -1)
    for index, value in enumerate((lane_of, spot_of)):
        turned = pltpu.roll(value, across, 1)
        wide_ref[index, 0, pl.ds(down, rows), :] = turned
        wide_ref[index, 1, pl.ds(down + 1, rows), :] = turned
    height = spots_ref.shape[0]
    near = lax.broadcasted_iota(jnp.int32, (height, BLOCK), 1) >= across
    lane_wide = jnp.where(near, wide_ref[0, 0, :height, :], wide_ref[0, 1, :height, :])
    spot_wide = jnp.where(near, wide_ref[1, 0, :height, :], wide_ref[1, 1, :height, :])
    held = jnp.zeros((height, BLOCK), F32)
    wide_column = lax.broadcasted_iota(jnp.int32, (height, BLOCK), 1)
    for lane in range(LANES):
        found = jnp.sum((lane_wide == lane).astype(F32), axis=1, keepdims=True)
        held = jnp.where(wide_column == lane, found, held)
    below = lax.broadcasted_iota(jnp.int32, (height, height), 1) < lax.broadcasted_iota(
        jnp.int32, (height, height), 0
    )
    before = nn_dot(below.astype(F32).astype(BF16), held.astype(BF16))
    table = jnp.minimum((leads + before).astype(jnp.int32) & -TILE, PIECE - WINDOW)
    table_ref[...] = table
    spots = spot_wide
    for lane in range(LANES):
        spots = jnp.where(lane_wide == lane, spot_wide - table[:, lane : lane + 1], spots)
    spots_ref[...] = jnp.where(lane_wide < 0, -1, spots)
    load.wait()


def index_tables(bricks, shift, counts, order, feats, after):
    height = 3 * BLOCKS
    table = jax.ShapeDtypeStruct((height, BLOCK), jnp.int32)
    return pl.pallas_call(
        functools.partial(index_kernel, bricks),
        out_shape=(table, table, jax.ShapeDtypeStruct((PIECE, feats.shape[1]), feats.dtype)),
        in_specs=[SMEM, SMEM, VMEM, HBM, ANY],
        out_specs=(VMEM,) * 3,
        scratch_shapes=[
            pltpu.VMEM((2, 2, height + 2 * BLOCKS, BLOCK), jnp.int32),
            pltpu.SemaphoreType.DMA,
        ],
        compiler_params=pltpu.CompilerParams(vmem_limit_bytes=4 << 20),
        name="index_tables",
    )(shift, counts, order, pltpu.with_memory_space_constraint(feats, pltpu.HBM), after)


def hot_rows(spots):
    tall = lax.broadcasted_iota(jnp.int32, (LANES * WINDOW, BLOCK), 0)
    return jnp.where(tall == spots, 1.0, 0.0).astype(BF16)


def gather_block(table_ref, spots_ref, place, lane_refs):
    windows = [
        lane_refs[lane][pl.ds(aligned(table_ref[place, lane]), WINDOW), :]
        for lane in range(LANES)
    ]
    stacked = jnp.concatenate(windows, axis=0)
    return tn_dot(hot_rows(spots_ref[place : place + 1, :]), stacked).astype(BF16)


def head_kernel(table_ref, spots_ref, *refs):
    out_ref = refs[-1]
    for block in range(BLOCKS):
        rows = slice(block * BLOCK, (block + 1) * BLOCK)
        out_ref[rows, :] = gather_block(table_ref, spots_ref, block, refs[:LANES])


def head_rows(table, spots, lanes, after):
    width = lanes[0].shape[1]
    return pl.pallas_call(
        head_kernel,
        out_shape=jax.ShapeDtypeStruct((PATCH, width), BF16),
        in_specs=[SMEM] + [VMEM] * (1 + LANES) + [ANY] * len(after),
        out_specs=VMEM,
        cost_estimate=pl.CostEstimate(
            flops=2 * PATCH * 768 * width, bytes_accessed=5 << 20, transcendentals=0
        ),
        compiler_params=pltpu.CompilerParams(vmem_limit_bytes=12 << 20),
        name="head_rows",
    )(table, spots, *lanes, *after)


def by_core(fill, weight_refs):
    odd = lax.rem(lax.axis_index("brick"), 2) == 1
    ahead, far, _, behind, ahead_other, far_other, _, behind_other = weight_refs[1:]
    mine, other = (ahead, far, behind), (ahead_other, far_other, behind_other)

    @pl.when(jnp.logical_not(odd))
    def _():
        fill(mine, other)

    @pl.when(odd)
    def _():
        fill(other, mine)


def largest(values, top):
    rows, columns = values.shape
    found = jnp.max(jnp.abs(values).reshape(rows // 8, 8, columns), axis=0)
    return found if top is None else jnp.maximum(top, found)


def project_kernel(part, table_ref, spots_ref, *refs):
    lane_refs, gain_ref = refs[:LANES], refs[LANES]
    weight_refs = refs[LANES + 1 : LANES + 10]
    extra_ref = refs[LANES + 10]
    own_ref, keys_ref, values_ref, query_ref, bound_ref, rows_ref, normed_ref, stack_ref = refs[-8:]
    queries = own_ref.shape[0]
    span = GROUP_HEADS * HEAD_DIM
    near_ref = weight_refs[0]
    for kind in range(3):
        stack_ref[kind, :span, :] = near_ref[kind * span : (kind + 1) * span, :]

    def fill(evens, odds):
        for group in range(1, 4):
            rows = slice(group * span, (group + 1) * span)
            stack_ref[0, rows, :] = evens[group - 1][:span, :]
            stack_ref[1, rows, :] = evens[group - 1][span : 2 * span, :]
            stack_ref[2, rows, :] = odds[group - 1][:span, :]

    by_core(fill, weight_refs)
    gain = gain_ref[0:1, :]
    value_top = None
    key_top = None
    for quarter in range(4):
        for block in range(quarter * 2, quarter * 2 + 2):
            rows = slice(block * BLOCK, (block + 1) * BLOCK)
            found = gather_block(table_ref, spots_ref, part * BLOCKS + BLOCKS + block, lane_refs)
            if part == 1:
                found = found + extra_ref[rows, :]
            rows_ref[rows, :] = found
            normed_ref[rows, :] = layer_norm(found, gain)
        rows = slice(quarter * 256, (quarter + 1) * 256)
        normed = normed_ref[rows, :]
        keys = nt_dot(normed, stack_ref[1])
        keys_ref[rows, :] = keys.astype(BF16)
        key_top = largest(keys, key_top)
        values = nt_dot(stack_ref[2], normed)
        values_ref[:, rows] = values.astype(BF16)
        value_top = largest(values, value_top)
    own_rows = pl.ds(pl.multiple_of(lax.axis_index("mp") * queries, queries), queries)
    own_ref[...] = rows_ref[own_rows, :]
    query = nt_dot(stack_ref[0], normed_ref[own_rows, :])
    query_ref[...] = query.astype(BF16)
    query = jnp.minimum(jnp.abs(query), 1e9)
    query_top = jnp.max(jnp.sum((query * query).reshape(-1, HEAD_DIM, queries), axis=1))
    key_top = jnp.minimum(jnp.max(key_top), 1e9)
    bound = 1.05 * SCALE**2 * HEAD_DIM * query_top * (key_top * key_top)
    bound_ref[0] = jnp.where(jnp.max(value_top) < SAFE_VALUE, bound, 2.0 * SAFE_SCORE**2)


def project(part, table, spots, lanes, gains, early, extra, queries):
    width = lanes[0].shape[1]
    shape = lambda *dims: jax.ShapeDtypeStruct(dims, BF16)
    return pl.pallas_call(
        functools.partial(project_kernel, part),
        out_shape=(
            shape(queries, width),
            shape(PATCH, width),
            shape(width, PATCH),
            shape(width, queries),
            jax.ShapeDtypeStruct((1,), F32),
        ),
        in_specs=[SMEM] + [VMEM] * (LANES + 11) + ([VMEM] + [ANY] * (len(extra) - 1) if part else [ANY] * len(extra)),
        out_specs=(VMEM,) * 4 + (SMEM,),
        scratch_shapes=[
            pltpu.VMEM((PATCH, width), BF16),
            pltpu.VMEM((PATCH, width), BF16),
            pltpu.VMEM((3, width, width), BF16),
        ],
        cost_estimate=pl.CostEstimate(flops=10 * 10**9, bytes_accessed=10 << 20, transcendentals=0),
        compiler_params=pltpu.CompilerParams(vmem_limit_bytes=20 << 20),
        name="project_last" if part else "project_first",
    )(table, spots, *lanes, gains, *early, *extra)


def attend_kernel(groups, final, bound_ref, keys_ref, values_ref, query_ref, *refs):
    mixed_ref, score_ref = refs[-2:]
    out_ref = refs[-4] if final else None
    queries = query_ref.shape[1]
    span = GROUP_HEADS * HEAD_DIM
    first = groups[0]

    head_of_row = lax.broadcasted_iota(jnp.int32, (span, queries), 0) // HEAD_DIM
    ones = jnp.ones((HEAD_DIM, BLOCK), BF16)

    def query_of(group, head):
        query = query_ref[group * span : (group + 1) * span, :]
        return jnp.where(head_of_row == head, query, jnp.zeros_like(query))

    def score(slot, group, query, chunk):
        rows = slice(chunk * BLOCK, (chunk + 1) * BLOCK)
        scores = nn_dot(keys_ref[rows, group * span : (group + 1) * span], query)
        score_ref[slot, rows, :] = scores

    def head_step(head, carry):
        for index, group in enumerate(groups):
            last = index + 1 == len(groups)
            later = groups[0] if last else groups[index + 1]
            query = query_of(later, jnp.minimum(head + 1, GROUP_HEADS - 1) if last else head)
            rows = pl.ds(pl.multiple_of(group * span + head * HEAD_DIM, HEAD_DIM), HEAD_DIM)
            total = None
            for chunk in range(BLOCKS):
                keys = slice(chunk * BLOCK, (chunk + 1) * BLOCK)
                score((index + 1) % 2, later, query, chunk)
                weights = jnp.exp2(score_ref[index % 2, keys, :] * SCALE).astype(BF16)
                values = jnp.concatenate([values_ref[rows, keys], ones], axis=0)
                term = nn_dot(values, weights)
                total = term if total is None else total + term
            held = pl.ds(pl.multiple_of((group - first) * span + head * HEAD_DIM, HEAD_DIM), HEAD_DIM)
            mixed_ref[held, :] = (total[:HEAD_DIM] / total[HEAD_DIM : HEAD_DIM + 1]).astype(BF16)
        return carry

    safe = bound_ref[0] < SAFE_SCORE * SAFE_SCORE

    @pl.when(safe)
    def _():
        query = query_of(first, 0)
        for chunk in range(BLOCKS):
            score(0, first, query, chunk)
        lax.fori_loop(0, GROUP_HEADS, head_step, 0)

    def careful_step(index, carry):
        base = pl.multiple_of((first + index // GROUP_HEADS) * span, span)
        head = index % GROUP_HEADS
        query = query_ref[pl.ds(base, span), :]
        query = jnp.where(head_of_row == head, query, jnp.zeros_like(query))
        top, total = None, None
        for chunk in range(BLOCKS):
            keys = slice(chunk * BLOCK, (chunk + 1) * BLOCK)
            scores = nn_dot(keys_ref[keys, pl.ds(base, span)], query)
            score_ref[0, keys, :] = scores
            high = jnp.max(scores, axis=0, keepdims=True)
            top = high if top is None else jnp.maximum(top, high)
        rows = pl.ds(pl.multiple_of(base + head * HEAD_DIM, HEAD_DIM), HEAD_DIM)
        for chunk in range(BLOCKS):
            keys = slice(chunk * BLOCK, (chunk + 1) * BLOCK)
            weights = jnp.exp2((score_ref[0, keys, :] - top) * SCALE).astype(BF16)
            values = jnp.concatenate([values_ref[rows, keys], ones], axis=0)
            term = nn_dot(values, weights)
            total = term if total is None else total + term
        held = pl.ds(pl.multiple_of(index * HEAD_DIM, HEAD_DIM), HEAD_DIM)
        mixed_ref[held, :] = (total[:HEAD_DIM] / total[HEAD_DIM : HEAD_DIM + 1]).astype(BF16)
        return carry

    @pl.when(jnp.logical_not(safe))
    def _():
        lax.fori_loop(0, len(groups) * GROUP_HEADS, careful_step, 0)

    if not final:
        return
    own_ref, weight_refs = refs[0], refs[1:10]
    proj_ref = refs[-3]
    near_ref = weight_refs[0]
    proj_ref[0] = near_ref[3 * span :, :]

    def fill(evens, odds):
        for group in range(1, 4):
            proj_ref[group] = odds[group - 1][span : 2 * span, :]

    by_core(fill, weight_refs)
    mixed = None
    for group in range(4):
        if group < first:
            held = refs[10][group * span : (group + 1) * span, :]
        else:
            held = mixed_ref[(group - first) * span : (group - first + 1) * span, :]
        term = tn_dot(held, proj_ref[group]).astype(BF16).astype(F32)
        mixed = term if mixed is None else mixed + term
    out_ref[...] = (own_ref[...].astype(F32) + mixed).astype(BF16)


def attend(groups, projected, early, prior, after):
    own, keys, values, query, bound = projected
    queries, width = own.shape
    span = GROUP_HEADS * HEAD_DIM
    height = len(groups) * span
    final = groups[-1] == 3
    operands = [bound, keys, values, query]
    if final:
        operands += [own, *early, *prior]
    scratch = [pltpu.VMEM((2, PATCH, queries), F32)]
    if final:
        scratch = [
            pltpu.VMEM((4, span, width), BF16),
            pltpu.VMEM((height, queries), BF16),
        ] + scratch
    return pl.pallas_call(
        functools.partial(attend_kernel, groups, final),
        out_shape=jax.ShapeDtypeStruct((queries, width) if final else (height, queries), BF16),
        in_specs=[SMEM] + [VMEM] * (len(operands) - 1) + [ANY] * len(after),
        out_specs=VMEM,
        scratch_shapes=scratch,
        cost_estimate=pl.CostEstimate(
            flops=8 * 10**9 * len(groups),
            bytes_accessed=5 << 20,
            transcendentals=(2 << 20) * len(groups),
        ),
        compiler_params=pltpu.CompilerParams(vmem_limit_bytes=16 << 20),
    )(*operands, *after)


def mlp_kernel(groups, hidden_ref, gain_ref, up_ref, down_ref, *refs):
    weight_refs, refs = refs[:9], refs[9:]
    refs, ups_ref, downs_ref = refs[:-2], refs[-2], refs[-1]
    depth = hidden_ref.shape[1]
    split = weight_refs[2].shape[0]
    lead = weight_refs[1].shape[0] - depth
    ahead, far_a, far_b, behind, ahead_o, far_a_o, far_b_o, behind_o = weight_refs[1:]
    mine, other = (ahead, far_a, far_b, behind), (ahead_o, far_a_o, far_b_o, behind_o)

    def fill(out_ref, sources):
        out_ref[0] = sources[0][lead:, :]
        out_ref[1, : split - lead, :] = sources[1][lead:, :]
        out_ref[1, split - lead :, :] = sources[2][...]
        out_ref[2] = sources[3][lead:, :]

    odd = lax.rem(lax.axis_index("brick"), 2) == 1

    @pl.when(jnp.logical_not(odd))
    def _():
        fill(ups_ref, mine)
        fill(downs_ref, other)

    @pl.when(odd)
    def _():
        fill(ups_ref, other)
        fill(downs_ref, mine)

    up_refs = (up_ref,) + tuple(ups_ref.at[group] for group in range(3))
    down_refs = (down_ref,) + tuple(downs_ref.at[group] for group in range(3))
    wide_ref, before_ref, result_ref = refs[-3:]
    outs = refs[-3 - groups : -3]
    queries, width = hidden_ref.shape
    normed = layer_norm(hidden_ref[...], gain_ref[1:2, :])
    pieces = [(group, chunk) for group in range(groups) for chunk in range(queries // BLOCK)]

    def widen(index):
        group, chunk = pieces[index]
        before_ref[index % 2] = nn_dot(normed[chunk * BLOCK : (chunk + 1) * BLOCK], up_refs[group][...])

    widen(0)
    for index, (group, chunk) in enumerate(pieces):
        if index + 1 < len(pieces):
            widen(index + 1)
        wide = before_ref[index % 2]
        wide_ref[group, chunk * BLOCK : (chunk + 1) * BLOCK, :] = (
            wide * (0.5 + 0.5 * lax.erf(wide * 0.5**0.5))
        ).astype(BF16)
    total = None
    for group in range(groups):
        term = nn_dot(wide_ref[group], down_refs[group][...]).astype(BF16).astype(F32)
        total = term if total is None else total + term
    result_ref[...] = (hidden_ref[...].astype(F32) + total).astype(BF16)
    cut = width // groups
    rank = lax.axis_index("mp")
    for step in range(groups):
        column = pl.multiple_of(lax.rem(rank + step, groups) * cut, cut)
        outs[step][...] = result_ref[:, pl.ds(column, cut)]


def mlp(hidden, gains, up, down, weights):
    groups = 4
    rows, width = hidden.shape
    middle = up.shape[1]
    return pl.pallas_call(
        functools.partial(mlp_kernel, groups),
        out_shape=(jax.ShapeDtypeStruct((rows, width // groups), BF16),) * groups,
        in_specs=[VMEM] * 13,
        out_specs=(VMEM,) * groups,
        scratch_shapes=[
            pltpu.VMEM((groups, rows, middle), BF16),
            pltpu.VMEM((2, BLOCK, middle), F32),
            pltpu.VMEM((rows, width), BF16),
            pltpu.VMEM((groups - 1, width, middle), BF16),
            pltpu.VMEM((groups - 1, middle, width), BF16),
        ],
        cost_estimate=pl.CostEstimate(
            flops=4 * rows * width * middle * groups, bytes_accessed=5 << 20, transcendentals=0
        ),
        compiler_params=pltpu.CompilerParams(vmem_limit_bytes=18 << 20),
        name="mlp",
    )(hidden, gains, up, down, *weights)


def collect_kernel(*refs):
    sources, out_ref = refs[:4], refs[4]
    collect(sources, out_ref, 0)


def collect(sources, out_ref, base):
    queries = sources[0].shape[0]
    rank = lax.axis_index("mp")
    for index, source in enumerate(sources):
        sender = lax.rem(rank - index + 4, 4)
        at = pl.multiple_of(base + sender * queries, queries)
        out_ref[pl.ds(at, queries), :] = source[...]


def collect_rows(sources):
    return pl.pallas_call(
        collect_kernel,
        out_shape=jax.ShapeDtypeStruct((PATCH, sources[0].shape[1]), BF16),
        in_specs=[VMEM] * 4,
        out_specs=VMEM,
        compiler_params=pltpu.CompilerParams(vmem_limit_bytes=4 << 20),
        name="collect_rows",
    )(*sources)


def pack_kernel(shift_ref, table_ref, spots_ref, *rest):
    tail_ref, last_ref, sources, rest = rest[0], rest[1], rest[2:6], rest[6:]
    outs, lanes_ref, rows_ref = rest[:LANES], rest[LANES], rest[LANES + 1]
    lanes_ref[...] = jnp.zeros_like(lanes_ref)
    rows_ref[:PATCH, :] = tail_ref[...]
    rows_ref[2 * PATCH :, :] = last_ref[...]
    collect(sources, rows_ref, PATCH)
    begin = lax.div(PATCH - shift_ref[0], BLOCK)
    for step in range(2 * BLOCKS + 1):
        place = jnp.minimum(begin + step, 3 * BLOCKS - 1)
        fresh = begin + step < 3 * BLOCKS
        spots = jnp.where(fresh, spots_ref[pl.ds(place, 1), :], -1)
        rows = rows_ref[pl.ds(pl.multiple_of(place * BLOCK, BLOCK), BLOCK), :]
        sent = nn_dot(hot_rows(spots), rows).astype(BF16)
        for lane in range(LANES):
            window = pl.ds(aligned(table_ref[place, lane]), WINDOW)
            lanes_ref[lane, window, :] = (
                lanes_ref[lane, window, :] + sent[lane * WINDOW : (lane + 1) * WINDOW]
            )
    for lane in range(LANES):
        outs[lane][...] = lanes_ref[lane]


def pack_lanes(shift, table, spots, sources):
    width = sources[0].shape[1]
    return pl.pallas_call(
        pack_kernel,
        out_shape=(jax.ShapeDtypeStruct((PIECE, width), BF16),) * LANES,
        in_specs=[SMEM, SMEM] + [VMEM] * (1 + len(sources)),
        out_specs=(VMEM,) * LANES,
        scratch_shapes=[
            pltpu.VMEM((LANES, PIECE, width), BF16),
            pltpu.VMEM((3 * PATCH, width), BF16),
        ],
        compiler_params=pltpu.CompilerParams(vmem_limit_bytes=12 << 20),
        name="pack_lanes",
    )(shift, table, spots, *sources)


def place_kernel(counts_ref, *refs):
    pieces, out_ref = refs[:LANES], refs[LANES]
    capacity = out_ref.shape[0]
    out_ref[...] = jnp.zeros_like(out_ref)
    row = lax.broadcasted_iota(jnp.int32, (PIECE, out_ref.shape[1]), 0)
    for lane in range(LANES):
        start = window_start(counts_ref[0, lane], capacity)
        slots = row + start
        mine = (slots >= counts_ref[0, lane]) & (slots < counts_ref[1, lane])
        window = pl.ds(start, PIECE)
        out_ref[window, :] = jnp.where(mine, pieces[lane][...], out_ref[window, :])


def place_rows(counts, pieces, capacity):
    width = pieces[0].shape[1]
    return pl.pallas_call(
        place_kernel,
        out_shape=jax.ShapeDtypeStruct((capacity, width), BF16),
        in_specs=[SMEM] + [VMEM] * LANES,
        out_specs=VMEM,
        compiler_params=pltpu.CompilerParams(vmem_limit_bytes=12 << 20),
        name="place_rows",
    )(counts, *pieces)


def body(
    voxel_feats,
    slot_rank,
    curve_order,
    patch_shift,
    qkv_weight,
    proj_weight,
    up_weight,
    down_weight,
    norm_gains,
):
    bricks = lax.axis_size("brick")
    parts = lax.axis_size("mp")
    capacity, _ = voxel_feats.shape
    shard = curve_order.shape[0]
    queries = PATCH // parts

    piece3, piece2, piece0, counts = cut_windows(
        bricks, shard, slot_rank.reshape(capacity // 128, 128), voxel_feats
    )
    lane3 = shifted(piece3, "brick", -2)
    lane2 = shifted(piece2, "brick", -1)
    lane0 = shifted(piece0, "brick", 1)
    near, half = sort_weights(qkv_weight, proj_weight, up_weight, down_weight, piece0)
    middle = half.shape[0] // 2

    def swapped(value):
        return lax.ppermute(value, "brick", [(brick, brick ^ 1) for brick in range(bricks)])

    ahead = shifted(half, "mp", 1)
    behind = shifted(half, "mp", -1)
    far_a = shifted(ahead[:middle], "mp", 1)
    far_b = shifted(behind[middle:], "mp", -1)
    ahead_other = swapped(ahead)
    behind_other = swapped(behind)
    far_a_other = swapped(far_a)
    far_b_other = swapped(far_b)
    weights = (near, ahead, far_a, far_b, behind, ahead_other, far_a_other, far_b_other, behind_other)

    spots, table, own = index_tables(
        bricks, patch_shift, counts, curve_order.reshape(shard // BLOCK, BLOCK), voxel_feats, near
    )
    lanes = (lane0, own, lane2, lane3)
    head = head_rows(table, spots, lanes, ())
    head_next = shifted(head, "brick", -1)
    common = (table, spots, lanes, norm_gains, weights)
    patch0 = project(0, *common, (head,), queries)
    mixed = attend((0, 1), patch0, weights, (), ())
    patch1 = project(1, *common, (head_next, mixed), queries)

    blocks = mlp(attend((0, 1, 2, 3), patch1, weights, (), ()), norm_gains, up_weight, down_weight, weights)

    last = [blocks[0]]
    for step in range(1, parts):
        last.append(shifted(blocks[step], "mp", step))
    hidden = attend((2, 3), patch0, weights, (mixed,), (blocks[0],))
    last = collect_rows(last)
    tail = shifted(last, "brick", 1)
    blocks = mlp(hidden, norm_gains, up_weight, down_weight, weights)
    first = [blocks[0]] + [shifted(blocks[step], "mp", step) for step in range(1, parts)]
    back0, back1, back2, back3 = pack_lanes(patch_shift, table, spots, (tail, last, *first))
    back3 = shifted(back3, "brick", 2)
    back2 = shifted(back2, "brick", 1)
    back0 = shifted(back0, "brick", -1)
    return place_rows(counts, (back0, back1, back2, back3), capacity)


def solution(mesh):
    return jax.shard_map(
        body,
        mesh=mesh,
        in_specs=(
            P("brick", None),
            P("brick"),
            P("brick"),
            P(),
            P(None, "mp"),
            P("mp", None),
            P(None, "mp"),
            P("mp", None),
            P(),
        ),
        out_specs=P("brick", "mp"),
        check_vma=False,
    )
```

```python
import functools

import jax
import jax.numpy as jnp
from jax import lax
from jax.experimental import pallas as pl
from jax.experimental.pallas import tpu as pltpu
from jax.sharding import PartitionSpec as P

PATCH = 1024
HEAD_DIM = 16
GROUP_HEADS = 8
EPSILON = 1e-05
SCALE = HEAD_DIM ** (-0.5) * 1.4426950408889634
SAFE_SCORE = 100.0
SAFE_VALUE = 1e4

TILE = 16
BLOCK = 128
WINDOW = 160
MOST_RUN = 768
PIECE = MOST_RUN + TILE
LANES = 4
BLOCKS = PATCH // BLOCK


F32 = jnp.float32
BF16 = jnp.bfloat16

ANY = pl.BlockSpec(memory_space=pl.ANY)
VMEM = pl.BlockSpec(memory_space=pltpu.VMEM)
SMEM = pl.BlockSpec(memory_space=pltpu.SMEM)
HBM = pl.BlockSpec(memory_space=pltpu.HBM)


def nt_dot(left, right):
    return lax.dot_general(left, right, (((1,), (1,)), ((), ())), preferred_element_type=F32)


def nn_dot(left, right):
    return jnp.dot(left, right, preferred_element_type=F32)


def tn_dot(left, right):
    return lax.dot_general(left, right, (((0,), (0,)), ((), ())), preferred_element_type=F32)


def aligned(value):
    return pl.multiple_of(value, TILE)


def shifted(value, axis, steps):
    count = lax.axis_size(axis)
    pairs = [(source, (source + steps) % count) for source in range(count)]
    return lax.ppermute(value, axis, pairs)


def layer_norm(values, gain):
    values = values.astype(F32)
    centred = values - jnp.mean(values, axis=-1, keepdims=True)
    spread = jnp.mean(centred * centred, axis=-1, keepdims=True)
    return (centred * lax.rsqrt(spread + EPSILON) * gain).astype(BF16)


def window_start(first, capacity):
    return aligned(jnp.minimum(lax.div(first, TILE) * TILE, capacity - PIECE))


def cut_kernel(bricks, shard, ranks_ref, feats_ref, *rest):
    outs, counts_ref, sems = rest[:3], rest[3], rest[4]
    capacity = feats_ref.shape[0]
    me = lax.axis_index("brick")
    ranks = ranks_ref[...]
    loads = []
    for index, lane in enumerate((3, 2, 0)):
        target = lax.rem(me - lane + 1 + bricks, bricks)
        first = jnp.sum((ranks < target * shard).astype(jnp.int32))
        counts_ref[0, lane] = first
        rows = pl.ds(window_start(first, capacity), PIECE)
        loads.append(pltpu.make_async_copy(feats_ref.at[rows], outs[index], sems.at[index]))
        loads[-1].start()
    counts_ref[0, 1] = jnp.sum((ranks < me * shard).astype(jnp.int32))
    for lane in range(LANES):
        target = lax.rem(me - lane + 1 + bricks, bricks)
        counts_ref[1, lane] = jnp.sum((ranks < (target + 1) * shard).astype(jnp.int32))
    for load in loads:
        load.wait()


def cut_windows(bricks, shard, ranks, feats):
    piece = jax.ShapeDtypeStruct((PIECE, feats.shape[1]), feats.dtype)
    return pl.pallas_call(
        functools.partial(cut_kernel, bricks, shard),
        out_shape=(piece,) * 3 + (jax.ShapeDtypeStruct((2, LANES), jnp.int32),),
        in_specs=[VMEM, HBM],
        out_specs=(VMEM,) * 3 + (SMEM,),
        scratch_shapes=[pltpu.SemaphoreType.DMA((3,))],
        compiler_params=pltpu.CompilerParams(vmem_limit_bytes=8 << 20),
        name="cut_windows",
    )(ranks, pltpu.with_memory_space_constraint(feats, pltpu.HBM))


def weights_kernel(qkv_ref, proj_ref, up_ref, down_ref, after_ref, near_ref, half_ref):
    span = GROUP_HEADS * HEAD_DIM
    shape = (3 * span, 3 * span)
    row = lax.broadcasted_iota(jnp.int32, shape, 0)
    column = lax.broadcasted_iota(jnp.int32, shape, 1)
    kind, rest = row // span, row % span
    source = rest // HEAD_DIM * (3 * HEAD_DIM) + kind * HEAD_DIM + rest % HEAD_DIM
    order = jnp.where(column == source, 1.0, 0.0).astype(BF16)
    near_ref[: 3 * span, :] = nt_dot(order, qkv_ref[...]).astype(BF16)
    near_ref[3 * span :, :] = proj_ref[...]
    odd = lax.rem(lax.axis_index("brick"), 2) == 1

    @pl.when(jnp.logical_not(odd))
    def _():
        half_ref[: 2 * span, :] = near_ref[: 2 * span, :]
        half_ref[2 * span :, :] = up_ref[...]

    @pl.when(odd)
    def _():
        half_ref[: 2 * span, :] = near_ref[2 * span :, :]
        half_ref[2 * span :, :] = down_ref[...]


def sort_weights(qkv, proj, up, down, after):
    width = proj.shape[1]
    span = GROUP_HEADS * HEAD_DIM
    return pl.pallas_call(
        weights_kernel,
        out_shape=(
            jax.ShapeDtypeStruct((4 * span, width), BF16),
            jax.ShapeDtypeStruct((2 * span + up.shape[0], width), BF16),
        ),
        in_specs=[VMEM] * 4 + [ANY],
        out_specs=(VMEM, VMEM),
        compiler_params=pltpu.CompilerParams(vmem_limit_bytes=8 << 20),
        name="sort_weights",
    )(qkv, proj, up, down, after)


def index_kernel(
    bricks, shift_ref, counts_ref, order_ref, feats_ref, after_ref, spots_ref, table_ref, own_ref, wide_ref, sem
):
    capacity = feats_ref.shape[0]
    rows = pl.ds(window_start(counts_ref[0, 1], capacity), PIECE)
    load = pltpu.make_async_copy(feats_ref.at[rows], own_ref, sem)
    load.start()
    me = lax.axis_index("brick")
    order = order_ref[...]
    rows = order.shape[0]
    lane_of = jnp.zeros_like(order)
    spot_of = jnp.zeros_like(order)
    column = lax.broadcasted_iota(jnp.int32, (1, BLOCK), 1)
    leads = jnp.zeros((1, BLOCK), F32)
    for lane in range(LANES):
        source = lax.rem(me + lane - 1 + bricks, bricks)
        slot = order - source * capacity
        mine = (slot >= 0) & (slot < capacity)
        first = jnp.min(jnp.where(mine, slot, capacity), keepdims=True)
        start = jnp.minimum(first & -TILE, capacity - PIECE)
        lane_of = jnp.where(mine, lane, lane_of)
        spot_of = jnp.where(mine, slot - start + lane * WINDOW, spot_of)
        leads = jnp.where(column == lane, (first - start).astype(F32), leads)
    ahead = PATCH - shift_ref[0]
    down, across = lax.div(ahead, BLOCK), lax.rem(ahead, BLOCK)
    wide_ref[...] = jnp.full_like(wide_ref, -1)
    for index, value in enumerate((lane_of, spot_of)):
        turned = pltpu.roll(value, across, 1)
        wide_ref[index, 0, pl.ds(down, rows), :] = turned
        wide_ref[index, 1, pl.ds(down + 1, rows), :] = turned
    height = spots_ref.shape[0]
    near = lax.broadcasted_iota(jnp.int32, (height, BLOCK), 1) >= across
    lane_wide = jnp.where(near, wide_ref[0, 0, :height, :], wide_ref[0, 1, :height, :])
    spot_wide = jnp.where(near, wide_ref[1, 0, :height, :], wide_ref[1, 1, :height, :])
    held = jnp.zeros((height, BLOCK), F32)
    wide_column = lax.broadcasted_iota(jnp.int32, (height, BLOCK), 1)
    for lane in range(LANES):
        found = jnp.sum((lane_wide == lane).astype(F32), axis=1, keepdims=True)
        held = jnp.where(wide_column == lane, found, held)
    below = lax.broadcasted_iota(jnp.int32, (height, height), 1) < lax.broadcasted_iota(
        jnp.int32, (height, height), 0
    )
    before = nn_dot(below.astype(F32).astype(BF16), held.astype(BF16))
    table = jnp.minimum((leads + before).astype(jnp.int32) & -TILE, PIECE - WINDOW)
    table_ref[...] = table
    spots = spot_wide
    for lane in range(LANES):
        spots = jnp.where(lane_wide == lane, spot_wide - table[:, lane : lane + 1], spots)
    spots_ref[...] = jnp.where(lane_wide < 0, -1, spots)
    load.wait()


def index_tables(bricks, shift, counts, order, feats, after):
    height = 3 * BLOCKS
    table = jax.ShapeDtypeStruct((height, BLOCK), jnp.int32)
    return pl.pallas_call(
        functools.partial(index_kernel, bricks),
        out_shape=(table, table, jax.ShapeDtypeStruct((PIECE, feats.shape[1]), feats.dtype)),
        in_specs=[SMEM, SMEM, VMEM, HBM, ANY],
        out_specs=(VMEM,) * 3,
        scratch_shapes=[
            pltpu.VMEM((2, 2, height + 2 * BLOCKS, BLOCK), jnp.int32),
            pltpu.SemaphoreType.DMA,
        ],
        compiler_params=pltpu.CompilerParams(vmem_limit_bytes=4 << 20),
        name="index_tables",
    )(shift, counts, order, pltpu.with_memory_space_constraint(feats, pltpu.HBM), after)


def hot_rows(spots):
    tall = lax.broadcasted_iota(jnp.int32, (LANES * WINDOW, BLOCK), 0)
    return jnp.where(tall == spots, 1.0, 0.0).astype(BF16)


def gather_block(table_ref, spots_ref, place, lane_refs):
    windows = [
        lane_refs[lane][pl.ds(aligned(table_ref[place, lane]), WINDOW), :]
        for lane in range(LANES)
    ]
    stacked = jnp.concatenate(windows, axis=0)
    return tn_dot(hot_rows(spots_ref[place : place + 1, :]), stacked).astype(BF16)


def head_kernel(table_ref, spots_ref, *refs):
    out_ref = refs[-1]
    for block in range(BLOCKS):
        rows = slice(block * BLOCK, (block + 1) * BLOCK)
        out_ref[rows, :] = gather_block(table_ref, spots_ref, block, refs[:LANES])


def head_rows(table, spots, lanes, after):
    width = lanes[0].shape[1]
    return pl.pallas_call(
        head_kernel,
        out_shape=jax.ShapeDtypeStruct((PATCH, width), BF16),
        in_specs=[SMEM] + [VMEM] * (1 + LANES) + [ANY] * len(after),
        out_specs=VMEM,
        cost_estimate=pl.CostEstimate(
            flops=2 * PATCH * 768 * width, bytes_accessed=5 << 20, transcendentals=0
        ),
        compiler_params=pltpu.CompilerParams(vmem_limit_bytes=12 << 20),
        name="head_rows",
    )(table, spots, *lanes, *after)


def by_core(fill, weight_refs):
    odd = lax.rem(lax.axis_index("brick"), 2) == 1
    ahead, far, _, behind, ahead_other, far_other, _, behind_other = weight_refs[1:]
    mine, other = (ahead, far, behind), (ahead_other, far_other, behind_other)

    @pl.when(jnp.logical_not(odd))
    def _():
        fill(mine, other)

    @pl.when(odd)
    def _():
        fill(other, mine)


def largest(values, top):
    rows, columns = values.shape
    found = jnp.max(jnp.abs(values).reshape(rows // 8, 8, columns), axis=0)
    return found if top is None else jnp.maximum(top, found)


def gather_kernel(table_ref, spots_ref, *refs):
    lane_refs, gain_ref = refs[:LANES], refs[LANES]
    own_ref, normed_ref, rows_ref = refs[-3:]
    gain = gain_ref[0:1, :]
    for block in range(BLOCKS):
        rows = slice(block * BLOCK, (block + 1) * BLOCK)
        found = gather_block(table_ref, spots_ref, BLOCKS + block, lane_refs)
        rows_ref[rows, :] = found
        normed_ref[rows, :] = layer_norm(found, gain)
    queries = own_ref.shape[0]
    own_rows = pl.ds(pl.multiple_of(lax.axis_index("mp") * queries, queries), queries)
    own_ref[...] = rows_ref[own_rows, :]


def gather_first(table, spots, lanes, gains, after, queries):
    width = lanes[0].shape[1]
    return pl.pallas_call(
        gather_kernel,
        out_shape=(
            jax.ShapeDtypeStruct((queries, width), BF16),
            jax.ShapeDtypeStruct((PATCH, width), BF16),
        ),
        in_specs=[SMEM] + [VMEM] * (LANES + 2) + [ANY],
        out_specs=(VMEM, VMEM),
        scratch_shapes=[pltpu.VMEM((PATCH, width), BF16)],
        cost_estimate=pl.CostEstimate(flops=10**9, bytes_accessed=5 << 20, transcendentals=0),
        compiler_params=pltpu.CompilerParams(vmem_limit_bytes=12 << 20),
        name="gather_first",
    )(table, spots, *lanes, gains, after)


def project_kernel(part, table_ref, spots_ref, *refs):
    lane_refs, gain_ref = refs[:LANES], refs[LANES]
    weight_refs = refs[LANES + 1 : LANES + 10]
    extra_ref = refs[LANES + 10]
    if part == 1:
        own_ref, keys_ref, values_ref, query_ref, bound_ref, rows_ref, normed_ref, stack_ref = refs[-8:]
    else:
        keys_ref, values_ref, query_ref, bound_ref, stack_ref = refs[-5:]
        normed_ref = extra_ref
    queries = query_ref.shape[1]
    span = GROUP_HEADS * HEAD_DIM
    near_ref = weight_refs[0]
    for kind in range(3):
        stack_ref[kind, :span, :] = near_ref[kind * span : (kind + 1) * span, :]

    def fill(evens, odds):
        for group in range(1, 4):
            rows = slice(group * span, (group + 1) * span)
            stack_ref[0, rows, :] = evens[group - 1][:span, :]
            stack_ref[1, rows, :] = evens[group - 1][span : 2 * span, :]
            stack_ref[2, rows, :] = odds[group - 1][:span, :]

    by_core(fill, weight_refs)
    gain = gain_ref[0:1, :]
    value_top = None
    key_top = None
    for quarter in range(4):
        for block in range(quarter * 2, quarter * 2 + 2) if part else ():
            rows = slice(block * BLOCK, (block + 1) * BLOCK)
            found = gather_block(table_ref, spots_ref, 2 * BLOCKS + block, lane_refs)
            found = found + extra_ref[rows, :]
            rows_ref[rows, :] = found
            normed_ref[rows, :] = layer_norm(found, gain)
        rows = slice(quarter * 256, (quarter + 1) * 256)
        normed = normed_ref[rows, :]
        keys = nt_dot(normed, stack_ref[1])
        keys_ref[rows, :] = keys.astype(BF16)
        key_top = largest(keys, key_top)
        values = nt_dot(stack_ref[2], normed)
        values_ref[:, rows] = values.astype(BF16)
        value_top = largest(values, value_top)
    own_rows = pl.ds(pl.multiple_of(lax.axis_index("mp") * queries, queries), queries)
    if part == 1:
        own_ref[...] = rows_ref[own_rows, :]
    query = nt_dot(stack_ref[0], normed_ref[own_rows, :])
    query_ref[...] = query.astype(BF16)
    query = jnp.minimum(jnp.abs(query), 1e9)
    query_top = jnp.max(jnp.sum((query * query).reshape(-1, HEAD_DIM, queries), axis=1))
    key_top = jnp.minimum(jnp.max(key_top), 1e9)
    bound = 1.05 * SCALE**2 * HEAD_DIM * query_top * (key_top * key_top)
    bound_ref[0] = jnp.where(jnp.max(value_top) < SAFE_VALUE, bound, 2.0 * SAFE_SCORE**2)


def project(part, table, spots, lanes, gains, weights, extra, queries):
    width = lanes[0].shape[1]
    shape = lambda *dims: jax.ShapeDtypeStruct(dims, BF16)
    rows = [pltpu.VMEM((PATCH, width), BF16)] * 2 if part else []
    return pl.pallas_call(
        functools.partial(project_kernel, part),
        out_shape=(shape(queries, width),) * part
        + (
            shape(PATCH, width),
            shape(width, PATCH),
            shape(width, queries),
            jax.ShapeDtypeStruct((1,), F32),
        ),
        in_specs=[SMEM] + [VMEM] * (LANES + 12) + [ANY] * (len(extra) - 1),
        out_specs=(VMEM,) * (3 + part) + (SMEM,),
        scratch_shapes=rows + [pltpu.VMEM((3, width, width), BF16)],
        cost_estimate=pl.CostEstimate(flops=10 * 10**9, bytes_accessed=10 << 20, transcendentals=0),
        compiler_params=pltpu.CompilerParams(vmem_limit_bytes=20 << 20),
        name="project_last" if part else "project_first",
    )(table, spots, *lanes, gains, *weights, *extra)


def attend_kernel(groups, final, bound_ref, keys_ref, values_ref, query_ref, *refs):
    mixed_ref, score_ref = refs[-2:]
    out_ref = refs[-4] if final else None
    queries = query_ref.shape[1]
    span = GROUP_HEADS * HEAD_DIM
    first = groups[0]

    head_of_row = lax.broadcasted_iota(jnp.int32, (span, queries), 0) // HEAD_DIM
    ones = jnp.ones((HEAD_DIM, BLOCK), BF16)

    def query_of(group, head):
        query = query_ref[group * span : (group + 1) * span, :]
        return jnp.where(head_of_row == head, query, jnp.zeros_like(query))

    def score(slot, group, query, chunk):
        rows = slice(chunk * BLOCK, (chunk + 1) * BLOCK)
        scores = nn_dot(keys_ref[rows, group * span : (group + 1) * span], query)
        score_ref[slot, rows, :] = scores

    def head_step(head, carry):
        for index, group in enumerate(groups):
            last = index + 1 == len(groups)
            later = groups[0] if last else groups[index + 1]
            query = query_of(later, jnp.minimum(head + 1, GROUP_HEADS - 1) if last else head)
            rows = pl.ds(pl.multiple_of(group * span + head * HEAD_DIM, HEAD_DIM), HEAD_DIM)
            total = None
            for chunk in range(BLOCKS):
                keys = slice(chunk * BLOCK, (chunk + 1) * BLOCK)
                score((index + 1) % 2, later, query, chunk)
                weights = jnp.exp2(score_ref[index % 2, keys, :] * SCALE).astype(BF16)
                values = jnp.concatenate([values_ref[rows, keys], ones], axis=0)
                term = nn_dot(values, weights)
                total = term if total is None else total + term
            held = pl.ds(pl.multiple_of((group - first) * span + head * HEAD_DIM, HEAD_DIM), HEAD_DIM)
            mixed_ref[held, :] = (total[:HEAD_DIM] / total[HEAD_DIM : HEAD_DIM + 1]).astype(BF16)
        return carry

    safe = bound_ref[0] < SAFE_SCORE * SAFE_SCORE

    @pl.when(safe)
    def _():
        query = query_of(first, 0)
        for chunk in range(BLOCKS):
            score(0, first, query, chunk)
        lax.fori_loop(0, GROUP_HEADS, head_step, 0)

    def careful_step(index, carry):
        base = pl.multiple_of((first + index // GROUP_HEADS) * span, span)
        head = index % GROUP_HEADS
        query = query_ref[pl.ds(base, span), :]
        query = jnp.where(head_of_row == head, query, jnp.zeros_like(query))
        top, total = None, None
        for chunk in range(BLOCKS):
            keys = slice(chunk * BLOCK, (chunk + 1) * BLOCK)
            scores = nn_dot(keys_ref[keys, pl.ds(base, span)], query)
            score_ref[0, keys, :] = scores
            high = jnp.max(scores, axis=0, keepdims=True)
            top = high if top is None else jnp.maximum(top, high)
        rows = pl.ds(pl.multiple_of(base + head * HEAD_DIM, HEAD_DIM), HEAD_DIM)
        for chunk in range(BLOCKS):
            keys = slice(chunk * BLOCK, (chunk + 1) * BLOCK)
            weights = jnp.exp2((score_ref[0, keys, :] - top) * SCALE).astype(BF16)
            values = jnp.concatenate([values_ref[rows, keys], ones], axis=0)
            term = nn_dot(values, weights)
            total = term if total is None else total + term
        held = pl.ds(pl.multiple_of(index * HEAD_DIM, HEAD_DIM), HEAD_DIM)
        mixed_ref[held, :] = (total[:HEAD_DIM] / total[HEAD_DIM : HEAD_DIM + 1]).astype(BF16)
        return carry

    @pl.when(jnp.logical_not(safe))
    def _():
        lax.fori_loop(0, len(groups) * GROUP_HEADS, careful_step, 0)

    if not final:
        return
    own_ref, weight_refs = refs[0], refs[1:10]
    proj_ref = refs[-3]
    near_ref = weight_refs[0]
    proj_ref[0] = near_ref[3 * span :, :]

    def fill(evens, odds):
        for group in range(1, 4):
            proj_ref[group] = odds[group - 1][span : 2 * span, :]

    by_core(fill, weight_refs)
    mixed = None
    for group in range(4):
        if group < first:
            held = refs[10][group * span : (group + 1) * span, :]
        else:
            held = mixed_ref[(group - first) * span : (group - first + 1) * span, :]
        term = tn_dot(held, proj_ref[group]).astype(BF16).astype(F32)
        mixed = term if mixed is None else mixed + term
    out_ref[...] = (own_ref[...].astype(F32) + mixed).astype(BF16)


def attend(groups, projected, early, prior, after):
    own, keys, values, query, bound = projected
    queries, width = own.shape
    span = GROUP_HEADS * HEAD_DIM
    height = len(groups) * span
    final = groups[-1] == 3
    operands = [bound, keys, values, query]
    if final:
        operands += [own, *early, *prior]
    scratch = [pltpu.VMEM((2, PATCH, queries), F32)]
    if final:
        scratch = [
            pltpu.VMEM((4, span, width), BF16),
            pltpu.VMEM((height, queries), BF16),
        ] + scratch
    return pl.pallas_call(
        functools.partial(attend_kernel, groups, final),
        out_shape=jax.ShapeDtypeStruct((queries, width) if final else (height, queries), BF16),
        in_specs=[SMEM] + [VMEM] * (len(operands) - 1) + [ANY] * len(after),
        out_specs=VMEM,
        scratch_shapes=scratch,
        cost_estimate=pl.CostEstimate(
            flops=8 * 10**9 * len(groups),
            bytes_accessed=5 << 20,
            transcendentals=(2 << 20) * len(groups),
        ),
        compiler_params=pltpu.CompilerParams(vmem_limit_bytes=16 << 20),
    )(*operands, *after)


def mlp_kernel(groups, hidden_ref, gain_ref, up_ref, down_ref, *refs):
    weight_refs, refs = refs[:9], refs[9:]
    refs, ups_ref, downs_ref = refs[:-2], refs[-2], refs[-1]
    depth = hidden_ref.shape[1]
    split = weight_refs[2].shape[0]
    lead = weight_refs[1].shape[0] - depth
    ahead, far_a, far_b, behind, ahead_o, far_a_o, far_b_o, behind_o = weight_refs[1:]
    mine, other = (ahead, far_a, far_b, behind), (ahead_o, far_a_o, far_b_o, behind_o)

    def fill(out_ref, sources):
        out_ref[0] = sources[0][lead:, :]
        out_ref[1, : split - lead, :] = sources[1][lead:, :]
        out_ref[1, split - lead :, :] = sources[2][...]
        out_ref[2] = sources[3][lead:, :]

    odd = lax.rem(lax.axis_index("brick"), 2) == 1

    @pl.when(jnp.logical_not(odd))
    def _():
        fill(ups_ref, mine)
        fill(downs_ref, other)

    @pl.when(odd)
    def _():
        fill(ups_ref, other)
        fill(downs_ref, mine)

    up_refs = (up_ref,) + tuple(ups_ref.at[group] for group in range(3))
    down_refs = (down_ref,) + tuple(downs_ref.at[group] for group in range(3))
    wide_ref, before_ref, result_ref = refs[-3:]
    outs = refs[-3 - groups : -3]
    queries, width = hidden_ref.shape
    normed = layer_norm(hidden_ref[...], gain_ref[1:2, :])
    pieces = [(group, chunk) for group in range(groups) for chunk in range(queries // BLOCK)]

    def widen(index):
        group, chunk = pieces[index]
        before_ref[index % 2] = nn_dot(normed[chunk * BLOCK : (chunk + 1) * BLOCK], up_refs[group][...])

    widen(0)
    for index, (group, chunk) in enumerate(pieces):
        if index + 1 < len(pieces):
            widen(index + 1)
        wide = before_ref[index % 2]
        wide_ref[group, chunk * BLOCK : (chunk + 1) * BLOCK, :] = (
            wide * (0.5 + 0.5 * lax.erf(wide * 0.5**0.5))
        ).astype(BF16)
    total = None
    for group in range(groups):
        term = nn_dot(wide_ref[group], down_refs[group][...]).astype(BF16).astype(F32)
        total = term if total is None else total + term
    result_ref[...] = (hidden_ref[...].astype(F32) + total).astype(BF16)
    cut = width // groups
    rank = lax.axis_index("mp")
    for step in range(groups):
        column = pl.multiple_of(lax.rem(rank + step, groups) * cut, cut)
        outs[step][...] = result_ref[:, pl.ds(column, cut)]


def mlp(hidden, gains, up, down, weights):
    groups = 4
    rows, width = hidden.shape
    middle = up.shape[1]
    return pl.pallas_call(
        functools.partial(mlp_kernel, groups),
        out_shape=(jax.ShapeDtypeStruct((rows, width // groups), BF16),) * groups,
        in_specs=[VMEM] * 13,
        out_specs=(VMEM,) * groups,
        scratch_shapes=[
            pltpu.VMEM((groups, rows, middle), BF16),
            pltpu.VMEM((2, BLOCK, middle), F32),
            pltpu.VMEM((rows, width), BF16),
            pltpu.VMEM((groups - 1, width, middle), BF16),
            pltpu.VMEM((groups - 1, middle, width), BF16),
        ],
        cost_estimate=pl.CostEstimate(
            flops=4 * rows * width * middle * groups, bytes_accessed=5 << 20, transcendentals=0
        ),
        compiler_params=pltpu.CompilerParams(vmem_limit_bytes=18 << 20),
        name="mlp",
    )(hidden, gains, up, down, *weights)


def collect_kernel(*refs):
    sources, out_ref = refs[:4], refs[4]
    collect(sources, out_ref, 0)


def collect(sources, out_ref, base):
    queries = sources[0].shape[0]
    rank = lax.axis_index("mp")
    for index, source in enumerate(sources):
        sender = lax.rem(rank - index + 4, 4)
        at = pl.multiple_of(base + sender * queries, queries)
        out_ref[pl.ds(at, queries), :] = source[...]


def collect_rows(sources):
    return pl.pallas_call(
        collect_kernel,
        out_shape=jax.ShapeDtypeStruct((PATCH, sources[0].shape[1]), BF16),
        in_specs=[VMEM] * 4,
        out_specs=VMEM,
        compiler_params=pltpu.CompilerParams(vmem_limit_bytes=4 << 20),
        name="collect_rows",
    )(*sources)


def pack_kernel(shift_ref, table_ref, spots_ref, *rest):
    tail_ref, last_ref, sources, rest = rest[0], rest[1], rest[2:6], rest[6:]
    outs, lanes_ref, rows_ref = rest[:LANES], rest[LANES], rest[LANES + 1]
    lanes_ref[...] = jnp.zeros_like(lanes_ref)
    rows_ref[:PATCH, :] = tail_ref[...]
    rows_ref[2 * PATCH :, :] = last_ref[...]
    collect(sources, rows_ref, PATCH)
    begin = lax.div(PATCH - shift_ref[0], BLOCK)
    for step in range(2 * BLOCKS + 1):
        place = jnp.minimum(begin + step, 3 * BLOCKS - 1)
        fresh = begin + step < 3 * BLOCKS
        spots = jnp.where(fresh, spots_ref[pl.ds(place, 1), :], -1)
        rows = rows_ref[pl.ds(pl.multiple_of(place * BLOCK, BLOCK), BLOCK), :]
        sent = nn_dot(hot_rows(spots), rows).astype(BF16)
        for lane in range(LANES):
            window = pl.ds(aligned(table_ref[place, lane]), WINDOW)
            lanes_ref[lane, window, :] = (
                lanes_ref[lane, window, :] + sent[lane * WINDOW : (lane + 1) * WINDOW]
            )
    for lane in range(LANES):
        outs[lane][...] = lanes_ref[lane]


def pack_lanes(shift, table, spots, sources):
    width = sources[0].shape[1]
    return pl.pallas_call(
        pack_kernel,
        out_shape=(jax.ShapeDtypeStruct((PIECE, width), BF16),) * LANES,
        in_specs=[SMEM, SMEM] + [VMEM] * (1 + len(sources)),
        out_specs=(VMEM,) * LANES,
        scratch_shapes=[
            pltpu.VMEM((LANES, PIECE, width), BF16),
            pltpu.VMEM((3 * PATCH, width), BF16),
        ],
        compiler_params=pltpu.CompilerParams(vmem_limit_bytes=12 << 20),
        name="pack_lanes",
    )(shift, table, spots, *sources)


def place_kernel(counts_ref, *refs):
    pieces, out_ref = refs[:LANES], refs[LANES]
    capacity = out_ref.shape[0]
    out_ref[...] = jnp.zeros_like(out_ref)
    row = lax.broadcasted_iota(jnp.int32, (PIECE, out_ref.shape[1]), 0)
    for lane in range(LANES):
        start = window_start(counts_ref[0, lane], capacity)
        slots = row + start
        mine = (slots >= counts_ref[0, lane]) & (slots < counts_ref[1, lane])
        window = pl.ds(start, PIECE)
        out_ref[window, :] = jnp.where(mine, pieces[lane][...], out_ref[window, :])


def place_rows(counts, pieces, capacity):
    width = pieces[0].shape[1]
    return pl.pallas_call(
        place_kernel,
        out_shape=jax.ShapeDtypeStruct((capacity, width), BF16),
        in_specs=[SMEM] + [VMEM] * LANES,
        out_specs=VMEM,
        compiler_params=pltpu.CompilerParams(vmem_limit_bytes=12 << 20),
        name="place_rows",
    )(counts, *pieces)


def body(
    voxel_feats,
    slot_rank,
    curve_order,
    patch_shift,
    qkv_weight,
    proj_weight,
    up_weight,
    down_weight,
    norm_gains,
):
    bricks = lax.axis_size("brick")
    parts = lax.axis_size("mp")
    capacity, _ = voxel_feats.shape
    shard = curve_order.shape[0]
    queries = PATCH // parts

    piece3, piece2, piece0, counts = cut_windows(
        bricks, shard, slot_rank.reshape(capacity // 128, 128), voxel_feats
    )
    lane3 = shifted(piece3, "brick", -2)
    lane2 = shifted(piece2, "brick", -1)
    lane0 = shifted(piece0, "brick", 1)
    near, half = sort_weights(qkv_weight, proj_weight, up_weight, down_weight, piece0)
    middle = half.shape[0] // 2

    def swapped(value):
        return lax.ppermute(value, "brick", [(brick, brick ^ 1) for brick in range(bricks)])

    ahead = shifted(half, "mp", 1)
    behind = shifted(half, "mp", -1)
    far_a = shifted(ahead[:middle], "mp", 1)
    far_b = shifted(behind[middle:], "mp", -1)
    ahead_other = swapped(ahead)
    behind_other = swapped(behind)
    far_a_other = swapped(far_a)
    far_b_other = swapped(far_b)
    weights = (near, ahead, far_a, far_b, behind, ahead_other, far_a_other, far_b_other, behind_other)

    spots, table, own = index_tables(
        bricks, patch_shift, counts, curve_order.reshape(shard // BLOCK, BLOCK), voxel_feats, near
    )
    lanes = (lane0, own, lane2, lane3)
    head = head_rows(table, spots, lanes, ())
    head_next = shifted(head, "brick", -1)
    common = (table, spots, lanes, norm_gains, weights)
    own_rows, normed = gather_first(table, spots, lanes, norm_gains, head, queries)
    patch0 = (own_rows, *project(0, *common, (normed,), queries))
    mixed = attend((0, 1), patch0, weights, (), ())
    patch1 = project(1, *common, (head_next, mixed), queries)

    blocks = mlp(attend((0, 1, 2, 3), patch1, weights, (), ()), norm_gains, up_weight, down_weight, weights)

    last = [blocks[0]]
    for step in range(1, parts):
        last.append(shifted(blocks[step], "mp", step))
    hidden = attend((2, 3), patch0, weights, (mixed,), (blocks[0],))
    last = collect_rows(last)
    tail = shifted(last, "brick", 1)
    blocks = mlp(hidden, norm_gains, up_weight, down_weight, weights)
    first = [blocks[0]]
    for step in range(1, parts):
        first.append(shifted(blocks[step], "mp", step))
    back0, back1, back2, back3 = pack_lanes(patch_shift, table, spots, (tail, last, *first))
    back3 = shifted(back3, "brick", 2)
    back2 = shifted(back2, "brick", 1)
    back0 = shifted(back0, "brick", -1)
    return place_rows(counts, (back0, back1, back2, back3), capacity)


def solution(mesh):
    return jax.shard_map(
        body,
        mesh=mesh,
        in_specs=(
            P("brick", None),
            P("brick"),
            P("brick"),
            P(),
            P(None, "mp"),
            P("mp", None),
            P(None, "mp"),
            P("mp", None),
            P(),
        ),
        out_specs=P("brick", "mp"),
        check_vma=False,
    )
```
